32 devices in a mesh: wide: 4 (over x, core), narrow: 8 (over z, y).
Axes of the slice: x: 2, y: 2, z: 4, core: 2. Of those that a mesh axis runs over, the one named last changes fastest.
Arguments:
- stream: bfloat16 [8256, 1152], P('wide', 'narrow'), may hold values from -6 to 6
- skip_in: bfloat16 [8256, 1152], P('wide', 'narrow'), may hold values from -6 to 6
- cotangent: bfloat16 [8256, 1152], P('wide', 'narrow'), may hold values from -6 to 6
- skip_weight: bfloat16 [2, 1152, 1152], P(None, 'narrow'), may hold values from -0.125 to 0.125
- qkv_weight: bfloat16 [1152, 3, 1152], P(None, None, 'narrow'), may hold values from -0.1875 to 0.1875
- out_weight: bfloat16 [1152, 1152], P('narrow'), may hold values from -1.5 to 1.5
- up_weight: bfloat16 [1152, 4608], P(None, 'narrow'), may hold values from -0.1875 to 0.1875
- down_weight: bfloat16 [4608, 1152], P('narrow'), may hold values from -0.09375 to 0.09375
- norm_gain: float32 [2, 1152], replicated, may hold values from 0.5 to 1.5
- norm_bias: float32 [2, 1152], replicated, may hold values from -3 to 3
- row_skip: float32 [2, 1152], P(None, 'narrow'), may hold values from 7.5 to 12000
- col_skip: float32 [1152], replicated, may hold values from 30 to 3000
- row_qkv: float32 [1152], replicated, may hold values from 30 to 3000
- col_qkv: float32 [3, 1152], P(None, 'narrow'), may hold values from 7.5 to 12000
- row_out: float32 [1152], P('narrow'), may hold values from 7.5 to 12000
- col_out: float32 [1152], replicated, may hold values from 30 to 3000
- row_up: float32 [1152], replicated, may hold values from 30 to 3000
- col_up: float32 [4608], P('narrow'), may hold values from 7.5 to 12000
- row_down: float32 [4608], P('narrow'), may hold values from 7.5 to 12000
- col_down: float32 [1152], replicated, may hold values from 30 to 3000
- second_gain: float32 [2, 1152], replicated, may hold values from 100 to 10000
- second_bias: float32 [2, 1152], replicated, may hold values from 100 to 10000
Outputs:
- block_out: bfloat16 [8256, 1152], P('wide', 'narrow')
- grad_stream: float32 [8256, 1152], P('wide', 'narrow')
- grad_skip_in: float32 [8256, 1152], P('wide', 'narrow')
- grad_skip_weight: float32 [2, 1152, 1152], P(None, 'narrow', 'wide')
- grad_qkv_weight: float32 [1152, 3, 1152], P('wide', None, 'narrow')
- grad_out_weight: float32 [1152, 1152], P('narrow', 'wide')
- grad_up_weight: float32 [1152, 4608], P('wide', 'narrow')
- grad_down_weight: float32 [4608, 1152], P('narrow', 'wide')
- grad_norm_gain: float32 [2, 1152], replicated
- grad_norm_bias: float32 [2, 1152], replicated
- new_row_skip: float32 [2, 1152], P(None, 'narrow')
- new_col_skip: float32 [1152], replicated
- new_row_qkv: float32 [1152], replicated
- new_col_qkv: float32 [3, 1152], P(None, 'narrow')
- new_row_out: float32 [1152], P('narrow')
- new_col_out: float32 [1152], replicated
- new_row_up: float32 [1152], replicated
- new_col_up: float32 [4608], P('narrow')
- new_row_down: float32 [4608], P('narrow')
- new_col_down: float32 [1152], replicated
- new_second_gain: float32 [2, 1152], replicated
- new_second_bias_one: float32 [1152], replicated
- new_second_bias_two: float32 [1152], replicated
- new_skip_weight: float32 [2, 1152, 1152], P(None, 'narrow')
- new_qkv_weight: float32 [1152, 3, 1152], P(None, None, 'narrow')
- out_weight_step: float32 [1152, 1152], P('narrow')
- new_up_weight: float32 [1152, 4608], P(None, 'narrow')
- new_down_weight: float32 [4608, 1152], P('narrow')
- norm_gain_step: float32 [2, 1152], replicated
- norm_bias_step: float32 [2, 1152], replicated
- clip_ratio: float32 [5], replicated
The draws below stay inside these ranges and needn't reach their ends.
All inputs are finite; a program needn't handle non-finite values.
Results may differ from the reference program's by a relative error of at most 0.023.
Values may be sent and summed in bfloat16 or wider, within the bound.
No kernel may reach another device: no remote copies, remote signals or barrier semaphores. Data moves between devices by JAX's collectives and lax.ppermute only.
A program may use at most 192 MiB of HBM per device.

```python
import math
import jax
import jax.numpy as jnp
from jax import lax

D = 1152
HEADS = 16
FF = 4608
SEQ = 258
HEAD = 72
IMAGES = 32
TOKENS = 8256


def ramp_state(key, shape):
    length = shape[-1]
    base = jnp.exp(jax.random.uniform(key, shape, jnp.float32, math.log(30.0), math.log(3000.0)))
    place = lax.broadcasted_iota(jnp.float32, shape, len(shape) - 1)
    return base * jnp.exp(math.log(4.0) * (2.0 * place / (length - 1) - 1.0))


def draw_row_skip(key, part):
    return ramp_state(jax.random.fold_in(key, 11), (2, D))


def draw_col_qkv(key, part):
    return ramp_state(jax.random.fold_in(key, 12), (3, D))


def draw_row_out(key, part):
    return ramp_state(jax.random.fold_in(key, 13), (D,))


def draw_col_up(key, part):
    return ramp_state(jax.random.fold_in(key, 14), (FF,))


def draw_row_down(key, part):
    return ramp_state(jax.random.fold_in(key, 15), (FF,))


def steps_of(own_key, dims, shards, low, high):
    def one(axis_at, blocks):
        draws = jax.random.uniform(jax.random.fold_in(jax.random.fold_in(own_key, 6), axis_at), (blocks,), jnp.float32, low / len(shards), high / len(shards))
        return jnp.repeat(jnp.exp(draws), dims[axis_at] // blocks).reshape((-1,) + (1,) * (len(dims) - axis_at - 1))

    level = one(*shards[0])
    for cut in shards[1:]:
        level = level * one(*cut)
    return level


def centred(own_key, shape, width, bound, shards=(), held_as=jnp.bfloat16):
    values = width * jax.random.normal(own_key, shape, jnp.float32)
    if shards:
        values = values * steps_of(own_key, shape, shards, -0.22, 0.18)
    return jnp.clip(values, -bound, bound).astype(held_as)


def setup_inputs(seed: int = 0) -> dict:
    streams_of = jax.random.split(jax.random.key(seed), 23)
    stream = centred(streams_of[0], (TOKENS, D), 1.0, 6.0, ((0, 4), (1, 8)))
    skip_in = centred(streams_of[1], (TOKENS, D), 1.0, 6.0, ((0, 4), (1, 8)))
    cotangent = centred(streams_of[2], (TOKENS, D), 1.0, 6.0, ((0, 4), (1, 8)))
    skip_weight = centred(streams_of[3], (2, D, D), (2 * D) ** -0.5, 0.125, ((1, 8),))
    qkv_weight = centred(streams_of[4], (D, 3, D), D ** -0.5, 0.1875, ((2, 8),))
    out_weight = centred(streams_of[5], (D, D), (D // 64) ** -0.5, 1.5, ((0, 8),))
    up_weight = centred(streams_of[6], (D, FF), D ** -0.5, 0.1875, ((1, 8),))
    down_weight = centred(streams_of[7], (FF, D), FF ** -0.5, 0.09375, ((0, 8),))
    norm_gain = jnp.clip(1.0 + 0.1 * jax.random.normal(streams_of[8], (2, D), jnp.float32), 0.5, 1.5)
    norm_bias = centred(streams_of[9], (2, D), 0.5, 3.0, (), jnp.float32)
    row_skip = draw_row_skip(jax.random.fold_in(streams_of[22], 71), 0)
    col_skip = jnp.clip(jnp.exp(jax.random.uniform(streams_of[11], (D,), jnp.float32, math.log(30.0), math.log(3000.0))), 30.0, 3000.0)
    row_qkv = jnp.clip(jnp.exp(jax.random.uniform(streams_of[12], (D,), jnp.float32, math.log(30.0), math.log(3000.0))), 30.0, 3000.0)
    col_qkv = draw_col_qkv(jax.random.fold_in(streams_of[22], 71), 0)
    row_out = draw_row_out(jax.random.fold_in(streams_of[22], 71), 0)
    col_out = jnp.clip(jnp.exp(jax.random.uniform(streams_of[15], (D,), jnp.float32, math.log(30.0), math.log(3000.0))), 30.0, 3000.0)
    row_up = jnp.clip(jnp.exp(jax.random.uniform(streams_of[16], (D,), jnp.float32, math.log(30.0), math.log(3000.0))), 30.0, 3000.0)
    col_up = draw_col_up(jax.random.fold_in(streams_of[22], 71), 0)
    row_down = draw_row_down(jax.random.fold_in(streams_of[22], 71), 0)
    col_down = jnp.clip(jnp.exp(jax.random.uniform(streams_of[19], (D,), jnp.float32, math.log(30.0), math.log(3000.0))), 30.0, 3000.0)
    second_gain = jnp.clip(jnp.exp(jax.random.uniform(streams_of[20], (2, D), jnp.float32, math.log(100.0), math.log(10000.0))), 100.0, 10000.0)
    second_bias = jnp.clip(jnp.exp(jax.random.uniform(streams_of[21], (2, D), jnp.float32, math.log(100.0), math.log(10000.0))), 100.0, 10000.0)
    return {"stream": stream, "skip_in": skip_in, "cotangent": cotangent, "skip_weight": skip_weight, "qkv_weight": qkv_weight, "out_weight": out_weight, "up_weight": up_weight, "down_weight": down_weight, "norm_gain": norm_gain, "norm_bias": norm_bias, "row_skip": row_skip, "col_skip": col_skip, "row_qkv": row_qkv, "col_qkv": col_qkv, "row_out": row_out, "col_out": col_out, "row_up": row_up, "col_up": col_up, "row_down": row_down, "col_down": col_down, "second_gain": second_gain, "second_bias": second_bias}


@jax.custom_vjp
def low(v):
    return lax.optimization_barrier(v.astype(jnp.bfloat16)).astype(jnp.float32)

@jax.custom_vjp
def low_back(v):
    return v

def low_keep(v):
    return (low(v), None)

def low_pass(kept, grad):
    return (grad,)

def back_keep(v):
    return (v, None)

def back_low(kept, grad):
    return (low(grad),)
low.defvjp(low_keep, low_pass)
low_back.defvjp(back_keep, back_low)
NORM_EPS = 1e-05
EPS_SQUARE = 1e-30
DECAY = 0.5
STEP_RATE = 0.05
CLIP_LEVEL = 0.25

def matmul_high(left, right):
    return jnp.dot(left, right, precision=lax.Precision.HIGHEST)

def layer_norm(values, gain, shift):
    average = lax.optimization_barrier(jnp.mean(values, axis=-1, keepdims=True))
    centered = values - average
    variance = lax.optimization_barrier(jnp.mean(centered * centered, axis=-1, keepdims=True))
    return centered * lax.rsqrt(variance + NORM_EPS) * gain + shift

def attend_image(inputs):
    queries, key_vectors, value_vectors = inputs
    scores = low_back(jnp.einsum('qhe,khe->hqk', queries, key_vectors, precision=lax.Precision.HIGHEST))
    scores = scores * (1.0 / math.sqrt(HEAD))
    probs = low(jax.nn.softmax(scores, axis=-1))
    return jnp.einsum('hqk,khe->qhe', probs, value_vectors, precision=lax.Precision.HIGHEST)

def forward(stream, skip_in, skip_weight, qkv_weight, out_weight, up_weight, down_weight, norm_gain, norm_bias):
    hidden_in = low_back(matmul_high(stream, skip_weight[0]) + matmul_high(skip_in, skip_weight[1]))
    normed = low(layer_norm(hidden_in, norm_gain[0], norm_bias[0]))
    projected = low(low_back(jnp.einsum('rd,dtc->rtc', normed, qkv_weight, precision=lax.Precision.HIGHEST)))
    shaped = projected.reshape(IMAGES, SEQ, 3, HEADS, HEAD)
    attended = lax.map(jax.checkpoint(attend_image), (shaped[:, :, 0], shaped[:, :, 1], shaped[:, :, 2]))
    attended = low(low_back(attended.reshape(TOKENS, D)))
    middle = hidden_in + low_back(matmul_high(attended, out_weight))
    mixed_in = low(layer_norm(middle, norm_gain[1], norm_bias[1]))
    up_input = low_back(matmul_high(mixed_in, up_weight))
    activation = low(jax.nn.gelu(up_input, approximate=False))
    return middle + low_back(matmul_high(activation, down_weight))

def factored(grad, row_old, col_old, rows_all, cols_all):
    grid = grad.reshape(rows_all, cols_all)
    squares = grid * grid + EPS_SQUARE
    row_new = DECAY * row_old.reshape(rows_all) + (1.0 - DECAY) * lax.optimization_barrier(jnp.mean(squares, axis=1))
    col_new = DECAY * col_old.reshape(cols_all) + (1.0 - DECAY) * lax.optimization_barrier(jnp.mean(squares, axis=0))
    second = row_new[:, None] * col_new[None, :] / jnp.mean(row_new)
    update = grid * lax.rsqrt(second)
    spread = jnp.sqrt(jnp.mean(update * update))
    update = update / jnp.maximum(1.0, spread / CLIP_LEVEL)
    step = -(STEP_RATE * update)
    return (row_new.reshape(row_old.shape), col_new.reshape(col_old.shape), step.reshape(grad.shape), spread / CLIP_LEVEL)

def plain_update(grad, second_old):
    second_new = DECAY * second_old + (1.0 - DECAY) * (grad * grad + EPS_SQUARE)
    update = grad * lax.rsqrt(second_new)
    spread = jnp.sqrt(jnp.mean(update * update))
    update = update / jnp.maximum(1.0, spread / CLIP_LEVEL)
    return (second_new, -(STEP_RATE * update))

def reference(stream, skip_in, cotangent, skip_weight, qkv_weight, out_weight, up_weight, down_weight, norm_gain, norm_bias, row_skip, col_skip, row_qkv, col_qkv, row_out, col_out, row_up, col_up, row_down, col_down, second_gain, second_bias):
    floats = (stream.astype(jnp.float32), skip_in.astype(jnp.float32), skip_weight.astype(jnp.float32), qkv_weight.astype(jnp.float32), out_weight.astype(jnp.float32), up_weight.astype(jnp.float32), down_weight.astype(jnp.float32), norm_gain.astype(jnp.float32), norm_bias.astype(jnp.float32))
    result, backward = jax.vjp(forward, *floats)
    grads = backward(cotangent.astype(jnp.float32))
    grad_stream, grad_skip_in, grad_skip, grad_qkv, grad_out, grad_up, grad_down, grad_gain, grad_bias = grads
    new_row_skip, new_col_skip, step_skip, ratio_skip = factored(grad_skip, row_skip, col_skip, 2 * D, D)
    new_row_qkv, new_col_qkv, step_qkv, ratio_qkv = factored(grad_qkv, row_qkv, col_qkv, D, 3 * D)
    new_row_out, new_col_out, step_out, ratio_out = factored(grad_out, row_out, col_out, D, D)
    new_row_up, new_col_up, step_up, ratio_up = factored(grad_up, row_up, col_up, D, FF)
    new_row_down, new_col_down, step_down, ratio_down = factored(grad_down, row_down, col_down, FF, D)
    new_skip = floats[2] + step_skip
    new_qkv = floats[3] + step_qkv
    new_up = floats[5] + step_up
    new_down = floats[6] + step_down
    new_second_gain, gain_step = plain_update(grad_gain, second_gain)
    new_second_bias, bias_step = plain_update(grad_bias, second_bias)
    clip_ratio = jnp.stack([ratio_skip, ratio_qkv, ratio_out, ratio_up, ratio_down])
    return (result.astype(jnp.bfloat16), grad_stream, grad_skip_in, grad_skip, grad_qkv, grad_out, grad_up, grad_down, grad_gain, grad_bias, new_row_skip, new_col_skip, new_row_qkv, new_col_qkv, new_row_out, new_col_out, new_row_up, new_col_up, new_row_down, new_col_down, new_second_gain, new_second_bias[0], new_second_bias[1], new_skip, new_qkv, step_out, new_up, new_down, gain_step, bias_step, clip_ratio)
```

```python
import math

import jax
import jax.numpy as jnp
from jax import lax
from jax.sharding import PartitionSpec as P

D = 1152
FF = 4608
SEQ = 258
HEAD = 72


NORM_EPS = 1e-05
EPS_SQUARE = 1e-30
DECAY = 0.5
STEP_RATE = 0.05
CLIP_LEVEL = 0.25


def layer_norm(values, gain, shift):
    average = jnp.mean(values, axis=-1, keepdims=True)
    centered = values - average
    variance = jnp.mean(centered * centered, axis=-1, keepdims=True)
    return centered * lax.rsqrt(variance + NORM_EPS) * gain + shift


def norm_back(values, grad, gain, own_rows):
    average = jnp.mean(values, axis=-1, keepdims=True)
    centered = values - average
    variance = jnp.mean(centered * centered, axis=-1, keepdims=True)
    inverse = lax.rsqrt(variance + NORM_EPS)
    unit = centered * inverse
    scaled = grad * gain
    inner = (
        scaled
        - jnp.mean(scaled, axis=-1, keepdims=True)
        - unit * jnp.mean(scaled * unit, axis=-1, keepdims=True)
    )
    weighted = grad * own_rows
    return (inner * inverse, jnp.sum(weighted * unit, axis=0), jnp.sum(weighted, axis=0))


def gelu_exact(inputs):
    return jax.nn.gelu(inputs, approximate=False)


def matmul(left, right, form):
    return jnp.einsum(form, left, right, preferred_element_type=jnp.float32)


def plain_update(grad, second_old):
    second_new = DECAY * second_old + (1.0 - DECAY) * (grad * grad + EPS_SQUARE)
    update = grad * lax.rsqrt(second_new)
    spread = jnp.sqrt(jnp.mean(update * update))
    update = update / jnp.maximum(1.0, spread / CLIP_LEVEL)
    return (second_new, -(STEP_RATE * update))


def wide_slice(array, dim_index, count, wide_index):
    piece_size = array.shape[dim_index] // count
    return lax.dynamic_slice_in_dim(array, wide_index * piece_size, piece_size, dim_index)


def local(
    stream,
    skip_in,
    cotangent,
    skip_weight,
    qkv_weight,
    out_weight,
    up_weight,
    down_weight,
    norm_gain,
    norm_bias,
    row_skip,
    col_skip,
    row_qkv,
    col_qkv,
    row_out,
    col_out,
    row_up,
    col_up,
    row_down,
    col_down,
    second_gain,
    second_bias,
):
    rows_local, feat_local = stream.shape
    images = rows_local // SEQ
    heads_local = feat_local // HEAD
    scale_factor = 1.0 / math.sqrt(HEAD)
    split_shape = (images, SEQ, heads_local, HEAD)
    narrow_count = lax.axis_size("narrow")
    narrow_index = lax.axis_index("narrow")
    share_rows = -(-rows_local // narrow_count)
    row_start = narrow_index * share_rows
    row_ids = lax.broadcasted_iota(jnp.int32, (rows_local, 1), 0)
    own_mask = ((row_ids >= row_start) & (row_ids < row_start + share_rows)).astype(jnp.float32)

    def full_sum(values):
        return lax.psum(values, "narrow")

    partial_in = matmul(stream, skip_weight[0], "rc,cd->rd") + matmul(
        skip_in, skip_weight[1], "rc,cd->rd"
    )
    hidden_in = full_sum(partial_in)
    normed = layer_norm(hidden_in, norm_gain[0], norm_bias[0]).astype(jnp.bfloat16)
    projected = matmul(normed, qkv_weight, "rd,dtc->rtc").astype(jnp.bfloat16)
    queries = projected[:, 0].reshape(split_shape)
    key_vectors = projected[:, 1].reshape(split_shape)
    value_vectors = projected[:, 2].reshape(split_shape)
    scores = matmul(queries, key_vectors, "bqhe,bkhe->bhqk") * scale_factor
    row_max = jnp.max(scores, axis=-1, keepdims=True)
    exponent = jnp.exp(scores - row_max)
    row_total = jnp.sum(exponent, axis=-1, keepdims=True)
    log_total = row_max + jnp.log(row_total)
    probs_low = (exponent / row_total).astype(jnp.bfloat16)
    attended = (
        matmul(probs_low, value_vectors, "bhqk,bkhe->bqhe")
        .reshape(rows_local, feat_local)
        .astype(jnp.bfloat16)
    )
    attn_part = matmul(attended, out_weight, "rc,cd->rd")
    middle = hidden_in + full_sum(attn_part)
    mixed_in = layer_norm(middle, norm_gain[1], norm_bias[1]).astype(jnp.bfloat16)
    middle_own = lax.dynamic_slice_in_dim(middle, narrow_index * feat_local, feat_local, 1)
    up_input = matmul(mixed_in, up_weight, "rd,df->rf")
    activation = gelu_exact(up_input).astype(jnp.bfloat16)
    down_part = matmul(activation, down_weight, "rf,fd->rd")
    block_out = (
        middle_own + lax.psum_scatter(down_part, "narrow", scatter_dimension=1, tiled=True)
    ).astype(jnp.bfloat16)
    grad_full = lax.all_gather(cotangent, "narrow", axis=1, tiled=True)
    grad_down = matmul(activation, grad_full, "rf,rd->fd")
    grad_act = matmul(grad_full, down_weight, "rd,fd->rf")
    gelu_value, gelu_back = jax.vjp(gelu_exact, up_input)
    grad_up_in = gelu_back(grad_act)[0].astype(jnp.bfloat16)
    grad_up = matmul(mixed_in, grad_up_in, "rd,rf->df")
    mixed_part = matmul(grad_up_in, up_weight, "rf,df->rd")
    grad_mixed = full_sum(mixed_part)
    back_middle, back_gain_two, back_bias_two = norm_back(
        middle, grad_mixed, norm_gain[1], own_mask
    )
    grad_middle = grad_full.astype(jnp.float32) + back_middle
    middle_low = grad_middle.astype(jnp.bfloat16)
    grad_out = matmul(attended, middle_low, "rc,rd->cd")
    grad_attended = (
        matmul(middle_low, out_weight, "rd,cd->rc").astype(jnp.bfloat16).reshape(split_shape)
    )
    scores_again = matmul(queries, key_vectors, "bqhe,bkhe->bhqk") * scale_factor
    probs = jnp.exp(scores_again - log_total)
    probs_again = probs.astype(jnp.bfloat16)
    grad_values = matmul(probs_again, grad_attended, "bhqk,bqhe->bkhe")
    grad_probs = matmul(grad_attended, value_vectors, "bqhe,bkhe->bhqk")
    inner_sum = jnp.sum(probs * grad_probs, axis=-1, keepdims=True)
    grad_scores = (probs * (grad_probs - inner_sum) * scale_factor).astype(jnp.bfloat16)
    grad_queries = matmul(grad_scores, key_vectors, "bhqk,bkhe->bqhe")
    grad_keys = matmul(grad_scores, queries, "bhqk,bqhe->bkhe")
    grad_projected = jnp.stack(
        [
            grad_queries.reshape(rows_local, feat_local),
            grad_keys.reshape(rows_local, feat_local),
            grad_values.reshape(rows_local, feat_local),
        ],
        axis=1,
    ).astype(jnp.bfloat16)
    grad_qkv = matmul(normed, grad_projected, "rd,rtc->dtc")
    normed_part = matmul(grad_projected, qkv_weight, "rtc,dtc->rd")
    grad_normed = full_sum(normed_part)
    back_hidden, back_gain_one, back_bias_one = norm_back(
        hidden_in, grad_normed, norm_gain[0], own_mask
    )
    hidden_low = (grad_middle + back_hidden).astype(jnp.bfloat16)
    grad_skip = jnp.stack(
        [matmul(stream, hidden_low, "rc,rd->cd"), matmul(skip_in, hidden_low, "rc,rd->cd")]
    )
    grad_stream = matmul(hidden_low, skip_weight[0], "rd,cd->rc")
    grad_skip_in = matmul(hidden_low, skip_weight[1], "rd,cd->rc")
    gain_grads = jnp.stack([back_gain_one, back_gain_two])
    bias_grads = jnp.stack([back_bias_one, back_bias_two])
    wide_count = lax.axis_size("wide")
    wide_index = lax.axis_index("wide")
    wide_dims = (2, 0, 1, 0, 1)
    wide_axes = ((0, 1), (1, 2), (0,), (1,), (0,))
    narrow_axes = ((2,), (0,), (1,), (0,), (1,))
    wide_counts = (2 * D, 3 * D, D, FF, FF)
    row_along_wide = (False, True, False, True, False)
    entry_counts = (2 * D * D, 3 * D * D, D * D, D * FF, FF * D)
    old_slots = (0, 0, 1, 0, 2)
    weights = (skip_weight, qkv_weight, out_weight, up_weight, down_weight)
    old_wide = (col_skip, row_qkv, col_out, row_up, col_down)
    old_narrow = (row_skip, col_qkv, row_out, col_up, row_down)
    summed = lax.psum(
        (grad_skip, grad_qkv, grad_out, grad_up, grad_down, gain_grads, bias_grads), "wide"
    )
    pieces = summed[:5]
    gain_section = summed[5]
    bias_section = summed[6]
    squares = [piece * piece + EPS_SQUARE for piece in pieces]
    wide_parts = [jnp.sum(squares[number], axis=wide_axes[number]) for number in range(5)]
    narrow_parts = [jnp.sum(squares[number], axis=narrow_axes[number]) for number in range(5)]
    old_sums = jnp.stack([jnp.sum(row_skip), jnp.sum(row_out), jnp.sum(row_down)])
    stat_total = lax.psum(
        (
            wide_parts[0],
            wide_parts[1],
            wide_parts[2],
            wide_parts[3],
            wide_parts[4],
            old_sums,
            gain_section,
            bias_section,
        ),
        "narrow",
    )
    old_row_means = (stat_total[5][0] / (2 * D), stat_total[5][1] / D, stat_total[5][2] / FF)
    wide_stats = stat_total[:5]
    gain_total = stat_total[6]
    bias_total = stat_total[7]
    new_wide = []
    new_narrow = []
    updates = []
    for number in range(5):
        wide_mean = wide_stats[number] / wide_counts[number]
        wide_new = DECAY * old_wide[number] + (1.0 - DECAY) * wide_mean
        narrow_new = DECAY * old_narrow[number] + (1.0 - DECAY) * narrow_parts[number] / D
        if row_along_wide[number]:
            row_mean = jnp.mean(wide_new)
        else:
            row_mean = DECAY * old_row_means[old_slots[number]] + (1.0 - DECAY) * jnp.mean(
                wide_mean
            )
        dim_index = wide_dims[number]
        piece_size = pieces[number].shape[dim_index]
        broadcast_shape = [1] * pieces[number].ndim
        broadcast_shape[dim_index] = piece_size
        second = (
            jnp.expand_dims(narrow_new, dim_index) * wide_new.reshape(broadcast_shape) / row_mean
        )
        updates.append(pieces[number] * lax.rsqrt(second))
        new_wide.append(wide_new)
        new_narrow.append(narrow_new)
    update_squares = jnp.stack([jnp.sum(update * update) for update in updates])
    square_totals = lax.psum(update_squares, "narrow")
    counts_array = jnp.array(entry_counts, jnp.float32)
    clip_ratio = jnp.sqrt(square_totals / counts_array) / CLIP_LEVEL
    new_pieces = []
    for number in range(5):
        spread = jnp.sqrt(square_totals[number] / entry_counts[number])
        step_piece = -(STEP_RATE * (updates[number] / jnp.maximum(1.0, spread / CLIP_LEVEL)))
        if number == 2:
            new_pieces.append(step_piece)
        else:
            weight_piece = weights[number]
            new_pieces.append(weight_piece.astype(jnp.float32) + step_piece)
    grad_outs = [
        wide_slice(pieces[number], wide_dims[number], wide_count, wide_index) for number in range(5)
    ]
    new_second_gain, gain_step = plain_update(gain_total, second_gain)
    new_second_bias, bias_step = plain_update(bias_total, second_bias)
    return (
        block_out,
        grad_stream,
        grad_skip_in,
        grad_outs[0],
        grad_outs[1],
        grad_outs[2],
        grad_outs[3],
        grad_outs[4],
        gain_total,
        bias_total,
        new_narrow[0],
        new_wide[0],
        new_wide[1],
        new_narrow[1],
        new_narrow[2],
        new_wide[2],
        new_wide[3],
        new_narrow[3],
        new_narrow[4],
        new_wide[4],
        new_second_gain,
        new_second_bias[0],
        new_second_bias[1],
        new_pieces[0],
        new_pieces[1],
        new_pieces[2],
        new_pieces[3],
        new_pieces[4],
        gain_step,
        bias_step,
        clip_ratio,
    )


def unit_parts(values):
    average = jnp.mean(values, axis=-1, keepdims=True)
    centered = values - average
    variance = jnp.mean(centered * centered, axis=-1, keepdims=True)
    inverse = lax.rsqrt(variance + NORM_EPS)
    return centered * inverse, inverse


def norm_back_own(unit, inverse, grad, gain):
    scaled = grad * gain
    inner = (
        scaled
        - jnp.mean(scaled, axis=-1, keepdims=True)
        - unit * jnp.mean(scaled * unit, axis=-1, keepdims=True)
    )
    rows = tuple(range(grad.ndim - 1))
    return inner * inverse, jnp.sum(grad * unit, axis=rows), jnp.sum(grad, axis=rows)


def pick(array, index, axis):
    return lax.dynamic_index_in_dim(array, index, axis, keepdims=False)


def chips(
    stream,
    skip_in,
    cotangent,
    skip_weight,
    qkv_weight,
    out_weight,
    up_weight,
    down_weight,
    norm_gain,
    norm_bias,
    row_skip,
    col_skip,
    row_qkv,
    col_qkv,
    row_out,
    col_out,
    row_up,
    col_up,
    row_down,
    col_down,
    second_gain,
    second_bias,
):
    bf16 = jnp.bfloat16
    f32 = jnp.float32
    axes = ("wide", "narrow")
    wide_count = lax.axis_size("wide")
    narrow_count = lax.axis_size("narrow")
    ZS, YS = narrow_count // 2, 2
    wide_index = lax.axis_index("wide")
    narrow_index = lax.axis_index("narrow")
    xi = wide_index // 2
    ci = wide_index % 2
    zi = narrow_index // 2
    yi = narrow_index % 2
    rows_local, feat = stream.shape
    half_head = feat // 2
    hidden = up_weight.shape[1]
    quarter = hidden // 4
    scale_factor = 1.0 / math.sqrt(HEAD)

    def perm(move):
        pairs = []
        for wide in range(wide_count):
            for narrow in range(narrow_count):
                x, c, z, y = move(wide // 2, wide % 2, narrow // 2, narrow % 2)
                target = (x * 2 + c) * narrow_count + z * 2 + y
                pairs.append((wide * narrow_count + narrow, target))
        return pairs

    def send(value, move):
        return lax.ppermute(value, axes, perm(move))

    def core(value):
        return send(value, lambda x, c, z, y: (x, 1 - c, z, y))

    def over_x(value):
        return send(value, lambda x, c, z, y: (1 - x, c, z, y))

    def over_y(value):
        return send(value, lambda x, c, z, y: (x, c, z, 1 - y))

    def over_z(value, step):
        return send(value, lambda x, c, z, y: (x, c, (z + step) % ZS, y))

    def xor_z(value, bit):
        return send(value, lambda x, c, z, y: (x, c, z ^ bit, y))

    def to_images(array):
        grid = array.reshape((ZS, YS) + array.shape[1:])
        mine = pick(grid, yi, 1)
        other = over_y(pick(grid, 1 - yi, 1))
        both = jnp.stack([mine, other])
        blocks = [pick(both, zi, 1)]
        for step in range(1, ZS):
            blocks.append(over_z(pick(both, (zi + step) % ZS, 1), step))
        return blocks

    def canonical(blocks):
        stacked = jnp.stack(blocks)
        out = []
        for number in range(narrow_count):
            step = (zi - number // 2) % ZS
            j = yi ^ (number % 2)
            out.append(pick(pick(stacked, step, 0), j, 0))
        return jnp.stack(out)

    def ring(block):
        blocks = [block]
        for _ in range(ZS - 1):
            blocks.append(over_z(blocks[-1], 1))
        return jnp.stack(blocks)

    def gather_plane(block):
        first = ring(block)
        return [first, over_y(first)]

    def gather_all(own, other):
        plane = gather_plane(own)
        near = jnp.concatenate([other[None], over_x(plane[0][1:])])
        return [plane, [near, over_x(plane[1])]]

    def reduce_ring(total):
        carry = total[ZS - 1]
        for step in range(ZS - 2, -1, -1):
            carry = over_z(carry.astype(bf16), -1).astype(f32) + total[step].astype(f32)
        return carry

    def add_low(left, right):
        return (left.astype(f32) + right.astype(f32)).astype(bf16)

    def reduce_plane(pieces):
        total = add_low(pieces[0], over_y(pieces[1]))
        return reduce_ring(total)

    def reduce_all(pieces):
        return reduce_plane([add_low(pieces[0][j], over_x(pieces[1][j])) for j in range(2)])

    def reduce_then_x(pieces):
        total = reduce_plane(pieces)
        halves = total.reshape((2, total.shape[0] // 2) + total.shape[1:])
        kept = pick(halves, xi, 0)
        given = over_x(pick(halves, 1 - xi, 0).astype(bf16))
        return kept + given.astype(f32)

    def spread(piece):
        low = piece.astype(bf16)
        pair = jnp.stack([low, over_x(low)])
        four = jnp.stack([pair, core(pair)])
        parts = []
        for c in range(2):
            for x in range(2):
                parts.append(pick(pick(four, c ^ ci, 0), x ^ xi, 0))
        return jnp.stack(parts)

    is_first = ci == 0
    mine = jnp.where(is_first, stream, skip_in)
    given = core(jnp.where(is_first, skip_in, stream))
    tokens = jnp.stack([mine, given]).reshape(2, narrow_count, SEQ, feat).transpose(1, 0, 2, 3)
    token_blocks = to_images(tokens)
    token_pairs = [
        jnp.concatenate([block[j] for block in token_blocks], axis=-1) for j in range(2)
    ]

    skip_half = pick(skip_weight, ci, 0)
    skip_full = gather_plane(skip_half)
    qkv_rows = qkv_weight.transpose(1, 2, 0).reshape(3, 2, half_head, D)
    attn_half = jnp.concatenate(
        [pick(qkv_rows, ci, 1), pick(out_weight.reshape(2, half_head, D), ci, 0)[None]]
    )
    attn_full = gather_plane(attn_half)
    up_rows = pick(up_weight.T.reshape(2, 2, quarter, D), ci, 0)
    up_full = gather_all(pick(up_rows, xi, 0), pick(up_rows, 1 - xi, 0))
    down_rows = pick(down_weight.reshape(2, 2, quarter, D), ci, 0)
    down_full = gather_all(pick(down_rows, xi, 0), pick(down_rows, 1 - xi, 0))

    cot_blocks = to_images(cotangent.reshape(narrow_count, SEQ, feat))
    cot_own = canonical(cot_blocks).transpose(1, 0, 2).reshape(SEQ, D)

    def both_images(own):
        return jnp.concatenate([own[None], core(own)[None]]).reshape(2 * SEQ, -1)

    def core_sum(partial):
        parts = partial.reshape(2, SEQ, D)
        return parts[0] + core(parts[1])

    flat = [pair.reshape(2 * SEQ, -1) for pair in token_pairs]
    skip_mats = [piece.reshape(-1, D) for piece in skip_full]
    hidden_in = core_sum(
        matmul(flat[0], skip_mats[0], "rc,cd->rd") + matmul(flat[1], skip_mats[1], "rc,cd->rd")
    )
    unit_one, inverse_one = unit_parts(hidden_in)
    normed = both_images((unit_one * norm_gain[0] + norm_bias[0]).astype(bf16))

    heads = ZS
    attended = []
    kept = []
    attn_part = 0.0
    for j in range(2):
        weights = attn_full[j]
        rows = [weights[:, t].reshape(heads * half_head, D) for t in range(4)]
        q, k, v = [
            matmul(normed, rows[t], "rd,cd->rc").astype(bf16).reshape(2, SEQ, heads, half_head)
            for t in range(3)
        ]
        scores = matmul(q, k, "bqhe,bkhe->bhqk") * scale_factor
        row_max = jnp.max(scores, axis=-1, keepdims=True)
        exponent = jnp.exp(scores - row_max)
        row_total = jnp.sum(exponent, axis=-1, keepdims=True)
        probs = exponent / row_total
        probs_low = probs.astype(bf16)
        out = (
            matmul(probs_low, v, "bhqk,bkhe->bqhe")
            .reshape(2 * SEQ, heads * half_head)
            .astype(bf16)
        )
        attended.append(out)
        attn_part = attn_part + matmul(out, rows[3], "rc,cd->rd")
        kept.append((q, k, v, probs, probs_low, rows))
    middle = hidden_in + core_sum(attn_part)
    unit_two, inverse_two = unit_parts(middle)
    mixed = both_images((unit_two * norm_gain[1] + norm_bias[1]).astype(bf16))
    cot = both_images(cot_own)

    down_part = 0.0
    mixed_part = 0.0
    grad_down = [[None, None], [None, None]]
    grad_up = [[None, None], [None, None]]
    for i in range(2):
        for j in range(2):
            up_mat = up_full[i][j].reshape(-1, D)
            down_mat = down_full[i][j].reshape(-1, D)
            shape = (ZS, quarter, D)
            up_input = matmul(mixed, up_mat, "rd,fd->rf")
            gelu_value, gelu_back = jax.vjp(gelu_exact, up_input)
            activation = gelu_value.astype(bf16)
            down_part = down_part + matmul(activation, down_mat, "rf,fd->rd")
            grad_down[i][j] = matmul(activation, cot, "rf,rd->fd").astype(bf16).reshape(shape)
            grad_act = matmul(cot, down_mat, "rd,fd->rf")
            grad_up_in = gelu_back(grad_act)[0].astype(bf16)
            grad_up[i][j] = matmul(grad_up_in, mixed, "rf,rd->fd").astype(bf16).reshape(shape)
            mixed_part = mixed_part + matmul(grad_up_in, up_mat, "rf,fd->rd")
    down_own = reduce_all(grad_down)
    up_own = reduce_all(grad_up)
    block_own = (middle + core_sum(down_part)).astype(bf16)

    back_middle, gain_two, bias_two = norm_back_own(
        unit_two, inverse_two, core_sum(mixed_part), norm_gain[1]
    )
    grad_middle = cot_own.astype(f32) + back_middle
    middle_low = both_images(grad_middle.astype(bf16))
    normed_part = 0.0
    grad_attn = []
    for j in range(2):
        q, k, v, probs, probs_low, rows = kept[j]
        grad_out = matmul(attended[j], middle_low, "rc,rd->cd").astype(bf16)
        grad_attended = (
            matmul(middle_low, rows[3], "rd,cd->rc").astype(bf16).reshape(2, SEQ, heads, half_head)
        )
        grad_v = matmul(probs_low, grad_attended, "bhqk,bqhe->bkhe")
        grad_probs = matmul(grad_attended, v, "bqhe,bkhe->bhqk")
        inner_sum = jnp.sum(probs * grad_probs, axis=-1, keepdims=True)
        grad_scores = (probs * (grad_probs - inner_sum) * scale_factor).astype(bf16)
        grad_q = matmul(grad_scores, k, "bhqk,bkhe->bqhe")
        grad_k = matmul(grad_scores, q, "bhqk,bqhe->bkhe")
        mats = []
        for t, grad in enumerate((grad_q, grad_k, grad_v)):
            low = grad.astype(bf16).reshape(2 * SEQ, heads * half_head)
            mats.append(matmul(low, normed, "rc,rd->cd").astype(bf16))
            normed_part = normed_part + matmul(low, rows[t], "rc,cd->rd")
        mats.append(grad_out)
        grad_attn.append(
            jnp.stack([mat.reshape(heads, half_head, D) for mat in mats], axis=1).reshape(
                heads, 4 * half_head, D
            )
        )
    attn_own = reduce_then_x(grad_attn)
    back_hidden, gain_one, bias_one = norm_back_own(
        unit_one, inverse_one, core_sum(normed_part), norm_gain[0]
    )
    hidden_own = (grad_middle + back_hidden).astype(bf16)
    hidden_low = both_images(hidden_own)
    grad_skip = [
        matmul(part, hidden_low, "rc,rd->cd").astype(bf16).reshape(ZS, feat, D) for part in flat
    ]
    skip_own = reduce_then_x(grad_skip)

    def to_features(grid):
        blocks = to_images(grid.reshape((narrow_count,) + grid.shape[2:]))
        return canonical(blocks)

    block_out = to_features(
        block_own.reshape(SEQ, ZS, YS, feat).transpose(1, 2, 0, 3)
    ).reshape(rows_local, feat)
    token_grads = [
        matmul(hidden_low, mat, "rd,cd->rc").astype(bf16).reshape(2, SEQ, ZS, feat)
        for mat in skip_mats
    ]
    kept_grads = jnp.stack([grad.transpose(2, 0, 1, 3) for grad in token_grads])
    returned = jnp.stack([kept_grads[0], over_y(kept_grads[1])])
    backs = [returned[:, 0]]
    for step in range(1, ZS):
        backs.append(over_z(returned[:, step], -step))
    stacked = jnp.stack(backs)
    ordered = []
    for number in range(narrow_count):
        step = (number // 2 - zi) % ZS
        ordered.append(pick(pick(stacked, step, 0), yi ^ (number % 2), 0))
    ordered = jnp.stack(ordered)
    grad_mine = ordered[:, 0].reshape(rows_local, feat)
    grad_given = core(ordered[:, 1].reshape(rows_local, feat))
    grad_stream = jnp.where(is_first, grad_mine, grad_given).astype(f32)
    grad_skip_in = jnp.where(is_first, grad_given, grad_mine).astype(f32)

    down_all = spread(down_own).reshape(hidden, D)
    up_all = spread(up_own).reshape(hidden, D)
    attn_all = spread(attn_own).reshape(2, 4, half_head, D)
    skip_all = spread(skip_own).reshape(2, feat, D)
    qkv_all = attn_all[:, :3].transpose(1, 0, 2, 3).reshape(3, feat, D)
    out_all = attn_all[:, 3].reshape(feat, D)

    def all_narrow(value):
        value = value + over_y(value)
        bit = 1
        while bit < ZS:
            value = value + xor_z(value, bit)
            bit *= 2
        return value

    norm_sums = jnp.stack([gain_one, gain_two, bias_one, bias_two])
    norm_sums = norm_sums + core(norm_sums)
    norm_sums = norm_sums + over_x(norm_sums)

    grads = [
        skip_all.reshape(-1, D).astype(f32),
        qkv_all.reshape(-1, D).astype(f32),
        out_all.astype(f32),
        up_all.astype(f32),
        down_all.astype(f32),
    ]
    old_wide = (col_skip, row_qkv, col_out, row_up, col_down)
    old_narrow = (row_skip.reshape(-1), col_qkv.reshape(-1), row_out, col_up, row_down)
    row_along_wide = (False, True, False, True, False)
    wide_counts = (2 * D, 3 * D, D, FF, FF)
    entry_counts = (2 * D * D, 3 * D * D, D * D, D * FF, FF * D)
    new_narrow = []
    sums = []
    for number in range(5):
        grad = grads[number]
        squares = grad * grad + EPS_SQUARE
        narrow_new = DECAY * old_narrow[number] + (1.0 - DECAY) * (jnp.sum(squares, axis=1) / D)
        new_narrow.append(narrow_new)
        old_sum = jnp.zeros((D,), f32).at[0].set(jnp.sum(old_narrow[number]))
        sums.append(
            jnp.stack(
                [
                    jnp.sum(squares, axis=0),
                    jnp.sum(grad * grad * (1.0 / narrow_new)[:, None], axis=0),
                    old_sum,
                ]
            )
        )
    early = all_narrow(jnp.concatenate([sums[number] for number in range(1, 5)]))
    late = all_narrow(jnp.concatenate([sums[0], norm_sums]))
    totals = [late[:3]] + [early[3 * number : 3 * number + 3] for number in range(4)]
    gain_total = late[3:5]
    bias_total = late[5:7]

    new_wide = []
    steps = []
    ratios = []
    for number in range(5):
        wide_mean = totals[number][0] / wide_counts[number]
        wide_new = DECAY * old_wide[number] + (1.0 - DECAY) * wide_mean
        if row_along_wide[number]:
            row_mean = jnp.mean(wide_new)
        else:
            row_mean = DECAY * (totals[number][2][0] / wide_counts[number]) + (
                1.0 - DECAY
            ) * jnp.mean(wide_mean)
        square_total = jnp.sum(totals[number][1] / wide_new) * row_mean
        ratio = jnp.sqrt(square_total / entry_counts[number]) / CLIP_LEVEL
        ratios.append(ratio)
        factor = -(STEP_RATE * jnp.sqrt(row_mean) / jnp.maximum(1.0, ratio))
        step = (
            grads[number]
            * lax.rsqrt(new_narrow[number])[:, None]
            * (lax.rsqrt(wide_new) * factor)[None, :]
        )
        new_wide.append(wide_new)
        steps.append(step)
    clip_ratio = jnp.stack(ratios)

    def columns(array):
        size = D // wide_count
        return lax.dynamic_slice_in_dim(array, wide_index * size, size, array.ndim - 1)

    new_skip = skip_weight.astype(f32) + steps[0].reshape(2, feat, D)
    new_qkv = qkv_weight.astype(f32) + steps[1].reshape(3, feat, D).transpose(2, 0, 1)
    new_up = up_weight.astype(f32) + steps[3].T
    new_down = down_weight.astype(f32) + steps[4]
    new_second_gain, gain_step = plain_update(gain_total, second_gain)
    new_second_bias, bias_step = plain_update(bias_total, second_bias)
    return (
        block_out,
        grad_stream,
        grad_skip_in,
        columns(grads[0]).reshape(2, feat, -1),
        columns(grads[1]).reshape(3, feat, -1).transpose(2, 0, 1),
        columns(grads[2]),
        columns(grads[3]).T,
        columns(grads[4]),
        gain_total,
        bias_total,
        new_narrow[0].reshape(2, feat),
        new_wide[0],
        new_wide[1],
        new_narrow[1].reshape(3, feat),
        new_narrow[2],
        new_wide[2],
        new_wide[3],
        new_narrow[3],
        new_narrow[4],
        new_wide[4],
        new_second_gain,
        new_second_bias[0],
        new_second_bias[1],
        new_skip,
        new_qkv,
        steps[2],
        new_up,
        new_down,
        gain_step,
        bias_step,
        clip_ratio,
    )


def solution(mesh):
    wide, narrow = mesh.shape["wide"], mesh.shape["narrow"]
    body = chips if (wide == 4 and narrow == 8) else local
    in_specs = (
        P("wide", "narrow"),
        P("wide", "narrow"),
        P("wide", "narrow"),
        P(None, "narrow", None),
        P(None, None, "narrow"),
        P("narrow", None),
        P(None, "narrow"),
        P("narrow", None),
        P(),
        P(),
        P(None, "narrow"),
        P(),
        P(),
        P(None, "narrow"),
        P("narrow"),
        P(),
        P(),
        P("narrow"),
        P("narrow"),
        P(),
        P(),
        P(),
    )
    out_specs = (
        P("wide", "narrow"),
        P("wide", "narrow"),
        P("wide", "narrow"),
        P(None, "narrow", "wide"),
        P("wide", None, "narrow"),
        P("narrow", "wide"),
        P("wide", "narrow"),
        P("narrow", "wide"),
        P(),
        P(),
        P(None, "narrow"),
        P(),
        P(),
        P(None, "narrow"),
        P("narrow"),
        P(),
        P(),
        P("narrow"),
        P("narrow"),
        P(),
        P(),
        P(),
        P(),
        P(None, "narrow", None),
        P(None, None, "narrow"),
        P("narrow", None),
        P(None, "narrow"),
        P("narrow", None),
        P(),
        P(),
        P(),
    )
    return jax.shard_map(body, mesh=mesh, in_specs=in_specs, out_specs=out_specs, check_vma=False)
```

```python
import math

import jax
import jax.numpy as jnp
from jax import lax
from jax.experimental import pallas as pl
from jax.experimental.pallas import tpu as pltpu
from jax.sharding import PartitionSpec as P

D = 1152
FF = 4608
SEQ = 258
HEAD = 72


NORM_EPS = 1e-05
EPS_SQUARE = 1e-30
DECAY = 0.5
STEP_RATE = 0.05
CLIP_LEVEL = 0.25


def layer_norm(values, gain, shift):
    average = jnp.mean(values, axis=-1, keepdims=True)
    centered = values - average
    variance = jnp.mean(centered * centered, axis=-1, keepdims=True)
    return centered * lax.rsqrt(variance + NORM_EPS) * gain + shift


def norm_back(values, grad, gain, own_rows):
    average = jnp.mean(values, axis=-1, keepdims=True)
    centered = values - average
    variance = jnp.mean(centered * centered, axis=-1, keepdims=True)
    inverse = lax.rsqrt(variance + NORM_EPS)
    unit = centered * inverse
    scaled = grad * gain
    inner = (
        scaled
        - jnp.mean(scaled, axis=-1, keepdims=True)
        - unit * jnp.mean(scaled * unit, axis=-1, keepdims=True)
    )
    weighted = grad * own_rows
    return (inner * inverse, jnp.sum(weighted * unit, axis=0), jnp.sum(weighted, axis=0))


def gelu_exact(inputs):
    return jax.nn.gelu(inputs, approximate=False)


def matmul(left, right, form):
    return jnp.einsum(form, left, right, preferred_element_type=jnp.float32)


def plain_update(grad, second_old):
    second_new = DECAY * second_old + (1.0 - DECAY) * (grad * grad + EPS_SQUARE)
    update = grad * lax.rsqrt(second_new)
    spread = jnp.sqrt(jnp.mean(update * update))
    update = update / jnp.maximum(1.0, spread / CLIP_LEVEL)
    return (second_new, -(STEP_RATE * update))


def wide_slice(array, dim_index, count, wide_index):
    piece_size = array.shape[dim_index] // count
    return lax.dynamic_slice_in_dim(array, wide_index * piece_size, piece_size, dim_index)


def local(
    stream,
    skip_in,
    cotangent,
    skip_weight,
    qkv_weight,
    out_weight,
    up_weight,
    down_weight,
    norm_gain,
    norm_bias,
    row_skip,
    col_skip,
    row_qkv,
    col_qkv,
    row_out,
    col_out,
    row_up,
    col_up,
    row_down,
    col_down,
    second_gain,
    second_bias,
):
    rows_local, feat_local = stream.shape
    images = rows_local // SEQ
    heads_local = feat_local // HEAD
    scale_factor = 1.0 / math.sqrt(HEAD)
    split_shape = (images, SEQ, heads_local, HEAD)
    narrow_count = lax.axis_size("narrow")
    narrow_index = lax.axis_index("narrow")
    share_rows = -(-rows_local // narrow_count)
    row_start = narrow_index * share_rows
    row_ids = lax.broadcasted_iota(jnp.int32, (rows_local, 1), 0)
    own_mask = ((row_ids >= row_start) & (row_ids < row_start + share_rows)).astype(jnp.float32)

    def full_sum(values):
        return lax.psum(values, "narrow")

    partial_in = matmul(stream, skip_weight[0], "rc,cd->rd") + matmul(
        skip_in, skip_weight[1], "rc,cd->rd"
    )
    hidden_in = full_sum(partial_in)
    normed = layer_norm(hidden_in, norm_gain[0], norm_bias[0]).astype(jnp.bfloat16)
    projected = matmul(normed, qkv_weight, "rd,dtc->rtc").astype(jnp.bfloat16)
    queries = projected[:, 0].reshape(split_shape)
    key_vectors = projected[:, 1].reshape(split_shape)
    value_vectors = projected[:, 2].reshape(split_shape)
    scores = matmul(queries, key_vectors, "bqhe,bkhe->bhqk") * scale_factor
    row_max = jnp.max(scores, axis=-1, keepdims=True)
    exponent = jnp.exp(scores - row_max)
    row_total = jnp.sum(exponent, axis=-1, keepdims=True)
    log_total = row_max + jnp.log(row_total)
    probs_low = (exponent / row_total).astype(jnp.bfloat16)
    attended = (
        matmul(probs_low, value_vectors, "bhqk,bkhe->bqhe")
        .reshape(rows_local, feat_local)
        .astype(jnp.bfloat16)
    )
    attn_part = matmul(attended, out_weight, "rc,cd->rd")
    middle = hidden_in + full_sum(attn_part)
    mixed_in = layer_norm(middle, norm_gain[1], norm_bias[1]).astype(jnp.bfloat16)
    middle_own = lax.dynamic_slice_in_dim(middle, narrow_index * feat_local, feat_local, 1)
    up_input = matmul(mixed_in, up_weight, "rd,df->rf")
    activation = gelu_exact(up_input).astype(jnp.bfloat16)
    down_part = matmul(activation, down_weight, "rf,fd->rd")
    block_out = (
        middle_own + lax.psum_scatter(down_part, "narrow", scatter_dimension=1, tiled=True)
    ).astype(jnp.bfloat16)
    grad_full = lax.all_gather(cotangent, "narrow", axis=1, tiled=True)
    grad_down = matmul(activation, grad_full, "rf,rd->fd")
    grad_act = matmul(grad_full, down_weight, "rd,fd->rf")
    gelu_value, gelu_back = jax.vjp(gelu_exact, up_input)
    grad_up_in = gelu_back(grad_act)[0].astype(jnp.bfloat16)
    grad_up = matmul(mixed_in, grad_up_in, "rd,rf->df")
    mixed_part = matmul(grad_up_in, up_weight, "rf,df->rd")
    grad_mixed = full_sum(mixed_part)
    back_middle, back_gain_two, back_bias_two = norm_back(
        middle, grad_mixed, norm_gain[1], own_mask
    )
    grad_middle = grad_full.astype(jnp.float32) + back_middle
    middle_low = grad_middle.astype(jnp.bfloat16)
    grad_out = matmul(attended, middle_low, "rc,rd->cd")
    grad_attended = (
        matmul(middle_low, out_weight, "rd,cd->rc").astype(jnp.bfloat16).reshape(split_shape)
    )
    scores_again = matmul(queries, key_vectors, "bqhe,bkhe->bhqk") * scale_factor
    probs = jnp.exp(scores_again - log_total)
    probs_again = probs.astype(jnp.bfloat16)
    grad_values = matmul(probs_again, grad_attended, "bhqk,bqhe->bkhe")
    grad_probs = matmul(grad_attended, value_vectors, "bqhe,bkhe->bhqk")
    inner_sum = jnp.sum(probs * grad_probs, axis=-1, keepdims=True)
    grad_scores = (probs * (grad_probs - inner_sum) * scale_factor).astype(jnp.bfloat16)
    grad_queries = matmul(grad_scores, key_vectors, "bhqk,bkhe->bqhe")
    grad_keys = matmul(grad_scores, queries, "bhqk,bqhe->bkhe")
    grad_projected = jnp.stack(
        [
            grad_queries.reshape(rows_local, feat_local),
            grad_keys.reshape(rows_local, feat_local),
            grad_values.reshape(rows_local, feat_local),
        ],
        axis=1,
    ).astype(jnp.bfloat16)
    grad_qkv = matmul(normed, grad_projected, "rd,rtc->dtc")
    normed_part = matmul(grad_projected, qkv_weight, "rtc,dtc->rd")
    grad_normed = full_sum(normed_part)
    back_hidden, back_gain_one, back_bias_one = norm_back(
        hidden_in, grad_normed, norm_gain[0], own_mask
    )
    hidden_low = (grad_middle + back_hidden).astype(jnp.bfloat16)
    grad_skip = jnp.stack(
        [matmul(stream, hidden_low, "rc,rd->cd"), matmul(skip_in, hidden_low, "rc,rd->cd")]
    )
    grad_stream = matmul(hidden_low, skip_weight[0], "rd,cd->rc")
    grad_skip_in = matmul(hidden_low, skip_weight[1], "rd,cd->rc")
    gain_grads = jnp.stack([back_gain_one, back_gain_two])
    bias_grads = jnp.stack([back_bias_one, back_bias_two])
    wide_count = lax.axis_size("wide")
    wide_index = lax.axis_index("wide")
    wide_dims = (2, 0, 1, 0, 1)
    wide_axes = ((0, 1), (1, 2), (0,), (1,), (0,))
    narrow_axes = ((2,), (0,), (1,), (0,), (1,))
    wide_counts = (2 * D, 3 * D, D, FF, FF)
    row_along_wide = (False, True, False, True, False)
    entry_counts = (2 * D * D, 3 * D * D, D * D, D * FF, FF * D)
    old_slots = (0, 0, 1, 0, 2)
    weights = (skip_weight, qkv_weight, out_weight, up_weight, down_weight)
    old_wide = (col_skip, row_qkv, col_out, row_up, col_down)
    old_narrow = (row_skip, col_qkv, row_out, col_up, row_down)
    summed = lax.psum(
        (grad_skip, grad_qkv, grad_out, grad_up, grad_down, gain_grads, bias_grads), "wide"
    )
    pieces = summed[:5]
    gain_section = summed[5]
    bias_section = summed[6]
    squares = [piece * piece + EPS_SQUARE for piece in pieces]
    wide_parts = [jnp.sum(squares[number], axis=wide_axes[number]) for number in range(5)]
    narrow_parts = [jnp.sum(squares[number], axis=narrow_axes[number]) for number in range(5)]
    old_sums = jnp.stack([jnp.sum(row_skip), jnp.sum(row_out), jnp.sum(row_down)])
    stat_total = lax.psum(
        (
            wide_parts[0],
            wide_parts[1],
            wide_parts[2],
            wide_parts[3],
            wide_parts[4],
            old_sums,
            gain_section,
            bias_section,
        ),
        "narrow",
    )
    old_row_means = (stat_total[5][0] / (2 * D), stat_total[5][1] / D, stat_total[5][2] / FF)
    wide_stats = stat_total[:5]
    gain_total = stat_total[6]
    bias_total = stat_total[7]
    new_wide = []
    new_narrow = []
    updates = []
    for number in range(5):
        wide_mean = wide_stats[number] / wide_counts[number]
        wide_new = DECAY * old_wide[number] + (1.0 - DECAY) * wide_mean
        narrow_new = DECAY * old_narrow[number] + (1.0 - DECAY) * narrow_parts[number] / D
        if row_along_wide[number]:
            row_mean = jnp.mean(wide_new)
        else:
            row_mean = DECAY * old_row_means[old_slots[number]] + (1.0 - DECAY) * jnp.mean(
                wide_mean
            )
        dim_index = wide_dims[number]
        piece_size = pieces[number].shape[dim_index]
        broadcast_shape = [1] * pieces[number].ndim
        broadcast_shape[dim_index] = piece_size
        second = (
            jnp.expand_dims(narrow_new, dim_index) * wide_new.reshape(broadcast_shape) / row_mean
        )
        updates.append(pieces[number] * lax.rsqrt(second))
        new_wide.append(wide_new)
        new_narrow.append(narrow_new)
    update_squares = jnp.stack([jnp.sum(update * update) for update in updates])
    square_totals = lax.psum(update_squares, "narrow")
    counts_array = jnp.array(entry_counts, jnp.float32)
    clip_ratio = jnp.sqrt(square_totals / counts_array) / CLIP_LEVEL
    new_pieces = []
    for number in range(5):
        spread = jnp.sqrt(square_totals[number] / entry_counts[number])
        step_piece = -(STEP_RATE * (updates[number] / jnp.maximum(1.0, spread / CLIP_LEVEL)))
        if number == 2:
            new_pieces.append(step_piece)
        else:
            weight_piece = weights[number]
            new_pieces.append(weight_piece.astype(jnp.float32) + step_piece)
    grad_outs = [
        wide_slice(pieces[number], wide_dims[number], wide_count, wide_index) for number in range(5)
    ]
    new_second_gain, gain_step = plain_update(gain_total, second_gain)
    new_second_bias, bias_step = plain_update(bias_total, second_bias)
    return (
        block_out,
        grad_stream,
        grad_skip_in,
        grad_outs[0],
        grad_outs[1],
        grad_outs[2],
        grad_outs[3],
        grad_outs[4],
        gain_total,
        bias_total,
        new_narrow[0],
        new_wide[0],
        new_wide[1],
        new_narrow[1],
        new_narrow[2],
        new_wide[2],
        new_wide[3],
        new_narrow[3],
        new_narrow[4],
        new_wide[4],
        new_second_gain,
        new_second_bias[0],
        new_second_bias[1],
        new_pieces[0],
        new_pieces[1],
        new_pieces[2],
        new_pieces[3],
        new_pieces[4],
        gain_step,
        bias_step,
        clip_ratio,
    )


def unit_parts(values):
    average = jnp.mean(values, axis=-1, keepdims=True)
    centered = values - average
    variance = jnp.mean(centered * centered, axis=-1, keepdims=True)
    inverse = lax.rsqrt(variance + NORM_EPS)
    return centered * inverse, inverse


def norm_back_own(unit, inverse, grad, gain):
    scaled = grad * gain
    inner = (
        scaled
        - jnp.mean(scaled, axis=-1, keepdims=True)
        - unit * jnp.mean(scaled * unit, axis=-1, keepdims=True)
    )
    rows = tuple(range(grad.ndim - 1))
    return inner * inverse, jnp.sum(grad * unit, axis=rows), jnp.sum(grad, axis=rows)


def pick(array, index, axis):
    return lax.dynamic_index_in_dim(array, index, axis, keepdims=False)


PAD = 272


def dot_nt(left, right):
    return lax.dot_general(left, right, (((1,), (1,)), ((), ())), preferred_element_type=jnp.float32)


def dot_nn(left, right):
    return lax.dot_general(left, right, (((1,), (0,)), ((), ())), preferred_element_type=jnp.float32)


def dot_tn(left, right):
    return lax.dot_general(left, right, (((0,), (0,)), ((), ())), preferred_element_type=jnp.float32)


def accumulate(step, refs, value):
    size = refs[0].shape[0]

    @pl.when(step == 0)
    def _():
        for number, ref in enumerate(refs):
            ref[...] = value[number * size : (number + 1) * size]

    @pl.when(step > 0)
    def _():
        for number, ref in enumerate(refs):
            ref[...] += value[number * size : (number + 1) * size]


def ffn_kernel(mixed_ref, cot_ref, weight_ref, down_a, down_b, mixed_a, mixed_b, grad_ref):
    step = pl.program_id(0)
    blocks, _, rows, _ = weight_ref.shape
    mixed = mixed_ref[...]
    cot = cot_ref[...]
    up = jnp.concatenate([weight_ref[n, 0] for n in range(blocks)], axis=0)
    down = jnp.concatenate([weight_ref[n, 1] for n in range(blocks)], axis=0)
    up_input = dot_nt(mixed, up)
    gate = 0.5 * (1.0 + lax.erf(up_input * (1.0 / math.sqrt(2.0))))
    activation = (up_input * gate).astype(jnp.bfloat16)
    slope = gate + up_input * (jnp.exp(-0.5 * up_input * up_input) * (1.0 / math.sqrt(2.0 * math.pi)))
    grad_up_in = (dot_nt(cot, down) * slope).astype(jnp.bfloat16)
    grad_up = dot_tn(grad_up_in, mixed).astype(jnp.bfloat16)
    grad_down = dot_tn(activation, cot).astype(jnp.bfloat16)
    for n in range(blocks):
        grad_ref[n, 0] = grad_up[n * rows : (n + 1) * rows]
        grad_ref[n, 1] = grad_down[n * rows : (n + 1) * rows]
    accumulate(step, (mixed_a, mixed_b), dot_nn(grad_up_in, up))
    accumulate(step, (down_a, down_b), dot_nn(activation, down))


def ffn(mixed, cot, weights):
    count, _, rows, _ = weights.shape
    tokens = mixed.shape[0]
    blocks = 4
    whole = pl.BlockSpec((tokens, D), lambda t: (0, 0))
    half = pl.BlockSpec((tokens // 2, D), lambda t: (0, 0))
    block = pl.BlockSpec((blocks, 2, rows, D), lambda t: (t, 0, 0, 0))
    part = jax.ShapeDtypeStruct((tokens // 2, D), jnp.float32)
    return pl.pallas_call(
        ffn_kernel,
        out_shape=[part] * 4 + [jax.ShapeDtypeStruct(weights.shape, jnp.bfloat16)],
        grid=(count // blocks,),
        in_specs=[whole, whole, block],
        out_specs=[half] * 4 + [block],
        compiler_params=pltpu.CompilerParams(
            dimension_semantics=("arbitrary",), vmem_limit_bytes=60 * 1024 * 1024
        ),
        cost_estimate=pl.CostEstimate(
            flops=12 * tokens * D * count * rows, transcendentals=0, bytes_accessed=32 * 1024 * 1024
        ),
        name="ffn",
    )(mixed, cot, weights)


def soft(q, k):
    scores = dot_nt(q, k) * (1.0 / math.sqrt(HEAD))
    column = lax.broadcasted_iota(jnp.int32, scores.shape, 1)
    scores = jnp.where(column < SEQ, scores, -1e30)
    exponent = jnp.exp(scores - jnp.max(scores, axis=-1, keepdims=True))
    return exponent / jnp.sum(exponent, axis=-1, keepdims=True)


def attn_forward_kernel(meta_ref, normed_ref, qk_ref, vo_ref, part_a, part_b, qkv_ref, attended_ref):
    step = pl.program_id(0)
    normed = normed_ref[...]
    qk = dot_nt(normed, qk_ref[0, 0])
    v_all = dot_nt(normed, vo_ref[0, 0, :HEAD])
    out_weight = vo_ref[0, 0, HEAD:]
    qkv_ref[0, :, : 2 * HEAD] = qk.astype(jnp.bfloat16)
    qkv_ref[0, :, 2 * HEAD :] = v_all.astype(jnp.bfloat16)
    for image in range(2):
        rows = slice(image * PAD, (image + 1) * PAD)
        q = qk[rows, :HEAD].astype(jnp.bfloat16)
        k = qk[rows, HEAD:].astype(jnp.bfloat16)
        v = v_all[rows].astype(jnp.bfloat16)
        probs = soft(q, k).astype(jnp.bfloat16)
        attended_ref[0, rows] = dot_nn(probs, v).astype(jnp.bfloat16)
    add = dot_nn(attended_ref[0], out_weight)

    accumulate(step, (part_a, part_b), add)


def attn_specs(rows, tokens):
    whole = pl.BlockSpec((tokens, D), lambda s, m: (0, 0))
    half = pl.BlockSpec((tokens // 2, D), lambda s, m: (0, 0))
    qk = pl.BlockSpec((1, 1, rows, D), lambda s, m: (m[0], s, 0, 0))
    vo = pl.BlockSpec((1, 1, rows, D), lambda s, m: (1 - m[0], s, 0, 0))
    qkv = pl.BlockSpec((1, tokens, 3 * HEAD), lambda s, m: (s, 0, 0))
    att = pl.BlockSpec((1, tokens, HEAD), lambda s, m: (s, 0, 0))
    return whole, half, qk, vo, qkv, att


def attn_forward(meta, normed, weights):
    heads, rows = weights.shape[1:3]
    tokens = normed.shape[0]
    whole, half, qk, vo, qkv, att = attn_specs(rows, tokens)
    return pl.pallas_call(
        attn_forward_kernel,
        out_shape=[
            jax.ShapeDtypeStruct((tokens // 2, D), jnp.float32),
            jax.ShapeDtypeStruct((tokens // 2, D), jnp.float32),
            jax.ShapeDtypeStruct((heads, tokens, 3 * HEAD), jnp.bfloat16),
            jax.ShapeDtypeStruct((heads, tokens, HEAD), jnp.bfloat16),
        ],
        grid_spec=pltpu.PrefetchScalarGridSpec(
            num_scalar_prefetch=1,
            grid=(heads,),
            in_specs=[whole, qk, vo],
            out_specs=[half, half, qkv, att],
        ),
        compiler_params=pltpu.CompilerParams(
            dimension_semantics=("arbitrary",), vmem_limit_bytes=40 * 1024 * 1024
        ),
        cost_estimate=pl.CostEstimate(
            flops=2 * tokens * D * heads * 2 * rows,
            transcendentals=0,
            bytes_accessed=16 * 1024 * 1024,
        ),
        name="attn_forward",
    )(meta, normed, weights, weights)


def attn_backward_kernel(
    meta_ref,
    normed_ref,
    low_ref,
    qk_ref,
    vo_ref,
    qkv_ref,
    attended_ref,
    part_a,
    part_b,
    grad_ref,
    grads_s,
    mat_s,
):
    step = pl.program_id(0)
    normed = normed_ref[...]
    low = low_ref[...]
    out_weight = vo_ref[0, 0, HEAD:]
    grad_attended = dot_nt(low, out_weight)
    for image in range(2):
        rows = slice(image * PAD, (image + 1) * PAD)
        q = qkv_ref[0, rows, :HEAD]
        k = qkv_ref[0, rows, HEAD : 2 * HEAD]
        v = qkv_ref[0, rows, 2 * HEAD :]
        grad = grad_attended[rows].astype(jnp.bfloat16)
        probs = soft(q, k)
        grad_v = dot_tn(probs.astype(jnp.bfloat16), grad)
        grad_probs = dot_nt(grad, v)
        inner = jnp.sum(probs * grad_probs, axis=-1, keepdims=True)
        grad_scores = (probs * (grad_probs - inner) * (1.0 / math.sqrt(HEAD))).astype(jnp.bfloat16)
        grads_s[rows, :HEAD] = dot_nn(grad_scores, k)
        grads_s[rows, HEAD : 2 * HEAD] = dot_tn(grad_scores, q)
        grads_s[rows, 2 * HEAD :] = grad_v
    projected = grads_s[...].astype(jnp.bfloat16)
    mat_s[: 3 * HEAD] = dot_tn(projected, normed)
    mat_s[3 * HEAD :] = dot_tn(attended_ref[0], low)
    which = meta_ref[0]
    grad_ref[which, 0] = mat_s[: 2 * HEAD].astype(jnp.bfloat16)
    grad_ref[1 - which, 0] = mat_s[2 * HEAD :].astype(jnp.bfloat16)
    add = dot_nn(projected[:, : 2 * HEAD], qk_ref[0, 0]) + dot_nn(
        projected[:, 2 * HEAD :], vo_ref[0, 0, :HEAD]
    )

    accumulate(step, (part_a, part_b), add)


def attn_backward(meta, normed, low, weights, qkv_kept, attended):
    heads, rows = weights.shape[1:3]
    tokens = normed.shape[0]
    whole, half, qk, vo, qkv, att = attn_specs(rows, tokens)
    return pl.pallas_call(
        attn_backward_kernel,
        out_shape=[
            jax.ShapeDtypeStruct((tokens // 2, D), jnp.float32),
            jax.ShapeDtypeStruct((tokens // 2, D), jnp.float32),
            jax.ShapeDtypeStruct((2, heads, rows, D), jnp.bfloat16),
        ],
        grid_spec=pltpu.PrefetchScalarGridSpec(
            num_scalar_prefetch=1,
            grid=(heads,),
            in_specs=[whole, whole, qk, vo, qkv, att],
            out_specs=[half, half, pl.BlockSpec((2, 1, rows, D), lambda s, m: (0, s, 0, 0))],
            scratch_shapes=[
                pltpu.VMEM((tokens, 3 * HEAD), jnp.float32),
                pltpu.VMEM((2 * rows, D), jnp.float32),
            ],
        ),
        compiler_params=pltpu.CompilerParams(
            dimension_semantics=("arbitrary",), vmem_limit_bytes=48 * 1024 * 1024
        ),
        cost_estimate=pl.CostEstimate(
            flops=4 * tokens * D * heads * 2 * rows,
            transcendentals=0,
            bytes_accessed=24 * 1024 * 1024,
        ),
        name="attn_backward",
    )(meta, normed, low, weights, weights, qkv_kept, attended)


def chips(
    stream,
    skip_in,
    cotangent,
    skip_weight,
    qkv_weight,
    out_weight,
    up_weight,
    down_weight,
    norm_gain,
    norm_bias,
    row_skip,
    col_skip,
    row_qkv,
    col_qkv,
    row_out,
    col_out,
    row_up,
    col_up,
    row_down,
    col_down,
    second_gain,
    second_bias,
):
    bf16 = jnp.bfloat16
    f32 = jnp.float32
    axes = ("wide", "narrow")
    wide_count = lax.axis_size("wide")
    narrow_count = lax.axis_size("narrow")
    ZS, YS = narrow_count // 2, 2
    wide_index = lax.axis_index("wide")
    narrow_index = lax.axis_index("narrow")
    xi = wide_index // 2
    ci = wide_index % 2
    zi = narrow_index // 2
    yi = narrow_index % 2
    rows_local, feat = stream.shape
    half_head = feat // 2
    hidden = up_weight.shape[1]
    quarter = hidden // 4
    scale_factor = 1.0 / math.sqrt(HEAD)

    def perm(move):
        pairs = []
        for wide in range(wide_count):
            for narrow in range(narrow_count):
                x, c, z, y = move(wide // 2, wide % 2, narrow // 2, narrow % 2)
                target = (x * 2 + c) * narrow_count + z * 2 + y
                pairs.append((wide * narrow_count + narrow, target))
        return pairs

    def send(value, move):
        return lax.ppermute(value, axes, perm(move))

    def core(value):
        return send(value, lambda x, c, z, y: (x, 1 - c, z, y))

    def over_x(value):
        return send(value, lambda x, c, z, y: (1 - x, c, z, y))

    def over_y(value):
        return send(value, lambda x, c, z, y: (x, c, z, 1 - y))

    def over_z(value, step):
        return send(value, lambda x, c, z, y: (x, c, (z + step) % ZS, y))

    def xor_z(value, bit):
        return send(value, lambda x, c, z, y: (x, c, z ^ bit, y))

    def tie(*values):
        return lax.optimization_barrier(values)

    def tie(*values):
        return lax.optimization_barrier(values)

    def add_low(left, right):
        return (left.astype(f32) + right.astype(f32)).astype(bf16)

    def padded(own):
        return jnp.pad(own, ((0, PAD - SEQ), (0, 0)))

    def shifted(line, sign=1):
        return [pick(line, (zi + sign * step) % ZS, 0) for step in range(ZS)]

    def canonical(blocks, sign=1):
        stacked = jnp.stack(blocks)
        out = []
        for number in range(narrow_count):
            step = (sign * (zi - number // 2)) % ZS
            out.append(pick(pick(stacked, step, 0), yi ^ (number % 2), 0))
        return jnp.stack(out)

    def split_y(array):
        grid = array.reshape((ZS, YS) + array.shape[1:])
        return pick(grid, yi, 1), pick(grid, 1 - yi, 1)

    def z_pieces(near, far):
        both = jnp.stack([near, far])
        return [pick(both, (zi + step) % ZS, 1) for step in range(ZS)]

    def z_line(pieces):
        return [pieces[0]] + [over_z(pieces[step], step) for step in range(1, ZS)]

    half = ZS // 2
    meta = xi.astype(jnp.int32)[None]
    is_first = ci == 0

    mine = jnp.where(is_first, stream, skip_in)
    given = core(jnp.where(is_first, skip_in, stream))
    skip_block = pick(pick(skip_weight, ci, 0).reshape(2, feat // 2, D), xi, 0)
    skip_line = jnp.stack(z_line([skip_block] * ZS))
    tokens = jnp.stack([mine, given]).reshape(2, narrow_count, SEQ, feat).transpose(1, 0, 2, 3)
    token_near, token_give = split_y(tokens)
    token_far = over_y(token_give)

    skip_line, token_far, cotangent, qkv_weight, out_weight = tie(
        skip_line, token_far, cotangent, qkv_weight, out_weight
    )
    token_blocks = z_line(z_pieces(token_near, token_far))
    skip_beside = over_y(skip_line)
    skip_across = over_x(skip_line)
    attn_rows = jnp.concatenate(
        [
            pick(qkv_weight.transpose(1, 2, 0).reshape(3, 2, half_head, D), ci, 1),
            pick(out_weight.reshape(2, half_head, D), ci, 0)[None],
        ]
    ).reshape(2, 2 * half_head, D)
    attn_block = pick(attn_rows, xi, 0)
    cot_near, cot_give = split_y(cotangent.reshape(narrow_count, SEQ, feat))

    *token_blocks, skip_beside, skip_across, attn_block, cot_give = tie(
        *token_blocks, skip_beside, skip_across, attn_block, cot_give
    )
    attn_line = jnp.stack(z_line([attn_block] * ZS))
    skip_corner = jnp.concatenate([over_x(skip_beside[:half]), over_y(skip_across[half:])])
    cot_far = over_y(cot_give)
    flat = jnp.concatenate([block[j] for j in range(2) for block in token_blocks], axis=-1)
    flat = jnp.pad(flat, ((0, 0), (0, PAD - SEQ), (0, 0))).reshape(2 * PAD, D)
    skip_near = jnp.concatenate([skip_line, skip_beside])
    skip_away = jnp.concatenate([skip_across, skip_corner])
    skip_mat = jnp.where(
        xi == 0,
        jnp.stack([skip_near, skip_away], axis=1),
        jnp.stack([skip_away, skip_near], axis=1),
    ).reshape(D, D)
    ffn_block = jnp.stack(
        [
            lax.dynamic_slice_in_dim(up_weight, (ci * 2 + xi) * quarter, quarter, 1).T,
            lax.dynamic_slice_in_dim(down_weight, (ci * 2 + xi) * quarter, quarter, 0),
        ]
    )

    attn_line, cot_far, skip_mat, ffn_block = tie(attn_line, cot_far, skip_mat, ffn_block)
    attn_beside = over_y(attn_line)
    attn_across = over_x(attn_line)
    cot_blocks = z_line(z_pieces(cot_near, cot_far))
    ffn_full = lax.all_gather(ffn_block[None], "narrow", tiled=True)

    def both_images(own):
        own = padded(own)
        return jnp.concatenate([own, core(own)])

    def core_sum(kept, given):
        return (kept + core(given))[:SEQ]

    skip_part = matmul(flat, skip_mat, "rc,cd->rd")
    hidden_in = core_sum(skip_part[:PAD], skip_part[PAD:])
    unit_one, inverse_one = unit_parts(hidden_in)
    normed = both_images((unit_one * norm_gain[0] + norm_bias[0]).astype(bf16))

    normed, attn_beside, attn_across, *cot_blocks = tie(
        normed, attn_beside, attn_across, *cot_blocks
    )
    attn_corner = jnp.concatenate([over_x(attn_beside[:half]), over_y(attn_across[half:])])
    cot_own = canonical(cot_blocks).transpose(1, 0, 2).reshape(SEQ, D)
    cot_pair = padded(cot_own)
    cot_pair = jnp.concatenate([cot_pair, over_x(cot_pair)])
    attn_full = jnp.stack(
        [
            jnp.concatenate([attn_line, attn_beside]),
            jnp.concatenate([attn_across, attn_corner]),
        ]
    )
    attn_a, attn_b, qkv_kept, attended = attn_forward(meta, normed, attn_full)
    attn_b, cot_pair = tie(attn_b, cot_pair)
    middle = hidden_in + core_sum(attn_a, attn_b)
    unit_two, inverse_two = unit_parts(middle)
    mixed_own = padded((unit_two * norm_gain[1] + norm_bias[1]).astype(bf16))
    mixed_pair = jnp.concatenate([mixed_own, over_x(mixed_own)])
    mixed = jnp.concatenate([mixed_pair, core(mixed_pair)])
    cot = jnp.concatenate([cot_pair, core(cot_pair)])

    down_a, down_b, mixed_a, mixed_b, ffn_grad = ffn(mixed, cot, ffn_full)
    mixed_sum = mixed_a + core(mixed_b)
    mixed_far = over_x(mixed_sum[PAD:].astype(bf16))
    ffn_near, ffn_give = split_y(ffn_grad)
    ffn_far = over_y(ffn_give)

    mixed_far, down_b = tie(mixed_far, down_b)
    down_sum = down_a + core(down_b)
    down_far = over_x(down_sum[PAD:].astype(bf16))
    back_middle, gain_two, bias_two = norm_back_own(
        unit_two,
        inverse_two,
        (mixed_sum[:PAD] + mixed_far.astype(f32))[:SEQ],
        norm_gain[1],
    )
    grad_middle = cot_own.astype(f32) + back_middle
    middle_low = both_images(grad_middle.astype(bf16))
    normed_a, normed_b, attn_grad = attn_backward(
        meta, normed, middle_low, attn_full, qkv_kept, attended
    )

    normed_b, ffn_far, down_far = tie(normed_b, ffn_far, down_far)
    own, other = attn_grad[0], attn_grad[1]
    attn_from_x = over_x(other[ZS : ZS + half])
    attn_from_y = over_y(other[ZS + half :])
    ffn_total = add_low(ffn_near, ffn_far)
    ffn_pieces = z_line(shifted(ffn_total))
    block_own = (middle + (down_sum[:PAD] + down_far.astype(f32))[:SEQ]).astype(bf16)
    block_near, block_give = split_y(
        block_own.reshape(SEQ, narrow_count, feat).transpose(1, 0, 2)
    )
    block_far = over_y(block_give)
    back_hidden, gain_one, bias_one = norm_back_own(
        unit_one, inverse_one, core_sum(normed_a, normed_b), norm_gain[0]
    )
    hidden_low = both_images((grad_middle + back_hidden).astype(bf16))

    hidden_low, attn_from_x, attn_from_y, block_far = tie(
        hidden_low, attn_from_x, attn_from_y, block_far
    )
    attn_beside = over_y(
        jnp.concatenate([add_low(own[ZS : ZS + half], attn_from_x), own[ZS + half :]])
    )
    attn_across = over_x(
        jnp.concatenate([other[:half], add_low(other[half:ZS], attn_from_y)])
    )
    grad_skip = matmul(flat, hidden_low, "rc,rd->cd").astype(bf16)
    grad_skip = grad_skip.reshape(narrow_count, 2, feat // 2, D)
    skip_own, skip_other = pick(grad_skip, xi, 1), pick(grad_skip, 1 - xi, 1)
    token_grad = matmul(hidden_low, skip_mat, "rd,cd->rc").astype(bf16)
    kept_grads = token_grad.reshape(2, PAD, 2, ZS, feat)[:, :SEQ].transpose(2, 3, 0, 1, 4)

    attn_beside, attn_across, skip_own, skip_other, kept_grads, *ffn_pieces = tie(
        attn_beside, attn_across, skip_own, skip_other, kept_grads, *ffn_pieces
    )
    skip_from_x = over_x(skip_other[ZS : ZS + half])
    skip_from_y = over_y(skip_other[ZS + half :])
    attn_total = (
        own[:ZS].astype(f32) + attn_beside.astype(f32) + attn_across.astype(f32)
    ).astype(bf16)
    attn_pieces = [attn_total[0]] + [over_z(attn_total[step], -step) for step in range(1, ZS)]
    grads_far = over_y(kept_grads[1])
    ffn_own = sum(piece.astype(f32) for piece in ffn_pieces).astype(bf16)
    ffn_x = over_x(ffn_own)

    skip_from_x, skip_from_y, grads_far, ffn_x = tie(skip_from_x, skip_from_y, grads_far, ffn_x)
    skip_beside = over_y(
        jnp.concatenate(
            [add_low(skip_own[ZS : ZS + half], skip_from_x), skip_own[ZS + half :]]
        )
    )
    skip_across = over_x(
        jnp.concatenate([skip_other[:half], add_low(skip_other[half:ZS], skip_from_y)])
    )
    returned = jnp.stack([kept_grads[0], grads_far])
    backs = [returned[:, 0]] + [over_z(returned[:, step], -step) for step in range(1, ZS)]
    ffn_pair = jnp.stack([ffn_own, ffn_x])
    ffn_core = core(ffn_pair)

    skip_beside, skip_across, ffn_core, *attn_pieces = tie(
        skip_beside, skip_across, ffn_core, *attn_pieces
    )
    skip_total = (
        skip_own[:ZS].astype(f32) + skip_beside.astype(f32) + skip_across.astype(f32)
    ).astype(bf16)
    skip_pieces = [skip_total[0]] + [over_z(skip_total[step], -step) for step in range(1, ZS)]
    attn_own = sum(piece.astype(f32) for piece in attn_pieces).astype(bf16)
    attn_x = over_x(attn_own)
    block_blocks = z_line(z_pieces(block_near, block_far))

    *backs, attn_x = tie(*backs, attn_x)
    attn_pair = jnp.stack([attn_own, attn_x])
    attn_core = core(attn_pair)
    ordered = canonical(backs, -1)
    grad_mine = ordered[:, 0].reshape(rows_local, feat)
    grad_given = core(ordered[:, 1].reshape(rows_local, feat))
    grad_stream = jnp.where(is_first, grad_mine, grad_given).astype(f32)
    grad_skip_in = jnp.where(is_first, grad_given, grad_mine).astype(f32)
    block_out = canonical(block_blocks).reshape(rows_local, feat)
    skip_last = sum(piece.astype(f32) for piece in skip_pieces).astype(bf16)
    skip_pair = jnp.stack([skip_last, over_x(skip_last)])
    skip_core = core(skip_pair)

    def in_order(pair, other_core):
        four = jnp.stack([pair, other_core])
        return jnp.stack(
            [pick(pick(four, c ^ ci, 0), x ^ xi, 0) for c in range(2) for x in range(2)]
        )

    ffn_all = in_order(ffn_pair, ffn_core)
    up_all = ffn_all[:, 0].reshape(hidden, D)
    down_all = ffn_all[:, 1].reshape(hidden, D)
    attn_all = in_order(attn_pair, attn_core).reshape(2, 4, half_head, D)
    skip_all = in_order(skip_pair, skip_core).reshape(2, feat, D)
    qkv_all = attn_all[:, :3].transpose(1, 0, 2, 3).reshape(3, feat, D)
    out_all = attn_all[:, 3].reshape(feat, D)

    def all_narrow(value):
        value = value + over_y(value)
        bit = 1
        while bit < ZS:
            value = value + xor_z(value, bit)
            bit *= 2
        return value

    norm_sums = jnp.stack([gain_one, gain_two, bias_one, bias_two])
    norm_sums = norm_sums + core(norm_sums)
    norm_sums = norm_sums + over_x(norm_sums)

    grads = [
        skip_all.reshape(-1, D).astype(f32),
        qkv_all.reshape(-1, D).astype(f32),
        out_all.astype(f32),
        up_all.astype(f32),
        down_all.astype(f32),
    ]
    old_wide = (col_skip, row_qkv, col_out, row_up, col_down)
    old_narrow = (row_skip.reshape(-1), col_qkv.reshape(-1), row_out, col_up, row_down)
    row_along_wide = (False, True, False, True, False)
    wide_counts = (2 * D, 3 * D, D, FF, FF)
    entry_counts = (2 * D * D, 3 * D * D, D * D, D * FF, FF * D)
    new_narrow = []
    sums = []
    for number in range(5):
        grad = grads[number]
        squares = grad * grad + EPS_SQUARE
        narrow_new = DECAY * old_narrow[number] + (1.0 - DECAY) * (jnp.sum(squares, axis=1) / D)
        new_narrow.append(narrow_new)
        old_sum = jnp.zeros((D,), f32).at[0].set(jnp.sum(old_narrow[number]))
        sums.append(
            jnp.stack(
                [
                    jnp.sum(squares, axis=0),
                    jnp.sum(grad * grad * (1.0 / narrow_new)[:, None], axis=0),
                    old_sum,
                ]
            )
        )
    early = all_narrow(jnp.concatenate([sums[number] for number in range(1, 5)]))
    late = all_narrow(jnp.concatenate([sums[0], norm_sums]))
    totals = [late[:3]] + [early[3 * number : 3 * number + 3] for number in range(4)]
    gain_total = late[3:5]
    bias_total = late[5:7]

    new_wide = []
    steps = []
    ratios = []
    for number in range(5):
        wide_mean = totals[number][0] / wide_counts[number]
        wide_new = DECAY * old_wide[number] + (1.0 - DECAY) * wide_mean
        if row_along_wide[number]:
            row_mean = jnp.mean(wide_new)
        else:
            row_mean = DECAY * (totals[number][2][0] / wide_counts[number]) + (
                1.0 - DECAY
            ) * jnp.mean(wide_mean)
        square_total = jnp.sum(totals[number][1] / wide_new) * row_mean
        ratio = jnp.sqrt(square_total / entry_counts[number]) / CLIP_LEVEL
        ratios.append(ratio)
        factor = -(STEP_RATE * jnp.sqrt(row_mean) / jnp.maximum(1.0, ratio))
        step = (
            grads[number]
            * lax.rsqrt(new_narrow[number])[:, None]
            * (lax.rsqrt(wide_new) * factor)[None, :]
        )
        new_wide.append(wide_new)
        steps.append(step)
    clip_ratio = jnp.stack(ratios)

    def columns(array):
        size = D // wide_count
        return lax.dynamic_slice_in_dim(array, wide_index * size, size, array.ndim - 1)

    new_skip = skip_weight.astype(f32) + steps[0].reshape(2, feat, D)
    new_qkv = qkv_weight.astype(f32) + steps[1].reshape(3, feat, D).transpose(2, 0, 1)
    new_up = up_weight.astype(f32) + steps[3].T
    new_down = down_weight.astype(f32) + steps[4]
    new_second_gain, gain_step = plain_update(gain_total, second_gain)
    new_second_bias, bias_step = plain_update(bias_total, second_bias)
    return (
        block_out,
        grad_stream,
        grad_skip_in,
        columns(grads[0]).reshape(2, feat, -1),
        columns(grads[1]).reshape(3, feat, -1).transpose(2, 0, 1),
        columns(grads[2]),
        columns(grads[3]).T,
        columns(grads[4]),
        gain_total,
        bias_total,
        new_narrow[0].reshape(2, feat),
        new_wide[0],
        new_wide[1],
        new_narrow[1].reshape(3, feat),
        new_narrow[2],
        new_wide[2],
        new_wide[3],
        new_narrow[3],
        new_narrow[4],
        new_wide[4],
        new_second_gain,
        new_second_bias[0],
        new_second_bias[1],
        new_skip,
        new_qkv,
        steps[2],
        new_up,
        new_down,
        gain_step,
        bias_step,
        clip_ratio,
    )


def solution(mesh):
    wide, narrow = mesh.shape["wide"], mesh.shape["narrow"]
    body = chips if (wide == 4 and narrow == 8) else local
    in_specs = (
        P("wide", "narrow"),
        P("wide", "narrow"),
        P("wide", "narrow"),
        P(None, "narrow", None),
        P(None, None, "narrow"),
        P("narrow", None),
        P(None, "narrow"),
        P("narrow", None),
        P(),
        P(),
        P(None, "narrow"),
        P(),
        P(),
        P(None, "narrow"),
        P("narrow"),
        P(),
        P(),
        P("narrow"),
        P("narrow"),
        P(),
        P(),
        P(),
    )
    out_specs = (
        P("wide", "narrow"),
        P("wide", "narrow"),
        P("wide", "narrow"),
        P(None, "narrow", "wide"),
        P("wide", None, "narrow"),
        P("narrow", "wide"),
        P("wide", "narrow"),
        P("narrow", "wide"),
        P(),
        P(),
        P(None, "narrow"),
        P(),
        P(),
        P(None, "narrow"),
        P("narrow"),
        P(),
        P(),
        P("narrow"),
        P("narrow"),
        P(),
        P(),
        P(),
        P(),
        P(None, "narrow", None),
        P(None, None, "narrow"),
        P("narrow", None),
        P(None, "narrow"),
        P("narrow", None),
        P(),
        P(),
        P(),
    )
    return jax.shard_map(body, mesh=mesh, in_specs=in_specs, out_specs=out_specs, check_vma=False)
```

```python
import math

import jax
import jax.numpy as jnp
from jax import lax
from jax.experimental import pallas as pl
from jax.experimental.pallas import tpu as pltpu
from jax.sharding import PartitionSpec as P

D = 1152
FF = 4608
SEQ = 258
HEAD = 72


NORM_EPS = 1e-05
EPS_SQUARE = 1e-30
DECAY = 0.5
STEP_RATE = 0.05
CLIP_LEVEL = 0.25


def layer_norm(values, gain, shift):
    average = jnp.mean(values, axis=-1, keepdims=True)
    centered = values - average
    variance = jnp.mean(centered * centered, axis=-1, keepdims=True)
    return centered * lax.rsqrt(variance + NORM_EPS) * gain + shift


def norm_back(values, grad, gain, own_rows):
    average = jnp.mean(values, axis=-1, keepdims=True)
    centered = values - average
    variance = jnp.mean(centered * centered, axis=-1, keepdims=True)
    inverse = lax.rsqrt(variance + NORM_EPS)
    unit = centered * inverse
    scaled = grad * gain
    inner = (
        scaled
        - jnp.mean(scaled, axis=-1, keepdims=True)
        - unit * jnp.mean(scaled * unit, axis=-1, keepdims=True)
    )
    weighted = grad * own_rows
    return (inner * inverse, jnp.sum(weighted * unit, axis=0), jnp.sum(weighted, axis=0))


def gelu_exact(inputs):
    return jax.nn.gelu(inputs, approximate=False)


def matmul(left, right, form):
    return jnp.einsum(form, left, right, preferred_element_type=jnp.float32)


def plain_update(grad, second_old):
    second_new = DECAY * second_old + (1.0 - DECAY) * (grad * grad + EPS_SQUARE)
    update = grad * lax.rsqrt(second_new)
    spread = jnp.sqrt(jnp.mean(update * update))
    update = update / jnp.maximum(1.0, spread / CLIP_LEVEL)
    return (second_new, -(STEP_RATE * update))


def wide_slice(array, dim_index, count, wide_index):
    piece_size = array.shape[dim_index] // count
    return lax.dynamic_slice_in_dim(array, wide_index * piece_size, piece_size, dim_index)


def local(
    stream,
    skip_in,
    cotangent,
    skip_weight,
    qkv_weight,
    out_weight,
    up_weight,
    down_weight,
    norm_gain,
    norm_bias,
    row_skip,
    col_skip,
    row_qkv,
    col_qkv,
    row_out,
    col_out,
    row_up,
    col_up,
    row_down,
    col_down,
    second_gain,
    second_bias,
):
    rows_local, feat_local = stream.shape
    images = rows_local // SEQ
    heads_local = feat_local // HEAD
    scale_factor = 1.0 / math.sqrt(HEAD)
    split_shape = (images, SEQ, heads_local, HEAD)
    narrow_count = lax.axis_size("narrow")
    narrow_index = lax.axis_index("narrow")
    share_rows = -(-rows_local // narrow_count)
    row_start = narrow_index * share_rows
    row_ids = lax.broadcasted_iota(jnp.int32, (rows_local, 1), 0)
    own_mask = ((row_ids >= row_start) & (row_ids < row_start + share_rows)).astype(jnp.float32)

    def full_sum(values):
        return lax.psum(values, "narrow")

    partial_in = matmul(stream, skip_weight[0], "rc,cd->rd") + matmul(
        skip_in, skip_weight[1], "rc,cd->rd"
    )
    hidden_in = full_sum(partial_in)
    normed = layer_norm(hidden_in, norm_gain[0], norm_bias[0]).astype(jnp.bfloat16)
    projected = matmul(normed, qkv_weight, "rd,dtc->rtc").astype(jnp.bfloat16)
    queries = projected[:, 0].reshape(split_shape)
    key_vectors = projected[:, 1].reshape(split_shape)
    value_vectors = projected[:, 2].reshape(split_shape)
    scores = matmul(queries, key_vectors, "bqhe,bkhe->bhqk") * scale_factor
    row_max = jnp.max(scores, axis=-1, keepdims=True)
    exponent = jnp.exp(scores - row_max)
    row_total = jnp.sum(exponent, axis=-1, keepdims=True)
    log_total = row_max + jnp.log(row_total)
    probs_low = (exponent / row_total).astype(jnp.bfloat16)
    attended = (
        matmul(probs_low, value_vectors, "bhqk,bkhe->bqhe")
        .reshape(rows_local, feat_local)
        .astype(jnp.bfloat16)
    )
    attn_part = matmul(attended, out_weight, "rc,cd->rd")
    middle = hidden_in + full_sum(attn_part)
    mixed_in = layer_norm(middle, norm_gain[1], norm_bias[1]).astype(jnp.bfloat16)
    middle_own = lax.dynamic_slice_in_dim(middle, narrow_index * feat_local, feat_local, 1)
    up_input = matmul(mixed_in, up_weight, "rd,df->rf")
    activation = gelu_exact(up_input).astype(jnp.bfloat16)
    down_part = matmul(activation, down_weight, "rf,fd->rd")
    block_out = (
        middle_own + lax.psum_scatter(down_part, "narrow", scatter_dimension=1, tiled=True)
    ).astype(jnp.bfloat16)
    grad_full = lax.all_gather(cotangent, "narrow", axis=1, tiled=True)
    grad_down = matmul(activation, grad_full, "rf,rd->fd")
    grad_act = matmul(grad_full, down_weight, "rd,fd->rf")
    gelu_value, gelu_back = jax.vjp(gelu_exact, up_input)
    grad_up_in = gelu_back(grad_act)[0].astype(jnp.bfloat16)
    grad_up = matmul(mixed_in, grad_up_in, "rd,rf->df")
    mixed_part = matmul(grad_up_in, up_weight, "rf,df->rd")
    grad_mixed = full_sum(mixed_part)
    back_middle, back_gain_two, back_bias_two = norm_back(
        middle, grad_mixed, norm_gain[1], own_mask
    )
    grad_middle = grad_full.astype(jnp.float32) + back_middle
    middle_low = grad_middle.astype(jnp.bfloat16)
    grad_out = matmul(attended, middle_low, "rc,rd->cd")
    grad_attended = (
        matmul(middle_low, out_weight, "rd,cd->rc").astype(jnp.bfloat16).reshape(split_shape)
    )
    scores_again = matmul(queries, key_vectors, "bqhe,bkhe->bhqk") * scale_factor
    probs = jnp.exp(scores_again - log_total)
    probs_again = probs.astype(jnp.bfloat16)
    grad_values = matmul(probs_again, grad_attended, "bhqk,bqhe->bkhe")
    grad_probs = matmul(grad_attended, value_vectors, "bqhe,bkhe->bhqk")
    inner_sum = jnp.sum(probs * grad_probs, axis=-1, keepdims=True)
    grad_scores = (probs * (grad_probs - inner_sum) * scale_factor).astype(jnp.bfloat16)
    grad_queries = matmul(grad_scores, key_vectors, "bhqk,bkhe->bqhe")
    grad_keys = matmul(grad_scores, queries, "bhqk,bqhe->bkhe")
    grad_projected = jnp.stack(
        [
            grad_queries.reshape(rows_local, feat_local),
            grad_keys.reshape(rows_local, feat_local),
            grad_values.reshape(rows_local, feat_local),
        ],
        axis=1,
    ).astype(jnp.bfloat16)
    grad_qkv = matmul(normed, grad_projected, "rd,rtc->dtc")
    normed_part = matmul(grad_projected, qkv_weight, "rtc,dtc->rd")
    grad_normed = full_sum(normed_part)
    back_hidden, back_gain_one, back_bias_one = norm_back(
        hidden_in, grad_normed, norm_gain[0], own_mask
    )
    hidden_low = (grad_middle + back_hidden).astype(jnp.bfloat16)
    grad_skip = jnp.stack(
        [matmul(stream, hidden_low, "rc,rd->cd"), matmul(skip_in, hidden_low, "rc,rd->cd")]
    )
    grad_stream = matmul(hidden_low, skip_weight[0], "rd,cd->rc")
    grad_skip_in = matmul(hidden_low, skip_weight[1], "rd,cd->rc")
    gain_grads = jnp.stack([back_gain_one, back_gain_two])
    bias_grads = jnp.stack([back_bias_one, back_bias_two])
    wide_count = lax.axis_size("wide")
    wide_index = lax.axis_index("wide")
    wide_dims = (2, 0, 1, 0, 1)
    wide_axes = ((0, 1), (1, 2), (0,), (1,), (0,))
    narrow_axes = ((2,), (0,), (1,), (0,), (1,))
    wide_counts = (2 * D, 3 * D, D, FF, FF)
    row_along_wide = (False, True, False, True, False)
    entry_counts = (2 * D * D, 3 * D * D, D * D, D * FF, FF * D)
    old_slots = (0, 0, 1, 0, 2)
    weights = (skip_weight, qkv_weight, out_weight, up_weight, down_weight)
    old_wide = (col_skip, row_qkv, col_out, row_up, col_down)
    old_narrow = (row_skip, col_qkv, row_out, col_up, row_down)
    summed = lax.psum(
        (grad_skip, grad_qkv, grad_out, grad_up, grad_down, gain_grads, bias_grads), "wide"
    )
    pieces = summed[:5]
    gain_section = summed[5]
    bias_section = summed[6]
    squares = [piece * piece + EPS_SQUARE for piece in pieces]
    wide_parts = [jnp.sum(squares[number], axis=wide_axes[number]) for number in range(5)]
    narrow_parts = [jnp.sum(squares[number], axis=narrow_axes[number]) for number in range(5)]
    old_sums = jnp.stack([jnp.sum(row_skip), jnp.sum(row_out), jnp.sum(row_down)])
    stat_total = lax.psum(
        (
            wide_parts[0],
            wide_parts[1],
            wide_parts[2],
            wide_parts[3],
            wide_parts[4],
            old_sums,
            gain_section,
            bias_section,
        ),
        "narrow",
    )
    old_row_means = (stat_total[5][0] / (2 * D), stat_total[5][1] / D, stat_total[5][2] / FF)
    wide_stats = stat_total[:5]
    gain_total = stat_total[6]
    bias_total = stat_total[7]
    new_wide = []
    new_narrow = []
    updates = []
    for number in range(5):
        wide_mean = wide_stats[number] / wide_counts[number]
        wide_new = DECAY * old_wide[number] + (1.0 - DECAY) * wide_mean
        narrow_new = DECAY * old_narrow[number] + (1.0 - DECAY) * narrow_parts[number] / D
        if row_along_wide[number]:
            row_mean = jnp.mean(wide_new)
        else:
            row_mean = DECAY * old_row_means[old_slots[number]] + (1.0 - DECAY) * jnp.mean(
                wide_mean
            )
        dim_index = wide_dims[number]
        piece_size = pieces[number].shape[dim_index]
        broadcast_shape = [1] * pieces[number].ndim
        broadcast_shape[dim_index] = piece_size
        second = (
            jnp.expand_dims(narrow_new, dim_index) * wide_new.reshape(broadcast_shape) / row_mean
        )
        updates.append(pieces[number] * lax.rsqrt(second))
        new_wide.append(wide_new)
        new_narrow.append(narrow_new)
    update_squares = jnp.stack([jnp.sum(update * update) for update in updates])
    square_totals = lax.psum(update_squares, "narrow")
    counts_array = jnp.array(entry_counts, jnp.float32)
    clip_ratio = jnp.sqrt(square_totals / counts_array) / CLIP_LEVEL
    new_pieces = []
    for number in range(5):
        spread = jnp.sqrt(square_totals[number] / entry_counts[number])
        step_piece = -(STEP_RATE * (updates[number] / jnp.maximum(1.0, spread / CLIP_LEVEL)))
        if number == 2:
            new_pieces.append(step_piece)
        else:
            weight_piece = weights[number]
            new_pieces.append(weight_piece.astype(jnp.float32) + step_piece)
    grad_outs = [
        wide_slice(pieces[number], wide_dims[number], wide_count, wide_index) for number in range(5)
    ]
    new_second_gain, gain_step = plain_update(gain_total, second_gain)
    new_second_bias, bias_step = plain_update(bias_total, second_bias)
    return (
        block_out,
        grad_stream,
        grad_skip_in,
        grad_outs[0],
        grad_outs[1],
        grad_outs[2],
        grad_outs[3],
        grad_outs[4],
        gain_total,
        bias_total,
        new_narrow[0],
        new_wide[0],
        new_wide[1],
        new_narrow[1],
        new_narrow[2],
        new_wide[2],
        new_wide[3],
        new_narrow[3],
        new_narrow[4],
        new_wide[4],
        new_second_gain,
        new_second_bias[0],
        new_second_bias[1],
        new_pieces[0],
        new_pieces[1],
        new_pieces[2],
        new_pieces[3],
        new_pieces[4],
        gain_step,
        bias_step,
        clip_ratio,
    )


def unit_parts(values):
    average = jnp.mean(values, axis=-1, keepdims=True)
    centered = values - average
    variance = jnp.mean(centered * centered, axis=-1, keepdims=True)
    inverse = lax.rsqrt(variance + NORM_EPS)
    return centered * inverse, inverse


def norm_back_own(unit, inverse, grad, gain):
    scaled = grad * gain
    inner = (
        scaled
        - jnp.mean(scaled, axis=-1, keepdims=True)
        - unit * jnp.mean(scaled * unit, axis=-1, keepdims=True)
    )
    rows = tuple(range(grad.ndim - 1))
    return inner * inverse, jnp.sum(grad * unit, axis=rows), jnp.sum(grad, axis=rows)


def pick(array, index, axis):
    return lax.dynamic_index_in_dim(array, index, axis, keepdims=False)


PAD = 272


def dot_nt(left, right):
    return lax.dot_general(left, right, (((1,), (1,)), ((), ())), preferred_element_type=jnp.float32)


def dot_nn(left, right):
    return lax.dot_general(left, right, (((1,), (0,)), ((), ())), preferred_element_type=jnp.float32)


def dot_tn(left, right):
    return lax.dot_general(left, right, (((0,), (0,)), ((), ())), preferred_element_type=jnp.float32)


def accumulate(step, refs, value):
    size = refs[0].shape[0]

    @pl.when(step == 0)
    def _():
        for number, ref in enumerate(refs):
            ref[...] = value[number * size : (number + 1) * size]

    @pl.when(step > 0)
    def _():
        for number, ref in enumerate(refs):
            ref[...] += value[number * size : (number + 1) * size]


def ffn_kernel(order_ref, mixed_ref, cot_ref, *refs):
    blocks = 4
    weights, (down_a, down_b, mixed_a, mixed_b), grads = refs[:blocks], refs[blocks : blocks + 4], refs[blocks + 4 :]
    step = pl.program_id(0)
    mixed = mixed_ref[...]
    cot = cot_ref[...]
    up = jnp.concatenate([ref[0, 0] for ref in weights], axis=0)
    down = jnp.concatenate([ref[0, 1] for ref in weights], axis=0)
    up_input = dot_nt(mixed, up)
    gate = 0.5 * (1.0 + lax.erf(up_input * (1.0 / math.sqrt(2.0))))
    activation = (up_input * gate).astype(jnp.bfloat16)
    slope = gate + up_input * (jnp.exp(-0.5 * up_input * up_input) * (1.0 / math.sqrt(2.0 * math.pi)))
    grad_up_in = (dot_nt(cot, down) * slope).astype(jnp.bfloat16)
    grad_up = dot_tn(grad_up_in, mixed).astype(jnp.bfloat16)
    grad_down = dot_tn(activation, cot).astype(jnp.bfloat16)
    for j in range(2):

        @pl.when(step == j)
        def _():
            grads[j][...] = grad_up.reshape(grads[j].shape)
            grads[2 + j][...] = grad_down.reshape(grads[j].shape)

    accumulate(step, (mixed_a, mixed_b), dot_nn(grad_up_in, up))
    accumulate(step, (down_a, down_b), dot_nn(activation, down))


def ffn(order, mixed, cot, weights):
    count, _, rows, _ = weights.shape
    tokens = mixed.shape[0]
    blocks = 4
    whole = pl.BlockSpec((tokens, D), lambda t, m: (0, 0))
    half = pl.BlockSpec((tokens // 2, D), lambda t, m: (0, 0))

    def weight_spec(slot):
        return pl.BlockSpec((1, 2, rows, D), lambda t, m: (m[blocks * t + slot], 0, 0, 0))

    grad_block = pl.BlockSpec((blocks, rows, D), lambda t, m: (0, 0, 0))
    part = jax.ShapeDtypeStruct((tokens // 2, D), jnp.float32)
    grad = jax.ShapeDtypeStruct((blocks, rows, D), jnp.bfloat16)
    return pl.pallas_call(
        ffn_kernel,
        out_shape=[part] * 4 + [grad] * 4,
        grid_spec=pltpu.PrefetchScalarGridSpec(
            num_scalar_prefetch=1,
            grid=(count // blocks,),
            in_specs=[whole, whole] + [weight_spec(slot) for slot in range(blocks)],
            out_specs=[half] * 4 + [grad_block] * 4,
        ),
        compiler_params=pltpu.CompilerParams(
            dimension_semantics=("arbitrary",), vmem_limit_bytes=60 * 1024 * 1024
        ),
        cost_estimate=pl.CostEstimate(
            flops=12 * tokens * D * count * rows, transcendentals=0, bytes_accessed=32 * 1024 * 1024
        ),
        name="ffn",
    )(order, mixed, cot, *([weights] * blocks))


def soft(q, k):
    scores = dot_nt(q, k) * (1.0 / math.sqrt(HEAD))
    column = lax.broadcasted_iota(jnp.int32, scores.shape, 1)
    scores = jnp.where(column < SEQ, scores, -1e30)
    exponent = jnp.exp(scores - jnp.max(scores, axis=-1, keepdims=True))
    return exponent / jnp.sum(exponent, axis=-1, keepdims=True)


def attn_forward_kernel(meta_ref, normed_ref, qk_ref, vo_ref, part_a, part_b, qkv_ref, attended_ref):
    step = pl.program_id(0)
    normed = normed_ref[...]
    qk = dot_nt(normed, qk_ref[0, 0])
    v_all = dot_nt(normed, vo_ref[0, 0, :HEAD])
    out_weight = vo_ref[0, 0, HEAD:]
    qkv_ref[0, :, : 2 * HEAD] = qk.astype(jnp.bfloat16)
    qkv_ref[0, :, 2 * HEAD :] = v_all.astype(jnp.bfloat16)
    for image in range(2):
        rows = slice(image * PAD, (image + 1) * PAD)
        q = qk[rows, :HEAD].astype(jnp.bfloat16)
        k = qk[rows, HEAD:].astype(jnp.bfloat16)
        v = v_all[rows].astype(jnp.bfloat16)
        probs = soft(q, k).astype(jnp.bfloat16)
        attended_ref[0, rows] = dot_nn(probs, v).astype(jnp.bfloat16)
    add = dot_nn(attended_ref[0], out_weight)

    accumulate(step, (part_a, part_b), add)


def attn_specs(rows, tokens):
    whole = pl.BlockSpec((tokens, D), lambda s, m: (0, 0))
    half = pl.BlockSpec((tokens // 2, D), lambda s, m: (0, 0))
    qk = pl.BlockSpec((1, 1, rows, D), lambda s, m: (m[0], s, 0, 0))
    vo = pl.BlockSpec((1, 1, rows, D), lambda s, m: (1 - m[0], s, 0, 0))
    qkv = pl.BlockSpec((1, tokens, 3 * HEAD), lambda s, m: (s, 0, 0))
    att = pl.BlockSpec((1, tokens, HEAD), lambda s, m: (s, 0, 0))
    return whole, half, qk, vo, qkv, att


def attn_forward(meta, normed, weights):
    heads, rows = weights.shape[1:3]
    tokens = normed.shape[0]
    whole, half, qk, vo, qkv, att = attn_specs(rows, tokens)
    return pl.pallas_call(
        attn_forward_kernel,
        out_shape=[
            jax.ShapeDtypeStruct((tokens // 2, D), jnp.float32),
            jax.ShapeDtypeStruct((tokens // 2, D), jnp.float32),
            jax.ShapeDtypeStruct((heads, tokens, 3 * HEAD), jnp.bfloat16),
            jax.ShapeDtypeStruct((heads, tokens, HEAD), jnp.bfloat16),
        ],
        grid_spec=pltpu.PrefetchScalarGridSpec(
            num_scalar_prefetch=1,
            grid=(heads,),
            in_specs=[whole, qk, vo],
            out_specs=[half, half, qkv, att],
        ),
        compiler_params=pltpu.CompilerParams(
            dimension_semantics=("arbitrary",), vmem_limit_bytes=40 * 1024 * 1024
        ),
        cost_estimate=pl.CostEstimate(
            flops=2 * tokens * D * heads * 2 * rows,
            transcendentals=0,
            bytes_accessed=16 * 1024 * 1024,
        ),
        name="attn_forward",
    )(meta, normed, weights, weights)


def attn_backward_kernel(
    meta_ref,
    normed_ref,
    low_ref,
    qk_ref,
    vo_ref,
    qkv_ref,
    attended_ref,
    part_a,
    part_b,
    own_ref,
    near_ref,
    far_x_ref,
    far_y_ref,
    grads_s,
    mat_s,
):
    step = pl.program_id(0)
    normed = normed_ref[...]
    low = low_ref[...]
    out_weight = vo_ref[0, 0, HEAD:]
    grad_attended = dot_nt(low, out_weight)
    for image in range(2):
        rows = slice(image * PAD, (image + 1) * PAD)
        q = qkv_ref[0, rows, :HEAD]
        k = qkv_ref[0, rows, HEAD : 2 * HEAD]
        v = qkv_ref[0, rows, 2 * HEAD :]
        grad = grad_attended[rows].astype(jnp.bfloat16)
        probs = soft(q, k)
        grad_v = dot_tn(probs.astype(jnp.bfloat16), grad)
        grad_probs = dot_nt(grad, v)
        inner = jnp.sum(probs * grad_probs, axis=-1, keepdims=True)
        grad_scores = (probs * (grad_probs - inner) * (1.0 / math.sqrt(HEAD))).astype(jnp.bfloat16)
        grads_s[rows, :HEAD] = dot_nn(grad_scores, k)
        grads_s[rows, HEAD : 2 * HEAD] = dot_tn(grad_scores, q)
        grads_s[rows, 2 * HEAD :] = grad_v
    projected = grads_s[...].astype(jnp.bfloat16)
    mat_s[: 3 * HEAD] = dot_tn(projected, normed)
    mat_s[3 * HEAD :] = dot_tn(attended_ref[0], low)
    first = meta_ref[0] == 0
    query_key = mat_s[: 2 * HEAD]
    value_out = mat_s[2 * HEAD :]
    own_ref[0] = jnp.where(first, query_key, value_out).astype(jnp.bfloat16)
    other = jnp.where(first, value_out, query_key).astype(jnp.bfloat16)

    @pl.when(step < 4)
    def _():
        near_ref[0] = other

    @pl.when((step >= 4) & (step < 6))
    def _():
        far_x_ref[0] = other

    @pl.when(step >= 6)
    def _():
        far_y_ref[0] = other

    add = dot_nn(projected[:, : 2 * HEAD], qk_ref[0, 0]) + dot_nn(
        projected[:, 2 * HEAD :], vo_ref[0, 0, :HEAD]
    )

    accumulate(step, (part_a, part_b), add)


def attn_backward(meta, normed, low, weights, qkv_kept, attended):
    heads, rows = weights.shape[1:3]
    tokens = normed.shape[0]
    whole, half, qk, vo, qkv, att = attn_specs(rows, tokens)
    return pl.pallas_call(
        attn_backward_kernel,
        out_shape=[
            jax.ShapeDtypeStruct((tokens // 2, D), jnp.float32),
            jax.ShapeDtypeStruct((tokens // 2, D), jnp.float32),
            jax.ShapeDtypeStruct((heads, rows, D), jnp.bfloat16),
            jax.ShapeDtypeStruct((4, rows, D), jnp.bfloat16),
            jax.ShapeDtypeStruct((2, rows, D), jnp.bfloat16),
            jax.ShapeDtypeStruct((2, rows, D), jnp.bfloat16),
        ],
        grid_spec=pltpu.PrefetchScalarGridSpec(
            num_scalar_prefetch=1,
            grid=(heads,),
            in_specs=[whole, whole, qk, vo, qkv, att],
            out_specs=[
                half,
                half,
                pl.BlockSpec((1, rows, D), lambda s, m: (s, 0, 0)),
                pl.BlockSpec((1, rows, D), lambda s, m: (jnp.minimum(s, 3), 0, 0)),
                pl.BlockSpec((1, rows, D), lambda s, m: (jnp.clip(s - 4, 0, 1), 0, 0)),
                pl.BlockSpec((1, rows, D), lambda s, m: (jnp.clip(s - 6, 0, 1), 0, 0)),
            ],
            scratch_shapes=[
                pltpu.VMEM((tokens, 3 * HEAD), jnp.float32),
                pltpu.VMEM((2 * rows, D), jnp.float32),
            ],
        ),
        compiler_params=pltpu.CompilerParams(
            dimension_semantics=("arbitrary",), vmem_limit_bytes=48 * 1024 * 1024
        ),
        cost_estimate=pl.CostEstimate(
            flops=4 * tokens * D * heads * 2 * rows,
            transcendentals=0,
            bytes_accessed=24 * 1024 * 1024,
        ),
        name="attn_backward",
    )(meta, normed, low, weights, weights, qkv_kept, attended)


def chips(
    stream,
    skip_in,
    cotangent,
    skip_weight,
    qkv_weight,
    out_weight,
    up_weight,
    down_weight,
    norm_gain,
    norm_bias,
    row_skip,
    col_skip,
    row_qkv,
    col_qkv,
    row_out,
    col_out,
    row_up,
    col_up,
    row_down,
    col_down,
    second_gain,
    second_bias,
):
    bf16 = jnp.bfloat16
    f32 = jnp.float32
    axes = ("wide", "narrow")
    wide_count = lax.axis_size("wide")
    narrow_count = lax.axis_size("narrow")
    ZS, YS = narrow_count // 2, 2
    wide_index = lax.axis_index("wide")
    narrow_index = lax.axis_index("narrow")
    xi = wide_index // 2
    ci = wide_index % 2
    zi = narrow_index // 2
    yi = narrow_index % 2
    rows_local, feat = stream.shape
    half_head = feat // 2
    hidden = up_weight.shape[1]
    quarter = hidden // 4
    scale_factor = 1.0 / math.sqrt(HEAD)

    def perm(move):
        pairs = []
        for wide in range(wide_count):
            for narrow in range(narrow_count):
                x, c, z, y = move(wide // 2, wide % 2, narrow // 2, narrow % 2)
                target = (x * 2 + c) * narrow_count + z * 2 + y
                pairs.append((wide * narrow_count + narrow, target))
        return pairs

    def send(value, move):
        return lax.ppermute(value, axes, perm(move))

    def core(value):
        return send(value, lambda x, c, z, y: (x, 1 - c, z, y))

    def over_x(value):
        return send(value, lambda x, c, z, y: (1 - x, c, z, y))

    def over_y(value):
        return send(value, lambda x, c, z, y: (x, c, z, 1 - y))

    def xor_z(value, bit):
        return send(value, lambda x, c, z, y: (x, c, z ^ bit, y))

    def tie(*values):
        return lax.optimization_barrier(values)

    def tie(*values):
        return lax.optimization_barrier(values)

    def add_low(left, right):
        return (left.astype(f32) + right.astype(f32)).astype(bf16)

    def padded(own):
        return jnp.pad(own, ((0, PAD - SEQ), (0, 0)))

    distances = [0]
    bit = ZS // 2
    while bit:
        distances += [distance ^ bit for distance in distances]
        bit //= 2

    def gather_z(block):
        line = block[None]
        bit = ZS // 2
        while bit:
            line = jnp.concatenate([line, xor_z(line, bit)])
            bit //= 2
        return line

    order = jnp.stack(
        [(zi ^ distance) * 2 + (yi ^ j) for j in range(2) for distance in distances]
    ).astype(jnp.int32)

    def canonical(blocks):
        def exchange(table, flag, bit, width):
            return [
                jnp.where(flag == 0, table[index], table[index ^ bit]) for index in range(width)
            ]

        table = [None] * narrow_count
        for place, distance in enumerate(distances):
            for j in range(2):
                table[distance * 2 + j] = blocks[j * ZS + place]
        bit = 1
        while bit < narrow_count:
            table = exchange(table, (narrow_index // bit) % 2, bit, narrow_count)
            bit *= 2
        return table

    def split_y(array):
        grid = array.reshape((ZS, YS) + array.shape[1:])
        return pick(grid, yi, 1), pick(grid, 1 - yi, 1)

    def z_pieces(near, far):
        return [
            jnp.concatenate([pick(near, zi ^ distance, 0), pick(far, zi ^ distance, 0)], axis=-1)
            for distance in distances
        ]

    def z_line(pieces):
        return [pieces[0]] + [
            xor_z(piece, distance) for piece, distance in zip(pieces[1:], distances[1:])
        ]

    def halves_z(total):
        return total[: ZS // 2], total[ZS // 2 :]

    half = ZS // 2
    meta = xi.astype(jnp.int32)[None]
    is_first = ci == 0

    def in_order(pair, other_core):
        four = jnp.stack([pair, other_core])
        return jnp.stack(
            [pick(pick(four, c ^ ci, 0), x ^ xi, 0) for c in range(2) for x in range(2)]
        )

    def all_narrow(value):
        value = value + over_y(value)
        bit = 1
        while bit < ZS:
            value = value + xor_z(value, bit)
            bit *= 2
        return value

    def columns(array):
        size = D // wide_count
        return lax.dynamic_slice_in_dim(array, wide_index * size, size, array.ndim - 1)

    def statistics(grad, old):
        squares = grad * grad + EPS_SQUARE
        new = DECAY * old + (1.0 - DECAY) * (jnp.sum(squares, axis=1) / D)
        old_sum = jnp.where(lax.broadcasted_iota(jnp.int32, (D,), 0) == 0, jnp.sum(old), 0.0)
        sums = [
            jnp.sum(squares, axis=0),
            jnp.sum(grad * grad * (1.0 / new)[:, None], axis=0),
            old_sum,
        ]
        return new, sums

    def step_of(grad, new, totals, old_wide, rows_all, row_along_wide):
        wide_mean = totals[0] / rows_all
        wide_new = DECAY * old_wide + (1.0 - DECAY) * wide_mean
        if row_along_wide:
            row_mean = jnp.mean(wide_new)
        else:
            row_mean = DECAY * (totals[2][0] / rows_all) + (1.0 - DECAY) * jnp.mean(wide_mean)
        square_total = jnp.sum(totals[1] / wide_new) * row_mean
        ratio = jnp.sqrt(square_total / (rows_all * D)) / CLIP_LEVEL
        factor = -(STEP_RATE * jnp.sqrt(row_mean) / jnp.maximum(1.0, ratio))
        step = grad * lax.rsqrt(new)[:, None] * (lax.rsqrt(wide_new) * factor)[None, :]
        return wide_new, ratio, step

    mine = jnp.where(is_first, stream, skip_in)
    given = core(jnp.where(is_first, skip_in, stream))
    skip_block = pick(pick(skip_weight, ci, 0).reshape(2, feat // 2, D), xi, 0)
    attn_rows = jnp.concatenate(
        [
            pick(qkv_weight.transpose(1, 2, 0).reshape(3, 2, half_head, D), ci, 1),
            pick(out_weight.reshape(2, half_head, D), ci, 0)[None],
        ]
    ).reshape(2, 2 * half_head, D)
    attn_block = pick(attn_rows, xi, 0)
    skip_two = xor_z(skip_block, 2)
    attn_two = xor_z(attn_block, 2)
    tokens = jnp.concatenate([mine, given, cotangent], axis=1).reshape(narrow_count, SEQ, 3 * feat)
    token_near, token_give = split_y(tokens)
    token_far = over_y(token_give)
    skip_two, attn_two, token_near = tie(skip_two, attn_two, token_near)
    skip_line = jnp.stack([skip_block, skip_two])
    attn_line = jnp.stack([attn_block, attn_two])
    skip_line = jnp.concatenate([skip_line, xor_z(skip_line, 1)])
    attn_line = jnp.concatenate([attn_line, xor_z(attn_line, 1)])

    token_blocks = z_line(z_pieces(token_near, token_far))
    skip_beside = over_y(skip_line)
    skip_across = over_x(skip_line)
    ffn_block = jnp.stack(
        [
            lax.dynamic_slice_in_dim(up_weight, (ci * 2 + xi) * quarter, quarter, 1).T,
            lax.dynamic_slice_in_dim(down_weight, (ci * 2 + xi) * quarter, quarter, 0),
        ]
    )

    skip_beside, skip_across, attn_line = tie(skip_beside, skip_across, attn_line)
    skip_corner = jnp.concatenate([over_x(skip_beside[:half]), over_y(skip_across[half:])])
    attn_beside = over_y(attn_line)
    attn_across = over_x(attn_line)

    *token_blocks, skip_corner, ffn_block = tie(*token_blocks, skip_corner, ffn_block)
    ffn_full = lax.all_gather(ffn_block[None], "narrow", tiled=True)
    parts = [
        [
            block[:, (3 * j + kind) * feat : (3 * j + kind + 1) * feat]
            for j in range(2)
            for block in token_blocks
        ]
        for kind in range(3)
    ]
    flat = jnp.concatenate(
        [padded(jnp.concatenate(parts[kind], axis=1)) for kind in range(2)]
    )
    flat, attn_beside, attn_across = tie(flat, attn_beside, attn_across)
    attn_corner_x = over_x(attn_beside[:half])
    attn_corner_y = over_y(attn_across[half:])
    cot_own = jnp.concatenate(canonical(parts[2]), axis=1)
    skip_near = jnp.concatenate([skip_line, skip_beside])
    skip_away = jnp.concatenate([skip_across, skip_corner])
    skip_mat = jnp.where(
        xi == 0,
        jnp.stack([skip_near, skip_away], axis=1),
        jnp.stack([skip_away, skip_near], axis=1),
    ).reshape(D, D)

    def both_images(own):
        own = padded(own)
        return jnp.concatenate([own, core(own)])

    def core_sum(kept, given):
        return (kept + core(given))[:SEQ]

    skip_part = matmul(flat, skip_mat, "rc,cd->rd")
    hidden_in = core_sum(skip_part[:PAD], skip_part[PAD:])
    unit_one, inverse_one = unit_parts(hidden_in)
    normed = both_images((unit_one * norm_gain[0] + norm_bias[0]).astype(bf16))

    attn_corner = jnp.concatenate([attn_corner_x, attn_corner_y])
    normed, cot_own, attn_corner = tie(normed, cot_own, attn_corner)
    cot_pair = padded(cot_own)
    cot_pair = jnp.concatenate([cot_pair, over_x(cot_pair)])
    attn_full = jnp.stack(
        [
            jnp.concatenate([attn_line, attn_beside]),
            jnp.concatenate([attn_across, attn_corner]),
        ]
    )
    attn_a, attn_b, qkv_kept, attended = attn_forward(meta, normed, attn_full)
    attn_b, cot_pair = tie(attn_b, cot_pair)
    middle = hidden_in + core_sum(attn_a, attn_b)
    unit_two, inverse_two = unit_parts(middle)
    mixed_own = padded((unit_two * norm_gain[1] + norm_bias[1]).astype(bf16))
    mixed_pair = jnp.concatenate([mixed_own, over_x(mixed_own)])
    mixed = jnp.concatenate([mixed_pair, core(mixed_pair)])
    cot = jnp.concatenate([cot_pair, core(cot_pair)])

    down_a, down_b, mixed_a, mixed_b, up_near, up_give, down_near, down_give = ffn(
        order, mixed, cot, ffn_full
    )
    mixed_sum = mixed_a + core(mixed_b)
    mixed_far = over_x(mixed_sum[PAD:].astype(bf16))
    ffn_far_down = over_y(down_give)

    mixed_far, ffn_far_down, down_b, up_give = tie(mixed_far, ffn_far_down, down_b, up_give)
    ffn_far_up = over_y(up_give)
    ffn_down, ffn_down_give = halves_z(add_low(down_near, ffn_far_down))
    ffn_down_one = xor_z(ffn_down_give, 1)
    down_sum = down_a + core(down_b)
    down_far = over_x(down_sum[PAD:].astype(bf16))
    back_middle, gain_two, bias_two = norm_back_own(
        unit_two,
        inverse_two,
        (mixed_sum[:PAD] + mixed_far.astype(f32))[:SEQ],
        norm_gain[1],
    )
    grad_middle = cot_own.astype(f32) + back_middle
    middle_low = both_images(grad_middle.astype(bf16))
    normed_a, normed_b, own, other_near, other_x, other_y = attn_backward(
        meta, normed, middle_low, attn_full, qkv_kept, attended
    )

    normed_b, ffn_far_up, ffn_down_one, down_far = tie(
        normed_b, ffn_far_up, ffn_down_one, down_far
    )
    attn_from_x = over_x(other_x)
    attn_from_y = over_y(other_y)
    ffn_up, ffn_up_give = halves_z(add_low(up_near, ffn_far_up))
    ffn_up_one = xor_z(ffn_up_give, 1)
    ffn_down = add_low(ffn_down, ffn_down_one)
    ffn_down_two = xor_z(ffn_down[1], 2)
    block_own = (middle + (down_sum[:PAD] + down_far.astype(f32))[:SEQ]).astype(bf16)
    back_hidden, gain_one, bias_one = norm_back_own(
        unit_one, inverse_one, core_sum(normed_a, normed_b), norm_gain[0]
    )
    hidden_low = both_images((grad_middle + back_hidden).astype(bf16))

    grad_skip = matmul(flat, hidden_low, "rc,rd->cd").astype(bf16)
    grad_skip = grad_skip.reshape(narrow_count, 2, feat // 2, D)
    skip_own, skip_other = pick(grad_skip, xi, 1), pick(grad_skip, 1 - xi, 1)
    skip_from_x = over_x(skip_other[ZS : ZS + half])
    skip_from_y = over_y(skip_other[ZS + half :])
    token_grad = matmul(hidden_low, skip_mat, "rd,cd->rc").astype(bf16)
    block_pieces = jnp.stack(jnp.split(block_own, narrow_count, axis=1))

    def back_piece(slot):
        columns_of = slice(slot * feat, (slot + 1) * feat)
        return jnp.concatenate(
            [
                token_grad[:SEQ, columns_of],
                token_grad[PAD : PAD + SEQ, columns_of],
                pick(block_pieces, order[slot], 0),
            ],
            axis=1,
        )

    back_near = [back_piece(slot) for slot in range(ZS)]
    back_give = jnp.stack([back_piece(slot) for slot in range(ZS, narrow_count)])

    attn_from_x, attn_from_y, back_give, ffn_up_one, ffn_down_two = tie(
        attn_from_x, attn_from_y, back_give, ffn_up_one, ffn_down_two
    )
    back_far = over_y(back_give)
    attn_across = over_x(
        jnp.concatenate([other_near[:half], add_low(other_near[half:], attn_from_y)])
    )
    attn_beside = over_y(
        jnp.concatenate([add_low(own[ZS : ZS + half], attn_from_x), own[ZS + half :]])
    )
    ffn_up = add_low(ffn_up, ffn_up_one)
    ffn_up_two = xor_z(ffn_up[1], 2)

    skip_from_x, skip_from_y, back_far = tie(skip_from_x, skip_from_y, back_far)
    skip_near_sum = add_low(skip_own[ZS : ZS + half], skip_from_x)
    skip_far_sum = add_low(skip_other[half:ZS], skip_from_y)
    back_pieces = [
        jnp.concatenate([back_near[place], back_far[place]], axis=1) for place in range(ZS)
    ]
    back_blocks = z_line(back_pieces)

    attn_beside, attn_across, ffn_up_two = tie(attn_beside, attn_across, ffn_up_two)
    attn_total, attn_give = halves_z(
        (own[:ZS].astype(f32) + attn_beside.astype(f32) + attn_across.astype(f32)).astype(bf16)
    )
    attn_one = xor_z(attn_give, 1)
    skip_across = over_x(jnp.concatenate([skip_other[:half], skip_far_sum]))
    skip_beside = over_y(jnp.concatenate([skip_near_sum, skip_own[ZS + half :]]))
    ffn_own = jnp.stack([add_low(ffn_up[0], ffn_up_two), add_low(ffn_down[0], ffn_down_two)])
    ffn_x = over_x(ffn_own)

    attn_one, ffn_x = tie(attn_one, ffn_x)
    attn_total = add_low(attn_total, attn_one)
    attn_two = xor_z(attn_total[1], 2)
    ffn_pair = jnp.stack([ffn_own, ffn_x])
    ffn_core = core(ffn_pair)

    ffn_all = in_order(ffn_pair, ffn_core).astype(f32)
    grad_up_rows = ffn_all[:, 0].reshape(hidden, D)
    grad_down = ffn_all[:, 1].reshape(hidden, D)
    new_col_up, up_sums = statistics(grad_up_rows, col_up)
    new_row_down, down_sums = statistics(grad_down, row_down)
    ffn_totals = all_narrow(jnp.stack(up_sums + down_sums))

    skip_beside, skip_across, ffn_totals, *back_blocks = tie(
        skip_beside, skip_across, ffn_totals, *back_blocks
    )
    new_row_up, ratio_up, step_up = step_of(
        grad_up_rows, new_col_up, ffn_totals[:3], row_up, hidden * narrow_count, True
    )
    new_col_down, ratio_down, step_down = step_of(
        grad_down, new_row_down, ffn_totals[3:], col_down, hidden * narrow_count, False
    )
    new_up = up_weight.astype(f32) + step_up.T
    new_down = down_weight.astype(f32) + step_down
    grad_up_out = columns(grad_up_rows).T
    grad_down_out = columns(grad_down)
    skip_total, skip_give = halves_z(
        (skip_own[:ZS].astype(f32) + skip_beside.astype(f32) + skip_across.astype(f32)).astype(
            bf16
        )
    )
    skip_one = xor_z(skip_give, 1)
    back = [block[:, j * 3 * feat : (j + 1) * 3 * feat] for j in range(2) for block in back_blocks]
    back = jnp.concatenate(canonical(back), axis=0)
    grad_mine = back[:, :feat]
    grad_given = core(back[:, feat : 2 * feat])
    block_out = back[:, 2 * feat :]

    attn_two, skip_one, grad_given, block_out, new_up, new_down, grad_up_out, grad_down_out = tie(
        attn_two, skip_one, grad_given, block_out, new_up, new_down, grad_up_out, grad_down_out
    )
    attn_own = add_low(attn_total[0], attn_two)
    skip_total = add_low(skip_total, skip_one)
    skip_two = xor_z(skip_total[1], 2)
    grad_stream = jnp.where(is_first, grad_mine, grad_given).astype(f32)
    grad_skip_in = jnp.where(is_first, grad_given, grad_mine).astype(f32)

    grad_stream, grad_skip_in, skip_two = tie(grad_stream, grad_skip_in, skip_two)
    last_own = jnp.concatenate([attn_own, add_low(skip_total[0], skip_two)])
    last_pair = jnp.stack([last_own, over_x(last_own)])
    last_all = in_order(last_pair, core(last_pair)).astype(f32)
    attn_rows_all = 2 * half_head
    attn_all = last_all[:, :attn_rows_all].reshape(2, 4, half_head, D)
    grad_skip_rows = last_all[:, attn_rows_all:].reshape(2 * feat, D)
    grad_qkv_rows = attn_all[:, :3].transpose(1, 0, 2, 3).reshape(3 * feat, D)
    grad_out = attn_all[:, 3].reshape(feat, D)

    norm_sums = jnp.stack([gain_one, gain_two, bias_one, bias_two])
    norm_sums = norm_sums + core(norm_sums)
    norm_sums = norm_sums + over_x(norm_sums)
    new_row_skip, skip_sums = statistics(grad_skip_rows, row_skip.reshape(-1))
    new_col_qkv, qkv_sums = statistics(grad_qkv_rows, col_qkv.reshape(-1))
    new_row_out, out_sums = statistics(grad_out, row_out)
    totals = all_narrow(jnp.concatenate([jnp.stack(skip_sums + qkv_sums + out_sums), norm_sums]))
    gain_total = totals[9:11]
    bias_total = totals[11:13]
    new_col_skip, ratio_skip, step_skip = step_of(
        grad_skip_rows, new_row_skip, totals[:3], col_skip, 2 * D, False
    )
    new_row_qkv, ratio_qkv, step_qkv = step_of(
        grad_qkv_rows, new_col_qkv, totals[3:6], row_qkv, 3 * D, True
    )
    new_col_out, ratio_out, step_out = step_of(
        grad_out, new_row_out, totals[6:9], col_out, D, False
    )
    clip_ratio = jnp.stack([ratio_skip, ratio_qkv, ratio_out, ratio_up, ratio_down])
    new_skip = skip_weight.astype(f32) + step_skip.reshape(2, feat, D)
    new_qkv = qkv_weight.astype(f32) + step_qkv.reshape(3, feat, D).transpose(2, 0, 1)
    new_second_gain, gain_step = plain_update(gain_total, second_gain)
    new_second_bias, bias_step = plain_update(bias_total, second_bias)
    return (
        block_out,
        grad_stream,
        grad_skip_in,
        columns(grad_skip_rows).reshape(2, feat, -1),
        columns(grad_qkv_rows).reshape(3, feat, -1).transpose(2, 0, 1),
        columns(grad_out),
        grad_up_out,
        grad_down_out,
        gain_total,
        bias_total,
        new_row_skip.reshape(2, feat),
        new_col_skip,
        new_row_qkv,
        new_col_qkv.reshape(3, feat),
        new_row_out,
        new_col_out,
        new_row_up,
        new_col_up,
        new_row_down,
        new_col_down,
        new_second_gain,
        new_second_bias[0],
        new_second_bias[1],
        new_skip,
        new_qkv,
        step_out,
        new_up,
        new_down,
        gain_step,
        bias_step,
        clip_ratio,
    )


def solution(mesh):
    wide, narrow = mesh.shape["wide"], mesh.shape["narrow"]
    body = chips if (wide == 4 and narrow == 8) else local
    in_specs = (
        P("wide", "narrow"),
        P("wide", "narrow"),
        P("wide", "narrow"),
        P(None, "narrow", None),
        P(None, None, "narrow"),
        P("narrow", None),
        P(None, "narrow"),
        P("narrow", None),
        P(),
        P(),
        P(None, "narrow"),
        P(),
        P(),
        P(None, "narrow"),
        P("narrow"),
        P(),
        P(),
        P("narrow"),
        P("narrow"),
        P(),
        P(),
        P(),
    )
    out_specs = (
        P("wide", "narrow"),
        P("wide", "narrow"),
        P("wide", "narrow"),
        P(None, "narrow", "wide"),
        P("wide", None, "narrow"),
        P("narrow", "wide"),
        P("wide", "narrow"),
        P("narrow", "wide"),
        P(),
        P(),
        P(None, "narrow"),
        P(),
        P(),
        P(None, "narrow"),
        P("narrow"),
        P(),
        P(),
        P("narrow"),
        P("narrow"),
        P(),
        P(),
        P(),
        P(),
        P(None, "narrow", None),
        P(None, None, "narrow"),
        P("narrow", None),
        P(None, "narrow"),
        P("narrow", None),
        P(),
        P(),
        P(),
    )
    return jax.shard_map(body, mesh=mesh, in_specs=in_specs, out_specs=out_specs, check_vma=False)
```

```python
import math

import jax
import jax.numpy as jnp
from jax import lax
from jax.experimental import pallas as pl
from jax.experimental.pallas import tpu as pltpu
from jax.sharding import PartitionSpec as P

D = 1152
FF = 4608
SEQ = 258
HEAD = 72


NORM_EPS = 1e-05
EPS_SQUARE = 1e-30
DECAY = 0.5
STEP_RATE = 0.05
CLIP_LEVEL = 0.25


def layer_norm(values, gain, shift):
    average = jnp.mean(values, axis=-1, keepdims=True)
    centered = values - average
    variance = jnp.mean(centered * centered, axis=-1, keepdims=True)
    return centered * lax.rsqrt(variance + NORM_EPS) * gain + shift


def norm_back(values, grad, gain, own_rows):
    average = jnp.mean(values, axis=-1, keepdims=True)
    centered = values - average
    variance = jnp.mean(centered * centered, axis=-1, keepdims=True)
    inverse = lax.rsqrt(variance + NORM_EPS)
    unit = centered * inverse
    scaled = grad * gain
    inner = (
        scaled
        - jnp.mean(scaled, axis=-1, keepdims=True)
        - unit * jnp.mean(scaled * unit, axis=-1, keepdims=True)
    )
    weighted = grad * own_rows
    return (inner * inverse, jnp.sum(weighted * unit, axis=0), jnp.sum(weighted, axis=0))


def gelu_exact(inputs):
    return jax.nn.gelu(inputs, approximate=False)


def matmul(left, right, form):
    return jnp.einsum(form, left, right, preferred_element_type=jnp.float32)


def plain_update(grad, second_old):
    second_new = DECAY * second_old + (1.0 - DECAY) * (grad * grad + EPS_SQUARE)
    update = grad * lax.rsqrt(second_new)
    spread = jnp.sqrt(jnp.mean(update * update))
    update = update / jnp.maximum(1.0, spread / CLIP_LEVEL)
    return (second_new, -(STEP_RATE * update))


def wide_slice(array, dim_index, count, wide_index):
    piece_size = array.shape[dim_index] // count
    return lax.dynamic_slice_in_dim(array, wide_index * piece_size, piece_size, dim_index)


def local(
    stream,
    skip_in,
    cotangent,
    skip_weight,
    qkv_weight,
    out_weight,
    up_weight,
    down_weight,
    norm_gain,
    norm_bias,
    row_skip,
    col_skip,
    row_qkv,
    col_qkv,
    row_out,
    col_out,
    row_up,
    col_up,
    row_down,
    col_down,
    second_gain,
    second_bias,
):
    rows_local, feat_local = stream.shape
    images = rows_local // SEQ
    heads_local = feat_local // HEAD
    scale_factor = 1.0 / math.sqrt(HEAD)
    split_shape = (images, SEQ, heads_local, HEAD)
    narrow_count = lax.axis_size("narrow")
    narrow_index = lax.axis_index("narrow")
    share_rows = -(-rows_local // narrow_count)
    row_start = narrow_index * share_rows
    row_ids = lax.broadcasted_iota(jnp.int32, (rows_local, 1), 0)
    own_mask = ((row_ids >= row_start) & (row_ids < row_start + share_rows)).astype(jnp.float32)

    def full_sum(values):
        return lax.psum(values, "narrow")

    partial_in = matmul(stream, skip_weight[0], "rc,cd->rd") + matmul(
        skip_in, skip_weight[1], "rc,cd->rd"
    )
    hidden_in = full_sum(partial_in)
    normed = layer_norm(hidden_in, norm_gain[0], norm_bias[0]).astype(jnp.bfloat16)
    projected = matmul(normed, qkv_weight, "rd,dtc->rtc").astype(jnp.bfloat16)
    queries = projected[:, 0].reshape(split_shape)
    key_vectors = projected[:, 1].reshape(split_shape)
    value_vectors = projected[:, 2].reshape(split_shape)
    scores = matmul(queries, key_vectors, "bqhe,bkhe->bhqk") * scale_factor
    row_max = jnp.max(scores, axis=-1, keepdims=True)
    exponent = jnp.exp(scores - row_max)
    row_total = jnp.sum(exponent, axis=-1, keepdims=True)
    log_total = row_max + jnp.log(row_total)
    probs_low = (exponent / row_total).astype(jnp.bfloat16)
    attended = (
        matmul(probs_low, value_vectors, "bhqk,bkhe->bqhe")
        .reshape(rows_local, feat_local)
        .astype(jnp.bfloat16)
    )
    attn_part = matmul(attended, out_weight, "rc,cd->rd")
    middle = hidden_in + full_sum(attn_part)
    mixed_in = layer_norm(middle, norm_gain[1], norm_bias[1]).astype(jnp.bfloat16)
    middle_own = lax.dynamic_slice_in_dim(middle, narrow_index * feat_local, feat_local, 1)
    up_input = matmul(mixed_in, up_weight, "rd,df->rf")
    activation = gelu_exact(up_input).astype(jnp.bfloat16)
    down_part = matmul(activation, down_weight, "rf,fd->rd")
    block_out = (
        middle_own + lax.psum_scatter(down_part, "narrow", scatter_dimension=1, tiled=True)
    ).astype(jnp.bfloat16)
    grad_full = lax.all_gather(cotangent, "narrow", axis=1, tiled=True)
    grad_down = matmul(activation, grad_full, "rf,rd->fd")
    grad_act = matmul(grad_full, down_weight, "rd,fd->rf")
    gelu_value, gelu_back = jax.vjp(gelu_exact, up_input)
    grad_up_in = gelu_back(grad_act)[0].astype(jnp.bfloat16)
    grad_up = matmul(mixed_in, grad_up_in, "rd,rf->df")
    mixed_part = matmul(grad_up_in, up_weight, "rf,df->rd")
    grad_mixed = full_sum(mixed_part)
    back_middle, back_gain_two, back_bias_two = norm_back(
        middle, grad_mixed, norm_gain[1], own_mask
    )
    grad_middle = grad_full.astype(jnp.float32) + back_middle
    middle_low = grad_middle.astype(jnp.bfloat16)
    grad_out = matmul(attended, middle_low, "rc,rd->cd")
    grad_attended = (
        matmul(middle_low, out_weight, "rd,cd->rc").astype(jnp.bfloat16).reshape(split_shape)
    )
    scores_again = matmul(queries, key_vectors, "bqhe,bkhe->bhqk") * scale_factor
    probs = jnp.exp(scores_again - log_total)
    probs_again = probs.astype(jnp.bfloat16)
    grad_values = matmul(probs_again, grad_attended, "bhqk,bqhe->bkhe")
    grad_probs = matmul(grad_attended, value_vectors, "bqhe,bkhe->bhqk")
    inner_sum = jnp.sum(probs * grad_probs, axis=-1, keepdims=True)
    grad_scores = (probs * (grad_probs - inner_sum) * scale_factor).astype(jnp.bfloat16)
    grad_queries = matmul(grad_scores, key_vectors, "bhqk,bkhe->bqhe")
    grad_keys = matmul(grad_scores, queries, "bhqk,bqhe->bkhe")
    grad_projected = jnp.stack(
        [
            grad_queries.reshape(rows_local, feat_local),
            grad_keys.reshape(rows_local, feat_local),
            grad_values.reshape(rows_local, feat_local),
        ],
        axis=1,
    ).astype(jnp.bfloat16)
    grad_qkv = matmul(normed, grad_projected, "rd,rtc->dtc")
    normed_part = matmul(grad_projected, qkv_weight, "rtc,dtc->rd")
    grad_normed = full_sum(normed_part)
    back_hidden, back_gain_one, back_bias_one = norm_back(
        hidden_in, grad_normed, norm_gain[0], own_mask
    )
    hidden_low = (grad_middle + back_hidden).astype(jnp.bfloat16)
    grad_skip = jnp.stack(
        [matmul(stream, hidden_low, "rc,rd->cd"), matmul(skip_in, hidden_low, "rc,rd->cd")]
    )
    grad_stream = matmul(hidden_low, skip_weight[0], "rd,cd->rc")
    grad_skip_in = matmul(hidden_low, skip_weight[1], "rd,cd->rc")
    gain_grads = jnp.stack([back_gain_one, back_gain_two])
    bias_grads = jnp.stack([back_bias_one, back_bias_two])
    wide_count = lax.axis_size("wide")
    wide_index = lax.axis_index("wide")
    wide_dims = (2, 0, 1, 0, 1)
    wide_axes = ((0, 1), (1, 2), (0,), (1,), (0,))
    narrow_axes = ((2,), (0,), (1,), (0,), (1,))
    wide_counts = (2 * D, 3 * D, D, FF, FF)
    row_along_wide = (False, True, False, True, False)
    entry_counts = (2 * D * D, 3 * D * D, D * D, D * FF, FF * D)
    old_slots = (0, 0, 1, 0, 2)
    weights = (skip_weight, qkv_weight, out_weight, up_weight, down_weight)
    old_wide = (col_skip, row_qkv, col_out, row_up, col_down)
    old_narrow = (row_skip, col_qkv, row_out, col_up, row_down)
    summed = lax.psum(
        (grad_skip, grad_qkv, grad_out, grad_up, grad_down, gain_grads, bias_grads), "wide"
    )
    pieces = summed[:5]
    gain_section = summed[5]
    bias_section = summed[6]
    squares = [piece * piece + EPS_SQUARE for piece in pieces]
    wide_parts = [jnp.sum(squares[number], axis=wide_axes[number]) for number in range(5)]
    narrow_parts = [jnp.sum(squares[number], axis=narrow_axes[number]) for number in range(5)]
    old_sums = jnp.stack([jnp.sum(row_skip), jnp.sum(row_out), jnp.sum(row_down)])
    stat_total = lax.psum(
        (
            wide_parts[0],
            wide_parts[1],
            wide_parts[2],
            wide_parts[3],
            wide_parts[4],
            old_sums,
            gain_section,
            bias_section,
        ),
        "narrow",
    )
    old_row_means = (stat_total[5][0] / (2 * D), stat_total[5][1] / D, stat_total[5][2] / FF)
    wide_stats = stat_total[:5]
    gain_total = stat_total[6]
    bias_total = stat_total[7]
    new_wide = []
    new_narrow = []
    updates = []
    for number in range(5):
        wide_mean = wide_stats[number] / wide_counts[number]
        wide_new = DECAY * old_wide[number] + (1.0 - DECAY) * wide_mean
        narrow_new = DECAY * old_narrow[number] + (1.0 - DECAY) * narrow_parts[number] / D
        if row_along_wide[number]:
            row_mean = jnp.mean(wide_new)
        else:
            row_mean = DECAY * old_row_means[old_slots[number]] + (1.0 - DECAY) * jnp.mean(
                wide_mean
            )
        dim_index = wide_dims[number]
        piece_size = pieces[number].shape[dim_index]
        broadcast_shape = [1] * pieces[number].ndim
        broadcast_shape[dim_index] = piece_size
        second = (
            jnp.expand_dims(narrow_new, dim_index) * wide_new.reshape(broadcast_shape) / row_mean
        )
        updates.append(pieces[number] * lax.rsqrt(second))
        new_wide.append(wide_new)
        new_narrow.append(narrow_new)
    update_squares = jnp.stack([jnp.sum(update * update) for update in updates])
    square_totals = lax.psum(update_squares, "narrow")
    counts_array = jnp.array(entry_counts, jnp.float32)
    clip_ratio = jnp.sqrt(square_totals / counts_array) / CLIP_LEVEL
    new_pieces = []
    for number in range(5):
        spread = jnp.sqrt(square_totals[number] / entry_counts[number])
        step_piece = -(STEP_RATE * (updates[number] / jnp.maximum(1.0, spread / CLIP_LEVEL)))
        if number == 2:
            new_pieces.append(step_piece)
        else:
            weight_piece = weights[number]
            new_pieces.append(weight_piece.astype(jnp.float32) + step_piece)
    grad_outs = [
        wide_slice(pieces[number], wide_dims[number], wide_count, wide_index) for number in range(5)
    ]
    new_second_gain, gain_step = plain_update(gain_total, second_gain)
    new_second_bias, bias_step = plain_update(bias_total, second_bias)
    return (
        block_out,
        grad_stream,
        grad_skip_in,
        grad_outs[0],
        grad_outs[1],
        grad_outs[2],
        grad_outs[3],
        grad_outs[4],
        gain_total,
        bias_total,
        new_narrow[0],
        new_wide[0],
        new_wide[1],
        new_narrow[1],
        new_narrow[2],
        new_wide[2],
        new_wide[3],
        new_narrow[3],
        new_narrow[4],
        new_wide[4],
        new_second_gain,
        new_second_bias[0],
        new_second_bias[1],
        new_pieces[0],
        new_pieces[1],
        new_pieces[2],
        new_pieces[3],
        new_pieces[4],
        gain_step,
        bias_step,
        clip_ratio,
    )


def unit_parts(values):
    average = jnp.mean(values, axis=-1, keepdims=True)
    centered = values - average
    variance = jnp.mean(centered * centered, axis=-1, keepdims=True)
    inverse = lax.rsqrt(variance + NORM_EPS)
    return centered * inverse, inverse


def norm_back_own(unit, inverse, grad, gain):
    scaled = grad * gain
    inner = (
        scaled
        - jnp.mean(scaled, axis=-1, keepdims=True)
        - unit * jnp.mean(scaled * unit, axis=-1, keepdims=True)
    )
    rows = tuple(range(grad.ndim - 1))
    return inner * inverse, jnp.sum(grad * unit, axis=rows), jnp.sum(grad, axis=rows)


def pick(array, index, axis):
    return lax.dynamic_index_in_dim(array, index, axis, keepdims=False)


PAD = 272


def dot_nt(left, right):
    return lax.dot_general(left, right, (((1,), (1,)), ((), ())), preferred_element_type=jnp.float32)


def dot_nn(left, right):
    return lax.dot_general(left, right, (((1,), (0,)), ((), ())), preferred_element_type=jnp.float32)


def dot_tn(left, right):
    return lax.dot_general(left, right, (((0,), (0,)), ((), ())), preferred_element_type=jnp.float32)


def accumulate(step, refs, value):
    size = refs[0].shape[0]

    @pl.when(step == 0)
    def _():
        for number, ref in enumerate(refs):
            ref[...] = value[number * size : (number + 1) * size]

    @pl.when(step > 0)
    def _():
        for number, ref in enumerate(refs):
            ref[...] += value[number * size : (number + 1) * size]


def ffn_kernel(order_ref, mixed_ref, cot_ref, *refs):
    blocks = 4
    weights, (down_a, down_b, mixed_a, mixed_b), grads = refs[:blocks], refs[blocks : blocks + 4], refs[blocks + 4 :]
    step = pl.program_id(0)
    mixed = mixed_ref[...]
    cot = cot_ref[...]
    up = jnp.concatenate([ref[0, 0] for ref in weights], axis=0)
    down = jnp.concatenate([ref[0, 1] for ref in weights], axis=0)
    up_input = dot_nt(mixed, up)
    gate = 0.5 * (1.0 + lax.erf(up_input * (1.0 / math.sqrt(2.0))))
    activation = (up_input * gate).astype(jnp.bfloat16)
    slope = gate + up_input * (jnp.exp(-0.5 * up_input * up_input) * (1.0 / math.sqrt(2.0 * math.pi)))
    grad_up_in = (dot_nt(cot, down) * slope).astype(jnp.bfloat16)
    grad_up = dot_tn(grad_up_in, mixed).astype(jnp.bfloat16)
    grad_down = dot_tn(activation, cot).astype(jnp.bfloat16)
    for j in range(2):

        @pl.when(step == j)
        def _():
            grads[j][...] = grad_up.reshape(grads[j].shape)

    down_rows = grad_down.reshape((2,) + grads[2].shape[1:])
    grads[2][0] = down_rows[0]
    grads[3][0] = down_rows[1]

    accumulate(step, (mixed_a, mixed_b), dot_nn(grad_up_in, up))
    accumulate(step, (down_a, down_b), dot_nn(activation, down))


def ffn(order, mixed, cot, weights):
    count, _, rows, _ = weights.shape
    tokens = mixed.shape[0]
    blocks = 4
    whole = pl.BlockSpec((tokens, D), lambda t, m: (0, 0))
    half = pl.BlockSpec((tokens // 2, D), lambda t, m: (0, 0))

    def weight_spec(slot):
        return pl.BlockSpec((1, 2, rows, D), lambda t, m: (m[blocks * t + slot], 0, 0, 0))

    grad_block = pl.BlockSpec((blocks, rows, D), lambda t, m: (0, 0, 0))
    part = jax.ShapeDtypeStruct((tokens // 2, D), jnp.float32)
    grad = jax.ShapeDtypeStruct((blocks, rows, D), jnp.bfloat16)
    turn_block = pl.BlockSpec((1, blocks // 2, rows, D), lambda t, m: (t, 0, 0, 0))
    turn = jax.ShapeDtypeStruct((2, blocks // 2, rows, D), jnp.bfloat16)
    return pl.pallas_call(
        ffn_kernel,
        out_shape=[part] * 4 + [grad] * 2 + [turn] * 2,
        grid_spec=pltpu.PrefetchScalarGridSpec(
            num_scalar_prefetch=1,
            grid=(count // blocks,),
            in_specs=[whole, whole] + [weight_spec(slot) for slot in range(blocks)],
            out_specs=[half] * 4 + [grad_block] * 2 + [turn_block] * 2,
        ),
        compiler_params=pltpu.CompilerParams(
            dimension_semantics=("arbitrary",), vmem_limit_bytes=60 * 1024 * 1024
        ),
        cost_estimate=pl.CostEstimate(
            flops=12 * tokens * D * count * rows, transcendentals=0, bytes_accessed=32 * 1024 * 1024
        ),
        name="ffn",
    )(order, mixed, cot, *([weights] * blocks))


def soft(q, k):
    scores = dot_nt(q, k) * (1.0 / math.sqrt(HEAD))
    column = lax.broadcasted_iota(jnp.int32, scores.shape, 1)
    scores = jnp.where(column < SEQ, scores, -1e30)
    exponent = jnp.exp(scores - jnp.max(scores, axis=-1, keepdims=True))
    return exponent / jnp.sum(exponent, axis=-1, keepdims=True)


GROUP = 4


def head_weights(qk_ref, vo_ref):
    qk = [qk_ref[0, head] for head in range(GROUP)]
    v = [vo_ref[0, head, :HEAD] for head in range(GROUP)]
    out = [vo_ref[0, head, HEAD:] for head in range(GROUP)]
    return jnp.concatenate(qk + v, axis=0), jnp.concatenate(out, axis=0)


def head_columns(head):
    first = 2 * HEAD * head
    value = 2 * HEAD * GROUP + HEAD * head
    return (
        slice(first, first + HEAD),
        slice(first + HEAD, first + 2 * HEAD),
        slice(value, value + HEAD),
    )


def attn_forward_kernel(meta_ref, normed_ref, qk_ref, vo_ref, part_a, part_b, qkv_ref, attended_ref):
    step = pl.program_id(0)
    weights, out_weight = head_weights(qk_ref, vo_ref)
    qkv_ref[0] = dot_nt(normed_ref[...], weights).astype(jnp.bfloat16)
    for head in range(GROUP):
        q_at, k_at, v_at = head_columns(head)
        for image in range(2):
            rows = slice(image * PAD, (image + 1) * PAD)
            probs = soft(qkv_ref[0, rows, q_at], qkv_ref[0, rows, k_at]).astype(jnp.bfloat16)
            attended_ref[0, rows, HEAD * head : HEAD * (head + 1)] = dot_nn(
                probs, qkv_ref[0, rows, v_at]
            ).astype(jnp.bfloat16)
    accumulate(step, (part_a, part_b), dot_nn(attended_ref[0], out_weight))


def attn_specs(rows, tokens):
    whole = pl.BlockSpec((tokens, D), lambda s, m: (0, 0))
    half = pl.BlockSpec((tokens // 2, D), lambda s, m: (0, 0))
    qk = pl.BlockSpec((1, GROUP, rows, D), lambda s, m: (m[0], s, 0, 0))
    vo = pl.BlockSpec((1, GROUP, rows, D), lambda s, m: (1 - m[0], s, 0, 0))
    qkv = pl.BlockSpec((1, tokens, 3 * HEAD * GROUP), lambda s, m: (s, 0, 0))
    att = pl.BlockSpec((1, tokens, HEAD * GROUP), lambda s, m: (s, 0, 0))
    return whole, half, qk, vo, qkv, att


def attn_forward(meta, normed, weights):
    heads, rows = weights.shape[1:3]
    tokens = normed.shape[0]
    whole, half, qk, vo, qkv, att = attn_specs(rows, tokens)
    return pl.pallas_call(
        attn_forward_kernel,
        out_shape=[
            jax.ShapeDtypeStruct((tokens // 2, D), jnp.float32),
            jax.ShapeDtypeStruct((tokens // 2, D), jnp.float32),
            jax.ShapeDtypeStruct((heads // GROUP, tokens, 3 * HEAD * GROUP), jnp.bfloat16),
            jax.ShapeDtypeStruct((heads // GROUP, tokens, HEAD * GROUP), jnp.bfloat16),
        ],
        grid_spec=pltpu.PrefetchScalarGridSpec(
            num_scalar_prefetch=1,
            grid=(heads // GROUP,),
            in_specs=[whole, qk, vo],
            out_specs=[half, half, qkv, att],
        ),
        compiler_params=pltpu.CompilerParams(
            dimension_semantics=("arbitrary",), vmem_limit_bytes=48 * 1024 * 1024
        ),
        cost_estimate=pl.CostEstimate(flops=0, transcendentals=0, bytes_accessed=1024 * 1024),
        name="attn_forward",
    )(meta, normed, weights, weights)


def attn_backward_kernel(
    meta_ref,
    normed_ref,
    low_ref,
    qk_ref,
    vo_ref,
    qkv_ref,
    attended_ref,
    part_a,
    part_b,
    own_ref,
    near_ref,
    far_x_ref,
    far_y_ref,
    grads_s,
    out_s,
):
    step = pl.program_id(0)
    normed = normed_ref[...]
    low = low_ref[...]
    weights, out_weight = head_weights(qk_ref, vo_ref)
    out_s[...] = dot_nt(low, out_weight).astype(jnp.bfloat16)
    for head in range(GROUP):
        q_at, k_at, v_at = head_columns(head)
        for image in range(2):
            rows = slice(image * PAD, (image + 1) * PAD)
            q = qkv_ref[0, rows, q_at]
            k = qkv_ref[0, rows, k_at]
            v = qkv_ref[0, rows, v_at]
            grad = out_s[rows, HEAD * head : HEAD * (head + 1)]
            probs = soft(q, k)
            grads_s[rows, v_at] = dot_tn(probs.astype(jnp.bfloat16), grad).astype(jnp.bfloat16)
            grad_probs = dot_nt(grad, v)
            inner = jnp.sum(probs * grad_probs, axis=-1, keepdims=True)
            grad_scores = (probs * (grad_probs - inner) * (1.0 / math.sqrt(HEAD))).astype(
                jnp.bfloat16
            )
            grads_s[rows, q_at] = dot_nn(grad_scores, k).astype(jnp.bfloat16)
            grads_s[rows, k_at] = dot_tn(grad_scores, q).astype(jnp.bfloat16)
    projected = grads_s[...]
    accumulate(step, (part_a, part_b), dot_nn(projected, weights))
    mats = dot_tn(projected, normed)
    outs = dot_tn(attended_ref[0], low)
    first = meta_ref[0] == 0
    for head in range(GROUP):
        q_at, k_at, v_at = head_columns(head)
        query_key = mats[q_at.start : k_at.stop]
        value_out = jnp.concatenate([mats[v_at], outs[HEAD * head : HEAD * (head + 1)]], axis=0)
        own_ref[head] = jnp.where(first, query_key, value_out).astype(jnp.bfloat16)
        other = jnp.where(first, value_out, query_key).astype(jnp.bfloat16)

        @pl.when(step == 0)
        def _():
            near_ref[head] = other

        @pl.when(step == 1)
        def _():
            if head < 2:
                far_x_ref[head] = other
            else:
                far_y_ref[head - 2] = other


def attn_backward(meta, normed, low, weights, qkv_kept, attended):
    heads, rows = weights.shape[1:3]
    tokens = normed.shape[0]
    whole, half, qk, vo, qkv, att = attn_specs(rows, tokens)

    def fixed(size):
        return pl.BlockSpec((size, rows, D), lambda s, m: (0, 0, 0))

    return pl.pallas_call(
        attn_backward_kernel,
        out_shape=[
            jax.ShapeDtypeStruct((tokens // 2, D), jnp.float32),
            jax.ShapeDtypeStruct((tokens // 2, D), jnp.float32),
            jax.ShapeDtypeStruct((heads, rows, D), jnp.bfloat16),
            jax.ShapeDtypeStruct((4, rows, D), jnp.bfloat16),
            jax.ShapeDtypeStruct((2, rows, D), jnp.bfloat16),
            jax.ShapeDtypeStruct((2, rows, D), jnp.bfloat16),
        ],
        grid_spec=pltpu.PrefetchScalarGridSpec(
            num_scalar_prefetch=1,
            grid=(heads // GROUP,),
            in_specs=[whole, whole, qk, vo, qkv, att],
            out_specs=[
                half,
                half,
                pl.BlockSpec((GROUP, rows, D), lambda s, m: (s, 0, 0)),
                fixed(4),
                fixed(2),
                fixed(2),
            ],
            scratch_shapes=[
                pltpu.VMEM((tokens, 3 * HEAD * GROUP), jnp.bfloat16),
                pltpu.VMEM((tokens, HEAD * GROUP), jnp.bfloat16),
            ],
        ),
        compiler_params=pltpu.CompilerParams(
            dimension_semantics=("arbitrary",), vmem_limit_bytes=56 * 1024 * 1024
        ),
        cost_estimate=pl.CostEstimate(
            flops=4 * tokens * D * heads * 2 * rows,
            transcendentals=0,
            bytes_accessed=24 * 1024 * 1024,
        ),
        name="attn_backward",
    )(meta, normed, low, weights, weights, qkv_kept, attended)


def by_narrow(blocks, flag_refs):
    table = [None] * 8
    for place, distance in enumerate((0, 2, 1, 3)):
        for j in range(2):
            table[distance * 2 + j] = blocks[j * 4 + place]
    for number, flag in enumerate(flag_refs):
        bit = 1 << number
        table = [jnp.where(flag == 0, table[i], table[i ^ bit]) for i in range(8)]
    return table


def by_slot(blocks, flag_refs):
    table = list(blocks)
    for number, flag in enumerate(flag_refs):
        bit = 1 << number
        table = [jnp.where(flag == 0, table[i], table[i ^ bit]) for i in range(8)]
    return [table[distance * 2 + j] for j in range(2) for distance in (0, 2, 1, 3)]


def take_kernel(flags_ref, *refs):
    blocks, (mine_ref, give_ref, cot_ref) = refs[:4], refs[4:]
    width = blocks[0].shape[1] // 6
    rows = blocks[0].shape[0]
    first = flags_ref[3] == 0
    for ref in (mine_ref, give_ref, cot_ref):
        ref[rows - 2 :] = jnp.zeros((ref.shape[0] - rows + 2, ref.shape[1]), ref.dtype)
    cots = []
    for j in range(2):
        for place in range(4):
            slot = j * 4 + place
            columns = slice(slot * width, (slot + 1) * width)
            one, two, three = [
                blocks[place][:, (3 * j + kind) * width : (3 * j + kind + 1) * width]
                for kind in range(3)
            ]
            mine_ref[:rows, columns] = jnp.where(first, one, two)
            give_ref[:rows, columns] = jnp.where(first, two, one)
            cots.append(three)
    for number, piece in enumerate(by_narrow(cots, [flags_ref[i] for i in range(3)])):
        cot_ref[:rows, number * width : (number + 1) * width] = piece


def take_tokens(flags, blocks):
    out = jax.ShapeDtypeStruct((PAD, D), jnp.bfloat16)
    full = pl.BlockSpec(memory_space=pltpu.VMEM)
    return pl.pallas_call(
        take_kernel,
        out_shape=[out] * 3,
        in_specs=[pl.BlockSpec(memory_space=pltpu.SMEM)] + [full] * 4,
        out_specs=[full] * 3,
        compiler_params=pltpu.CompilerParams(vmem_limit_bytes=24 * 1024 * 1024),
        cost_estimate=pl.CostEstimate(flops=0, transcendentals=0, bytes_accessed=4 * 1024 * 1024),
        name="take_tokens",
    )(flags, *blocks)


def give_kernel(flags_ref, kept_ref, other_ref, block_ref, near_ref, far_ref):
    rows = near_ref.shape[1]
    width = near_ref.shape[2] // 3
    first = flags_ref[3] == 0
    parts = [block_ref[:rows, n * width : (n + 1) * width] for n in range(8)]
    parts = by_slot(parts, [flags_ref[i] for i in range(3)])
    for slot in range(8):
        columns = slice(slot * width, (slot + 1) * width)
        kept = kept_ref[:rows, columns]
        other = other_ref[:rows, columns]
        target = (near_ref, far_ref)[slot // 4]
        target[slot % 4, :, :width] = jnp.where(first, kept, other)
        target[slot % 4, :, width : 2 * width] = jnp.where(first, other, kept)
        target[slot % 4, :, 2 * width :] = parts[slot]


def give_tokens(flags, kept, other, block):
    out = jax.ShapeDtypeStruct((4, SEQ, 3 * (D // 8)), jnp.bfloat16)
    full = pl.BlockSpec(memory_space=pltpu.VMEM)
    return pl.pallas_call(
        give_kernel,
        out_shape=[out] * 2,
        in_specs=[pl.BlockSpec(memory_space=pltpu.SMEM)] + [full] * 3,
        out_specs=[full] * 2,
        compiler_params=pltpu.CompilerParams(vmem_limit_bytes=24 * 1024 * 1024),
        cost_estimate=pl.CostEstimate(flops=0, transcendentals=0, bytes_accessed=4 * 1024 * 1024),
        name="give_tokens",
    )(flags, kept, other, block)


def join_kernel(near_ref, far_ref, *out_refs):
    width = near_ref.shape[2]
    for place, ref in enumerate(out_refs):
        ref[:, :width] = near_ref[place]
        ref[:, width:] = far_ref[place]


def join_lanes(near, far):
    count, rows, width = near.shape
    full = pl.BlockSpec(memory_space=pltpu.VMEM)
    return pl.pallas_call(
        join_kernel,
        out_shape=[jax.ShapeDtypeStruct((rows, 2 * width), near.dtype)] * count,
        in_specs=[full] * 2,
        out_specs=[full] * count,
        compiler_params=pltpu.CompilerParams(vmem_limit_bytes=24 * 1024 * 1024),
        cost_estimate=pl.CostEstimate(flops=0, transcendentals=0, bytes_accessed=4 * 1024 * 1024),
        name="join_lanes",
    )(near, far)
def pack_kernel(flags_ref, stream_ref, skip_ref, cot_ref, near_ref, give_ref):
    rows = near_ref.shape[1]
    pieces = []
    for number in range(8):
        at = slice(number * rows, (number + 1) * rows)
        piece = jnp.concatenate([stream_ref[:, at], skip_ref[:, at], cot_ref[:, at]], axis=0)
        pieces.append(piece.T)
    pieces = by_slot(pieces, [flags_ref[i] for i in range(3)])
    for place in range(4):
        near_ref[place] = pieces[place]
        give_ref[place] = pieces[4 + place]


def pack_tokens(flags, stream, skip_in, cotangent):
    out = jax.ShapeDtypeStruct((4, SEQ, 3 * stream.shape[0]), stream.dtype)
    full = pl.BlockSpec(memory_space=pltpu.VMEM)
    return pl.pallas_call(
        pack_kernel,
        out_shape=[out] * 2,
        in_specs=[pl.BlockSpec(memory_space=pltpu.SMEM)] + [full] * 3,
        out_specs=[full] * 2,
        compiler_params=pltpu.CompilerParams(vmem_limit_bytes=24 * 1024 * 1024),
        cost_estimate=pl.CostEstimate(flops=0, transcendentals=0, bytes_accessed=4 * 1024 * 1024),
        name="pack_tokens",
    )(flags, stream, skip_in, cotangent)


def back_kernel(flags_ref, *refs):
    blocks, (stream_ref, skip_ref, block_ref) = refs[:4], refs[4:]
    width = stream_ref.shape[0]
    rows = blocks[0].shape[0]
    pieces = [
        blocks[place][:, 3 * j * width : 3 * (j + 1) * width] for j in range(2) for place in range(4)
    ]
    for number, piece in enumerate(by_narrow(pieces, [flags_ref[i] for i in range(3)])):
        at = slice(number * rows, (number + 1) * rows)
        turned = piece.T
        stream_ref[:, at] = turned[:width].astype(jnp.float32)
        skip_ref[:, at] = turned[width : 2 * width].astype(jnp.float32)
        block_ref[:, at] = turned[2 * width :]


def back_tokens(flags, blocks):
    rows, width = blocks[0].shape
    shape = (width // 6, 8 * rows)
    full = pl.BlockSpec(memory_space=pltpu.VMEM)
    return pl.pallas_call(
        back_kernel,
        out_shape=[
            jax.ShapeDtypeStruct(shape, jnp.float32),
            jax.ShapeDtypeStruct(shape, jnp.float32),
            jax.ShapeDtypeStruct(shape, jnp.bfloat16),
        ],
        in_specs=[pl.BlockSpec(memory_space=pltpu.SMEM)] + [full] * 4,
        out_specs=[full] * 3,
        compiler_params=pltpu.CompilerParams(vmem_limit_bytes=24 * 1024 * 1024),
        cost_estimate=pl.CostEstimate(flops=0, transcendentals=0, bytes_accessed=8 * 1024 * 1024),
        name="back_tokens",
    )(flags, *blocks)


def chips(
    stream,
    skip_in,
    cotangent,
    skip_weight,
    qkv_weight,
    out_weight,
    up_weight,
    down_weight,
    norm_gain,
    norm_bias,
    row_skip,
    col_skip,
    row_qkv,
    col_qkv,
    row_out,
    col_out,
    row_up,
    col_up,
    row_down,
    col_down,
    second_gain,
    second_bias,
):
    bf16 = jnp.bfloat16
    f32 = jnp.float32
    axes = ("wide", "narrow")
    wide_count = lax.axis_size("wide")
    narrow_count = lax.axis_size("narrow")
    ZS, YS = narrow_count // 2, 2
    wide_index = lax.axis_index("wide")
    narrow_index = lax.axis_index("narrow")
    xi = wide_index // 2
    ci = wide_index % 2
    zi = narrow_index // 2
    yi = narrow_index % 2
    rows_local, feat = stream.shape
    half_head = feat // 2
    hidden = up_weight.shape[1]
    quarter = hidden // 4
    scale_factor = 1.0 / math.sqrt(HEAD)

    def perm(move):
        pairs = []
        for wide in range(wide_count):
            for narrow in range(narrow_count):
                x, c, z, y = move(wide // 2, wide % 2, narrow // 2, narrow % 2)
                target = (x * 2 + c) * narrow_count + z * 2 + y
                pairs.append((wide * narrow_count + narrow, target))
        return pairs

    def send(value, move):
        return lax.ppermute(value, axes, perm(move))

    def core(value):
        return send(value, lambda x, c, z, y: (x, 1 - c, z, y))

    def over_x(value):
        return send(value, lambda x, c, z, y: (1 - x, c, z, y))

    def over_y(value):
        return send(value, lambda x, c, z, y: (x, c, z, 1 - y))

    def xor_z(value, bit):
        return send(value, lambda x, c, z, y: (x, c, z ^ bit, y))

    def tie(*values):
        return lax.optimization_barrier(values)

    def tie(*values):
        return lax.optimization_barrier(values)

    def add_low(left, right):
        return (left.astype(f32) + right.astype(f32)).astype(bf16)

    def padded(own):
        return jnp.pad(own, ((0, PAD - SEQ), (0, 0)))

    distances = [0]
    bit = ZS // 2
    while bit:
        distances += [distance ^ bit for distance in distances]
        bit //= 2

    def gather_z(block):
        line = block[None]
        bit = ZS // 2
        while bit:
            line = jnp.concatenate([line, xor_z(line, bit)])
            bit //= 2
        return line

    order = jnp.stack(
        [(zi ^ distance) * 2 + (yi ^ j) for j in range(2) for distance in distances]
    ).astype(jnp.int32)

    def canonical(blocks):
        def exchange(table, flag, bit, width):
            return [
                jnp.where(flag == 0, table[index], table[index ^ bit]) for index in range(width)
            ]

        table = [None] * narrow_count
        for place, distance in enumerate(distances):
            for j in range(2):
                table[distance * 2 + j] = blocks[j * ZS + place]
        bit = 1
        while bit < narrow_count:
            table = exchange(table, (narrow_index // bit) % 2, bit, narrow_count)
            bit *= 2
        return table

    def split_y(array):
        grid = array.reshape((ZS, YS) + array.shape[1:])
        return pick(grid, yi, 1), pick(grid, 1 - yi, 1)

    def z_pieces(near, far):
        return [
            jnp.concatenate([pick(near, zi ^ distance, 0), pick(far, zi ^ distance, 0)], axis=-1)
            for distance in distances
        ]

    def z_line(pieces):
        return [pieces[0]] + [
            xor_z(piece, distance) for piece, distance in zip(pieces[1:], distances[1:])
        ]

    def halves_z(total):
        return total[: ZS // 2], total[ZS // 2 :]

    half = ZS // 2
    meta = xi.astype(jnp.int32)[None]
    is_first = ci == 0

    def in_order(pair, other_core):
        four = jnp.stack([pair, other_core])
        return jnp.stack(
            [pick(pick(four, c ^ ci, 0), x ^ xi, 0) for c in range(2) for x in range(2)]
        )

    def all_narrow(value):
        value = value + over_y(value)
        bit = 1
        while bit < ZS:
            value = value + xor_z(value, bit)
            bit *= 2
        return value

    def columns(array):
        size = D // wide_count
        return lax.dynamic_slice_in_dim(array, wide_index * size, size, array.ndim - 1).astype(f32)

    def statistics(grad, old):
        grad = grad.astype(f32)
        squares = grad * grad + EPS_SQUARE
        new = DECAY * old + (1.0 - DECAY) * (jnp.sum(squares, axis=1) / D)
        old_sum = jnp.where(lax.broadcasted_iota(jnp.int32, (D,), 0) == 0, jnp.sum(old), 0.0)
        sums = [
            jnp.sum(squares, axis=0),
            jnp.sum(grad * grad * (1.0 / new)[:, None], axis=0),
            old_sum,
        ]
        return new, sums

    def step_of(grad, new, totals, old_wide, rows_all, row_along_wide):
        wide_mean = totals[0] / rows_all
        wide_new = DECAY * old_wide + (1.0 - DECAY) * wide_mean
        if row_along_wide:
            row_mean = jnp.mean(wide_new)
        else:
            row_mean = DECAY * (totals[2][0] / rows_all) + (1.0 - DECAY) * jnp.mean(wide_mean)
        square_total = jnp.sum(totals[1] / wide_new) * row_mean
        ratio = jnp.sqrt(square_total / (rows_all * D)) / CLIP_LEVEL
        factor = -(STEP_RATE * jnp.sqrt(row_mean) / jnp.maximum(1.0, ratio))
        step = grad.astype(f32) * lax.rsqrt(new)[:, None] * (lax.rsqrt(wide_new) * factor)[None, :]
        return wide_new, ratio, step

    flags = jnp.stack([yi, zi % 2, zi // 2, ci]).astype(jnp.int32)
    token_near, token_give = pack_tokens(flags, stream.T, skip_in.T, cotangent.T)
    skip_block = pick(pick(skip_weight, ci, 0).reshape(2, feat // 2, D), xi, 0)
    attn_rows = jnp.concatenate(
        [
            pick(qkv_weight.transpose(1, 2, 0).reshape(3, 2, half_head, D), ci, 1),
            pick(out_weight.reshape(2, half_head, D), ci, 0)[None],
        ]
    ).reshape(2, 2 * half_head, D)
    attn_block = pick(attn_rows, xi, 0)
    skip_block, attn_block, token_give = tie(skip_block, attn_block, token_give)
    token_far = over_y(token_give)
    skip_two = xor_z(skip_block, 2)
    attn_two = xor_z(attn_block, 2)
    skip_line = jnp.stack([skip_block, skip_two])
    attn_line = jnp.stack([attn_block, attn_two])
    skip_line = jnp.concatenate([skip_line, xor_z(skip_line, 1)])
    attn_line = jnp.concatenate([attn_line, xor_z(attn_line, 1)])

    token_far, up_weight, down_weight = tie(token_far, up_weight, down_weight)
    token_blocks = z_line(join_lanes(token_near, token_far))
    skip_beside = over_y(skip_line)
    skip_across = over_x(skip_line)
    ffn_block = jnp.stack(
        [
            lax.dynamic_slice_in_dim(up_weight, (ci * 2 + xi) * quarter, quarter, 1).T,
            lax.dynamic_slice_in_dim(down_weight, (ci * 2 + xi) * quarter, quarter, 0),
        ]
    )

    skip_beside, skip_across, attn_line = tie(skip_beside, skip_across, attn_line)
    skip_corner = jnp.concatenate([over_x(skip_beside[:half]), over_y(skip_across[half:])])
    attn_beside = over_y(attn_line)
    attn_across = over_x(attn_line)

    ffn_full = lax.all_gather(ffn_block[None], "narrow", tiled=True)
    mine, give, cot_pad = take_tokens(flags, token_blocks)
    flat = jnp.concatenate([mine, core(give)])
    cot_own = cot_pad[:SEQ]
    attn_corner_x = over_x(attn_beside[:half])
    attn_corner_y = over_y(attn_across[half:])
    skip_near = jnp.concatenate([skip_line, skip_beside])
    skip_away = jnp.concatenate([skip_across, skip_corner])
    skip_mat = jnp.where(
        xi == 0,
        jnp.stack([skip_near, skip_away], axis=1),
        jnp.stack([skip_away, skip_near], axis=1),
    ).reshape(D, D)

    def both_images(own):
        own = padded(own)
        return jnp.concatenate([own, core(own)])

    def core_sum(kept, given):
        return (kept + core(given))[:SEQ]

    skip_part = matmul(flat, skip_mat, "rc,cd->rd")
    hidden_in = core_sum(skip_part[:PAD], skip_part[PAD:])
    unit_one, inverse_one = unit_parts(hidden_in)
    normed = both_images((unit_one * norm_gain[0] + norm_bias[0]).astype(bf16))

    attn_corner = jnp.concatenate([attn_corner_x, attn_corner_y])
    normed, cot_pad, attn_corner = tie(normed, cot_pad, attn_corner)
    cot_pair = jnp.concatenate([cot_pad, over_x(cot_pad)])
    attn_full = jnp.stack(
        [
            jnp.concatenate([attn_line, attn_beside]),
            jnp.concatenate([attn_across, attn_corner]),
        ]
    )
    attn_a, attn_b, qkv_kept, attended = attn_forward(meta, normed, attn_full)
    attn_b, cot_pair = tie(attn_b, cot_pair)
    middle = hidden_in + core_sum(attn_a, attn_b)
    unit_two, inverse_two = unit_parts(middle)
    mixed_own = padded((unit_two * norm_gain[1] + norm_bias[1]).astype(bf16))
    mixed_pair = jnp.concatenate([mixed_own, over_x(mixed_own)])
    mixed = jnp.concatenate([mixed_pair, core(mixed_pair)])
    cot = jnp.concatenate([cot_pair, core(cot_pair)])

    down_a, down_b, mixed_a, mixed_b, up_near, up_give, down_near, down_give = ffn(
        order, mixed, cot, ffn_full
    )
    mixed_sum = mixed_a + core(mixed_b)
    mixed_far = over_x(mixed_sum[PAD:].astype(bf16))
    ffn_far_up = over_y(up_give)
    ffn_down_one = xor_z(down_give, 1)

    mixed_far, down_b = tie(mixed_far, down_b)
    down_sum = down_a + core(down_b)
    down_far = over_x(down_sum[PAD:].astype(bf16))
    back_middle, gain_two, bias_two = norm_back_own(
        unit_two,
        inverse_two,
        (mixed_sum[:PAD] + mixed_far.astype(f32))[:SEQ],
        norm_gain[1],
    )
    grad_middle = cot_own.astype(f32) + back_middle
    middle_low = both_images(grad_middle.astype(bf16))
    normed_a, normed_b, own, other_near, other_x, other_y = attn_backward(
        meta, normed, middle_low, attn_full, qkv_kept, attended
    )

    normed_b, ffn_far_up, ffn_down_one, down_far = tie(
        normed_b, ffn_far_up, ffn_down_one, down_far
    )
    attn_from_x = over_x(other_x)
    attn_from_y = over_y(other_y)
    ffn_down = add_low(down_near, ffn_down_one)
    ffn_down_two = xor_z(ffn_down[:, 1], 2)
    ffn_up, ffn_up_give = halves_z(add_low(up_near, ffn_far_up))
    ffn_up_one = xor_z(ffn_up_give, 1)
    block_own = (middle + (down_sum[:PAD] + down_far.astype(f32))[:SEQ]).astype(bf16)
    back_hidden, gain_one, bias_one = norm_back_own(
        unit_one, inverse_one, core_sum(normed_a, normed_b), norm_gain[0]
    )
    hidden_low = both_images((grad_middle + back_hidden).astype(bf16))
    token_grad = matmul(hidden_low, skip_mat, "rd,cd->rc").astype(bf16)
    back_near, back_give = give_tokens(
        flags, token_grad[:PAD], core(token_grad[PAD:]), padded(block_own)
    )
    grad_skip = matmul(flat, hidden_low, "rc,rd->cd").astype(bf16)
    grad_skip = grad_skip.reshape(narrow_count, 2, feat // 2, D)
    skip_own, skip_other = pick(grad_skip, xi, 1), pick(grad_skip, 1 - xi, 1)

    attn_from_x, attn_from_y, back_give, skip_other = tie(
        attn_from_x, attn_from_y, back_give, skip_other
    )
    skip_from_x = over_x(skip_other[ZS : ZS + half])
    skip_from_y = over_y(skip_other[ZS + half :])
    back_far = over_y(back_give)
    attn_across = over_x(
        jnp.concatenate([other_near[:half], add_low(other_near[half:], attn_from_y)])
    )
    attn_beside = over_y(
        jnp.concatenate([add_low(own[ZS : ZS + half], attn_from_x), own[ZS + half :]])
    )

    skip_from_x, skip_from_y, ffn_down_two, ffn_up_one = tie(
        skip_from_x, skip_from_y, ffn_down_two, ffn_up_one
    )
    ffn_up = add_low(ffn_up, ffn_up_one)
    ffn_up_two = xor_z(ffn_up[1], 2)
    ffn_down = add_low(ffn_down[:, 0], ffn_down_two)
    ffn_down_far = over_y(ffn_down[1])
    skip_across = over_x(
        jnp.concatenate([skip_other[:half], add_low(skip_other[half:ZS], skip_from_y)])
    )
    skip_beside = over_y(
        jnp.concatenate([add_low(skip_own[ZS : ZS + half], skip_from_x), skip_own[ZS + half :]])
    )
    back_blocks = z_line(join_lanes(back_near, back_far))

    attn_beside, attn_across, ffn_up_two, ffn_down_far = tie(
        attn_beside, attn_across, ffn_up_two, ffn_down_far
    )
    attn_total, attn_give = halves_z(
        (own[:ZS].astype(f32) + attn_beside.astype(f32) + attn_across.astype(f32)).astype(bf16)
    )
    attn_one = xor_z(attn_give, 1)
    ffn_own = jnp.stack([add_low(ffn_up[0], ffn_up_two), add_low(ffn_down[0], ffn_down_far)])
    ffn_x = over_x(ffn_own)

    attn_one, ffn_x = tie(attn_one, ffn_x)
    attn_total = add_low(attn_total, attn_one)
    attn_two = xor_z(attn_total[1], 2)
    ffn_pair = jnp.stack([ffn_own, ffn_x])
    (ffn_all,) = tie(in_order(ffn_pair, core(ffn_pair)))
    grad_up_rows = ffn_all[:, 0].reshape(hidden, D)
    grad_down = ffn_all[:, 1].reshape(hidden, D)
    new_col_up, up_sums = statistics(grad_up_rows, col_up)
    new_row_down, down_sums = statistics(grad_down, row_down)

    skip_beside, skip_across, *ffn_sums = tie(skip_beside, skip_across, *up_sums, *down_sums)
    skip_total, skip_give = halves_z(
        (skip_own[:ZS].astype(f32) + skip_beside.astype(f32) + skip_across.astype(f32)).astype(
            bf16
        )
    )
    skip_one = xor_z(skip_give, 1)

    attn_two, skip_one, *back_blocks = tie(attn_two, skip_one, *back_blocks)
    attn_own = add_low(attn_total[0], attn_two)
    attn_x = over_x(attn_own)
    skip_total = add_low(skip_total, skip_one)
    skip_two = xor_z(skip_total[1], 2)
    grad_stream, grad_skip_in, block_out = [
        part.T for part in back_tokens(flags, back_blocks)
    ]
    attn_pair = jnp.stack([attn_own, attn_x])
    (attn_all,) = tie(in_order(attn_pair, core(attn_pair)))
    attn_all = attn_all.reshape(2, 4, half_head, D)
    grad_qkv_rows = attn_all[:, :3].transpose(1, 0, 2, 3).reshape(3 * feat, D)
    grad_out = attn_all[:, 3].reshape(feat, D)
    new_col_qkv, qkv_sums = statistics(grad_qkv_rows, col_qkv.reshape(-1))
    new_row_out, out_sums = statistics(grad_out, row_out)
    grad_up_out = columns(grad_up_rows).T
    grad_down_out = columns(grad_down)

    grad_stream, grad_skip_in, block_out, grad_up_out, grad_down_out, skip_two, *sums = tie(
        grad_stream,
        grad_skip_in,
        block_out,
        grad_up_out,
        grad_down_out,
        skip_two,
        *qkv_sums,
        *out_sums,
    )
    skip_last = add_low(skip_total[0], skip_two)
    skip_pair = jnp.stack([skip_last, over_x(skip_last)])
    (skip_all,) = tie(in_order(skip_pair, core(skip_pair)))
    grad_skip_rows = skip_all.reshape(2 * feat, D)

    norm_sums = jnp.stack([gain_one, gain_two, bias_one, bias_two])
    norm_sums = norm_sums + core(norm_sums)
    norm_sums = norm_sums + over_x(norm_sums)
    new_row_skip, skip_sums = statistics(grad_skip_rows, row_skip.reshape(-1))
    totals = all_narrow(
        jnp.concatenate([jnp.stack(skip_sums + sums + list(ffn_sums)), norm_sums])
    )
    gain_total = totals[15:17]
    bias_total = totals[17:19]
    new_col_skip, ratio_skip, step_skip = step_of(
        grad_skip_rows, new_row_skip, totals[:3], col_skip, 2 * D, False
    )
    new_row_qkv, ratio_qkv, step_qkv = step_of(
        grad_qkv_rows, new_col_qkv, totals[3:6], row_qkv, 3 * D, True
    )
    new_col_out, ratio_out, step_out = step_of(
        grad_out, new_row_out, totals[6:9], col_out, D, False
    )
    new_row_up, ratio_up, step_up = step_of(
        grad_up_rows, new_col_up, totals[9:12], row_up, hidden * narrow_count, True
    )
    new_col_down, ratio_down, step_down = step_of(
        grad_down, new_row_down, totals[12:15], col_down, hidden * narrow_count, False
    )
    new_up = up_weight.astype(f32) + step_up.T
    new_down = down_weight.astype(f32) + step_down
    clip_ratio = jnp.stack([ratio_skip, ratio_qkv, ratio_out, ratio_up, ratio_down])
    new_skip = skip_weight.astype(f32) + step_skip.reshape(2, feat, D)
    new_qkv = qkv_weight.astype(f32) + step_qkv.reshape(3, feat, D).transpose(2, 0, 1)
    new_second_gain, gain_step = plain_update(gain_total, second_gain)
    new_second_bias, bias_step = plain_update(bias_total, second_bias)
    return (
        block_out,
        grad_stream,
        grad_skip_in,
        columns(grad_skip_rows).reshape(2, feat, -1),
        columns(grad_qkv_rows).reshape(3, feat, -1).transpose(2, 0, 1),
        columns(grad_out),
        grad_up_out,
        grad_down_out,
        gain_total,
        bias_total,
        new_row_skip.reshape(2, feat),
        new_col_skip,
        new_row_qkv,
        new_col_qkv.reshape(3, feat),
        new_row_out,
        new_col_out,
        new_row_up,
        new_col_up,
        new_row_down,
        new_col_down,
        new_second_gain,
        new_second_bias[0],
        new_second_bias[1],
        new_skip,
        new_qkv,
        step_out,
        new_up,
        new_down,
        gain_step,
        bias_step,
        clip_ratio,
    )


def solution(mesh):
    wide, narrow = mesh.shape["wide"], mesh.shape["narrow"]
    body = chips if (wide == 4 and narrow == 8) else local
    in_specs = (
        P("wide", "narrow"),
        P("wide", "narrow"),
        P("wide", "narrow"),
        P(None, "narrow", None),
        P(None, None, "narrow"),
        P("narrow", None),
        P(None, "narrow"),
        P("narrow", None),
        P(),
        P(),
        P(None, "narrow"),
        P(),
        P(),
        P(None, "narrow"),
        P("narrow"),
        P(),
        P(),
        P("narrow"),
        P("narrow"),
        P(),
        P(),
        P(),
    )
    out_specs = (
        P("wide", "narrow"),
        P("wide", "narrow"),
        P("wide", "narrow"),
        P(None, "narrow", "wide"),
        P("wide", None, "narrow"),
        P("narrow", "wide"),
        P("wide", "narrow"),
        P("narrow", "wide"),
        P(),
        P(),
        P(None, "narrow"),
        P(),
        P(),
        P(None, "narrow"),
        P("narrow"),
        P(),
        P(),
        P("narrow"),
        P("narrow"),
        P(),
        P(),
        P(),
        P(),
        P(None, "narrow", None),
        P(None, None, "narrow"),
        P("narrow", None),
        P(None, "narrow"),
        P("narrow", None),
        P(),
        P(),
        P(),
    )
    return jax.shard_map(body, mesh=mesh, in_specs=in_specs, out_specs=out_specs, check_vma=False)
```

```python
import math

import jax
import jax.numpy as jnp
from jax import lax
from jax.experimental import pallas as pl
from jax.experimental.pallas import tpu as pltpu
from jax.sharding import PartitionSpec as P

D = 1152
FF = 4608
SEQ = 258
HEAD = 72


NORM_EPS = 1e-05
EPS_SQUARE = 1e-30
DECAY = 0.5
STEP_RATE = 0.05
CLIP_LEVEL = 0.25


def layer_norm(values, gain, shift):
    average = jnp.mean(values, axis=-1, keepdims=True)
    centered = values - average
    variance = jnp.mean(centered * centered, axis=-1, keepdims=True)
    return centered * lax.rsqrt(variance + NORM_EPS) * gain + shift


def norm_back(values, grad, gain, own_rows):
    average = jnp.mean(values, axis=-1, keepdims=True)
    centered = values - average
    variance = jnp.mean(centered * centered, axis=-1, keepdims=True)
    inverse = lax.rsqrt(variance + NORM_EPS)
    unit = centered * inverse
    scaled = grad * gain
    inner = (
        scaled
        - jnp.mean(scaled, axis=-1, keepdims=True)
        - unit * jnp.mean(scaled * unit, axis=-1, keepdims=True)
    )
    weighted = grad * own_rows
    return (inner * inverse, jnp.sum(weighted * unit, axis=0), jnp.sum(weighted, axis=0))


def gelu_exact(inputs):
    return jax.nn.gelu(inputs, approximate=False)


def matmul(left, right, form):
    return jnp.einsum(form, left, right, preferred_element_type=jnp.float32)


def plain_update(grad, second_old):
    second_new = DECAY * second_old + (1.0 - DECAY) * (grad * grad + EPS_SQUARE)
    update = grad * lax.rsqrt(second_new)
    spread = jnp.sqrt(jnp.mean(update * update))
    update = update / jnp.maximum(1.0, spread / CLIP_LEVEL)
    return (second_new, -(STEP_RATE * update))


def wide_slice(array, dim_index, count, wide_index):
    piece_size = array.shape[dim_index] // count
    return lax.dynamic_slice_in_dim(array, wide_index * piece_size, piece_size, dim_index)


def local(
    stream,
    skip_in,
    cotangent,
    skip_weight,
    qkv_weight,
    out_weight,
    up_weight,
    down_weight,
    norm_gain,
    norm_bias,
    row_skip,
    col_skip,
    row_qkv,
    col_qkv,
    row_out,
    col_out,
    row_up,
    col_up,
    row_down,
    col_down,
    second_gain,
    second_bias,
):
    rows_local, feat_local = stream.shape
    images = rows_local // SEQ
    heads_local = feat_local // HEAD
    scale_factor = 1.0 / math.sqrt(HEAD)
    split_shape = (images, SEQ, heads_local, HEAD)
    narrow_count = lax.axis_size("narrow")
    narrow_index = lax.axis_index("narrow")
    share_rows = -(-rows_local // narrow_count)
    row_start = narrow_index * share_rows
    row_ids = lax.broadcasted_iota(jnp.int32, (rows_local, 1), 0)
    own_mask = ((row_ids >= row_start) & (row_ids < row_start + share_rows)).astype(jnp.float32)

    def full_sum(values):
        return lax.psum(values, "narrow")

    partial_in = matmul(stream, skip_weight[0], "rc,cd->rd") + matmul(
        skip_in, skip_weight[1], "rc,cd->rd"
    )
    hidden_in = full_sum(partial_in)
    normed = layer_norm(hidden_in, norm_gain[0], norm_bias[0]).astype(jnp.bfloat16)
    projected = matmul(normed, qkv_weight, "rd,dtc->rtc").astype(jnp.bfloat16)
    queries = projected[:, 0].reshape(split_shape)
    key_vectors = projected[:, 1].reshape(split_shape)
    value_vectors = projected[:, 2].reshape(split_shape)
    scores = matmul(queries, key_vectors, "bqhe,bkhe->bhqk") * scale_factor
    row_max = jnp.max(scores, axis=-1, keepdims=True)
    exponent = jnp.exp(scores - row_max)
    row_total = jnp.sum(exponent, axis=-1, keepdims=True)
    log_total = row_max + jnp.log(row_total)
    probs_low = (exponent / row_total).astype(jnp.bfloat16)
    attended = (
        matmul(probs_low, value_vectors, "bhqk,bkhe->bqhe")
        .reshape(rows_local, feat_local)
        .astype(jnp.bfloat16)
    )
    attn_part = matmul(attended, out_weight, "rc,cd->rd")
    middle = hidden_in + full_sum(attn_part)
    mixed_in = layer_norm(middle, norm_gain[1], norm_bias[1]).astype(jnp.bfloat16)
    middle_own = lax.dynamic_slice_in_dim(middle, narrow_index * feat_local, feat_local, 1)
    up_input = matmul(mixed_in, up_weight, "rd,df->rf")
    activation = gelu_exact(up_input).astype(jnp.bfloat16)
    down_part = matmul(activation, down_weight, "rf,fd->rd")
    block_out = (
        middle_own + lax.psum_scatter(down_part, "narrow", scatter_dimension=1, tiled=True)
    ).astype(jnp.bfloat16)
    grad_full = lax.all_gather(cotangent, "narrow", axis=1, tiled=True)
    grad_down = matmul(activation, grad_full, "rf,rd->fd")
    grad_act = matmul(grad_full, down_weight, "rd,fd->rf")
    gelu_value, gelu_back = jax.vjp(gelu_exact, up_input)
    grad_up_in = gelu_back(grad_act)[0].astype(jnp.bfloat16)
    grad_up = matmul(mixed_in, grad_up_in, "rd,rf->df")
    mixed_part = matmul(grad_up_in, up_weight, "rf,df->rd")
    grad_mixed = full_sum(mixed_part)
    back_middle, back_gain_two, back_bias_two = norm_back(
        middle, grad_mixed, norm_gain[1], own_mask
    )
    grad_middle = grad_full.astype(jnp.float32) + back_middle
    middle_low = grad_middle.astype(jnp.bfloat16)
    grad_out = matmul(attended, middle_low, "rc,rd->cd")
    grad_attended = (
        matmul(middle_low, out_weight, "rd,cd->rc").astype(jnp.bfloat16).reshape(split_shape)
    )
    scores_again = matmul(queries, key_vectors, "bqhe,bkhe->bhqk") * scale_factor
    probs = jnp.exp(scores_again - log_total)
    probs_again = probs.astype(jnp.bfloat16)
    grad_values = matmul(probs_again, grad_attended, "bhqk,bqhe->bkhe")
    grad_probs = matmul(grad_attended, value_vectors, "bqhe,bkhe->bhqk")
    inner_sum = jnp.sum(probs * grad_probs, axis=-1, keepdims=True)
    grad_scores = (probs * (grad_probs - inner_sum) * scale_factor).astype(jnp.bfloat16)
    grad_queries = matmul(grad_scores, key_vectors, "bhqk,bkhe->bqhe")
    grad_keys = matmul(grad_scores, queries, "bhqk,bqhe->bkhe")
    grad_projected = jnp.stack(
        [
            grad_queries.reshape(rows_local, feat_local),
            grad_keys.reshape(rows_local, feat_local),
            grad_values.reshape(rows_local, feat_local),
        ],
        axis=1,
    ).astype(jnp.bfloat16)
    grad_qkv = matmul(normed, grad_projected, "rd,rtc->dtc")
    normed_part = matmul(grad_projected, qkv_weight, "rtc,dtc->rd")
    grad_normed = full_sum(normed_part)
    back_hidden, back_gain_one, back_bias_one = norm_back(
        hidden_in, grad_normed, norm_gain[0], own_mask
    )
    hidden_low = (grad_middle + back_hidden).astype(jnp.bfloat16)
    grad_skip = jnp.stack(
        [matmul(stream, hidden_low, "rc,rd->cd"), matmul(skip_in, hidden_low, "rc,rd->cd")]
    )
    grad_stream = matmul(hidden_low, skip_weight[0], "rd,cd->rc")
    grad_skip_in = matmul(hidden_low, skip_weight[1], "rd,cd->rc")
    gain_grads = jnp.stack([back_gain_one, back_gain_two])
    bias_grads = jnp.stack([back_bias_one, back_bias_two])
    wide_count = lax.axis_size("wide")
    wide_index = lax.axis_index("wide")
    wide_dims = (2, 0, 1, 0, 1)
    wide_axes = ((0, 1), (1, 2), (0,), (1,), (0,))
    narrow_axes = ((2,), (0,), (1,), (0,), (1,))
    wide_counts = (2 * D, 3 * D, D, FF, FF)
    row_along_wide = (False, True, False, True, False)
    entry_counts = (2 * D * D, 3 * D * D, D * D, D * FF, FF * D)
    old_slots = (0, 0, 1, 0, 2)
    weights = (skip_weight, qkv_weight, out_weight, up_weight, down_weight)
    old_wide = (col_skip, row_qkv, col_out, row_up, col_down)
    old_narrow = (row_skip, col_qkv, row_out, col_up, row_down)
    summed = lax.psum(
        (grad_skip, grad_qkv, grad_out, grad_up, grad_down, gain_grads, bias_grads), "wide"
    )
    pieces = summed[:5]
    gain_section = summed[5]
    bias_section = summed[6]
    squares = [piece * piece + EPS_SQUARE for piece in pieces]
    wide_parts = [jnp.sum(squares[number], axis=wide_axes[number]) for number in range(5)]
    narrow_parts = [jnp.sum(squares[number], axis=narrow_axes[number]) for number in range(5)]
    old_sums = jnp.stack([jnp.sum(row_skip), jnp.sum(row_out), jnp.sum(row_down)])
    stat_total = lax.psum(
        (
            wide_parts[0],
            wide_parts[1],
            wide_parts[2],
            wide_parts[3],
            wide_parts[4],
            old_sums,
            gain_section,
            bias_section,
        ),
        "narrow",
    )
    old_row_means = (stat_total[5][0] / (2 * D), stat_total[5][1] / D, stat_total[5][2] / FF)
    wide_stats = stat_total[:5]
    gain_total = stat_total[6]
    bias_total = stat_total[7]
    new_wide = []
    new_narrow = []
    updates = []
    for number in range(5):
        wide_mean = wide_stats[number] / wide_counts[number]
        wide_new = DECAY * old_wide[number] + (1.0 - DECAY) * wide_mean
        narrow_new = DECAY * old_narrow[number] + (1.0 - DECAY) * narrow_parts[number] / D
        if row_along_wide[number]:
            row_mean = jnp.mean(wide_new)
        else:
            row_mean = DECAY * old_row_means[old_slots[number]] + (1.0 - DECAY) * jnp.mean(
                wide_mean
            )
        dim_index = wide_dims[number]
        piece_size = pieces[number].shape[dim_index]
        broadcast_shape = [1] * pieces[number].ndim
        broadcast_shape[dim_index] = piece_size
        second = (
            jnp.expand_dims(narrow_new, dim_index) * wide_new.reshape(broadcast_shape) / row_mean
        )
        updates.append(pieces[number] * lax.rsqrt(second))
        new_wide.append(wide_new)
        new_narrow.append(narrow_new)
    update_squares = jnp.stack([jnp.sum(update * update) for update in updates])
    square_totals = lax.psum(update_squares, "narrow")
    counts_array = jnp.array(entry_counts, jnp.float32)
    clip_ratio = jnp.sqrt(square_totals / counts_array) / CLIP_LEVEL
    new_pieces = []
    for number in range(5):
        spread = jnp.sqrt(square_totals[number] / entry_counts[number])
        step_piece = -(STEP_RATE * (updates[number] / jnp.maximum(1.0, spread / CLIP_LEVEL)))
        if number == 2:
            new_pieces.append(step_piece)
        else:
            weight_piece = weights[number]
            new_pieces.append(weight_piece.astype(jnp.float32) + step_piece)
    grad_outs = [
        wide_slice(pieces[number], wide_dims[number], wide_count, wide_index) for number in range(5)
    ]
    new_second_gain, gain_step = plain_update(gain_total, second_gain)
    new_second_bias, bias_step = plain_update(bias_total, second_bias)
    return (
        block_out,
        grad_stream,
        grad_skip_in,
        grad_outs[0],
        grad_outs[1],
        grad_outs[2],
        grad_outs[3],
        grad_outs[4],
        gain_total,
        bias_total,
        new_narrow[0],
        new_wide[0],
        new_wide[1],
        new_narrow[1],
        new_narrow[2],
        new_wide[2],
        new_wide[3],
        new_narrow[3],
        new_narrow[4],
        new_wide[4],
        new_second_gain,
        new_second_bias[0],
        new_second_bias[1],
        new_pieces[0],
        new_pieces[1],
        new_pieces[2],
        new_pieces[3],
        new_pieces[4],
        gain_step,
        bias_step,
        clip_ratio,
    )


def unit_parts(values):
    average = jnp.mean(values, axis=-1, keepdims=True)
    centered = values - average
    variance = jnp.mean(centered * centered, axis=-1, keepdims=True)
    inverse = lax.rsqrt(variance + NORM_EPS)
    return centered * inverse, inverse


def norm_back_own(unit, inverse, grad, gain):
    scaled = grad * gain
    inner = (
        scaled
        - jnp.mean(scaled, axis=-1, keepdims=True)
        - unit * jnp.mean(scaled * unit, axis=-1, keepdims=True)
    )
    rows = tuple(range(grad.ndim - 1))
    return inner * inverse, jnp.sum(grad * unit, axis=rows), jnp.sum(grad, axis=rows)


def pick(array, index, axis):
    return lax.dynamic_index_in_dim(array, index, axis, keepdims=False)


PAD = 272


def dot_nt(left, right):
    return lax.dot_general(left, right, (((1,), (1,)), ((), ())), preferred_element_type=jnp.float32)


def dot_nn(left, right):
    return lax.dot_general(left, right, (((1,), (0,)), ((), ())), preferred_element_type=jnp.float32)


def dot_tn(left, right):
    return lax.dot_general(left, right, (((0,), (0,)), ((), ())), preferred_element_type=jnp.float32)


def accumulate(step, refs, value):
    size = refs[0].shape[0]

    @pl.when(step == 0)
    def _():
        for number, ref in enumerate(refs):
            ref[...] = value[number * size : (number + 1) * size]

    @pl.when(step > 0)
    def _():
        for number, ref in enumerate(refs):
            ref[...] += value[number * size : (number + 1) * size]


def ffn_first_kernel(order_ref, mixed_ref, cot_ref, *refs):
    weights, (mixed_a, mixed_b, act_ref, grad_ref) = refs[:4], refs[4:]
    up = jnp.concatenate([ref[0, 0] for ref in weights], axis=0)
    down = jnp.concatenate([ref[0, 1] for ref in weights], axis=0)
    up_input = dot_nt(mixed_ref[...], up)
    gate = 0.5 * (1.0 + lax.erf(up_input * (1.0 / math.sqrt(2.0))))
    act_ref[0] = (up_input * gate).astype(jnp.bfloat16)
    slope = gate + up_input * (jnp.exp(-0.5 * up_input * up_input) * (1.0 / math.sqrt(2.0 * math.pi)))
    grad = (dot_nt(cot_ref[...], down) * slope).astype(jnp.bfloat16)
    grad_ref[0] = grad
    accumulate(pl.program_id(0), (mixed_a, mixed_b), dot_nn(grad, up))


def ffn_second_kernel(order_ref, mixed_ref, cot_ref, act_ref, grad_ref, *refs):
    weights, (down_a, down_b, up_near, up_far, down_near, down_far) = refs[:4], refs[4:]
    step = pl.program_id(0)
    down = jnp.concatenate([ref[0, 0] for ref in weights], axis=0)
    grad_up = dot_tn(grad_ref[0], mixed_ref[...]).astype(jnp.bfloat16)
    grad_down = dot_tn(act_ref[0], cot_ref[...]).astype(jnp.bfloat16)
    for j, ref in enumerate((up_near, up_far)):

        @pl.when(step == j)
        def _():
            ref[...] = grad_up.reshape(ref.shape)

    halves = grad_down.reshape((2,) + down_near.shape[1:])
    down_near[0] = halves[0]
    down_far[0] = halves[1]
    accumulate(step, (down_a, down_b), dot_nn(act_ref[0], down))


def ffn_specs(tokens, rows):
    whole = pl.BlockSpec((tokens, D), lambda t, m: (0, 0))
    half = pl.BlockSpec((tokens // 2, D), lambda t, m: (0, 0))
    units = pl.BlockSpec((1, tokens, 4 * rows), lambda t, m: (t, 0, 0))
    return whole, half, units


def ffn_first(order, mixed, cot, weights):
    count, _, rows, _ = weights.shape
    tokens = mixed.shape[0]
    whole, half, units = ffn_specs(tokens, rows)

    def weight_spec(slot):
        return pl.BlockSpec((1, 2, rows, D), lambda t, m: (m[4 * t + slot], 0, 0, 0))

    part = jax.ShapeDtypeStruct((tokens // 2, D), jnp.float32)
    hidden = jax.ShapeDtypeStruct((count // 4, tokens, 4 * rows), jnp.bfloat16)
    return pl.pallas_call(
        ffn_first_kernel,
        out_shape=[part] * 2 + [hidden] * 2,
        grid_spec=pltpu.PrefetchScalarGridSpec(
            num_scalar_prefetch=1,
            grid=(count // 4,),
            in_specs=[whole, whole] + [weight_spec(slot) for slot in range(4)],
            out_specs=[half] * 2 + [units] * 2,
        ),
        compiler_params=pltpu.CompilerParams(
            dimension_semantics=("arbitrary",), vmem_limit_bytes=56 * 1024 * 1024
        ),
        cost_estimate=pl.CostEstimate(
            flops=6 * tokens * D * count * rows, transcendentals=0, bytes_accessed=24 * 1024 * 1024
        ),
        name="ffn_first",
    )(order, mixed, cot, *([weights] * 4))


def ffn_second(order, mixed, cot, act, grad, weights):
    count, _, rows, _ = weights.shape
    tokens = mixed.shape[0]
    whole, half, units = ffn_specs(tokens, rows)

    def weight_spec(slot):
        return pl.BlockSpec((1, 1, rows, D), lambda t, m: (m[4 * t + slot], 1, 0, 0))

    part = jax.ShapeDtypeStruct((tokens // 2, D), jnp.float32)
    side = jax.ShapeDtypeStruct((4, rows, D), jnp.bfloat16)
    turn = jax.ShapeDtypeStruct((2, 2, rows, D), jnp.bfloat16)
    side_block = pl.BlockSpec((4, rows, D), lambda t, m: (0, 0, 0))
    turn_block = pl.BlockSpec((1, 2, rows, D), lambda t, m: (t, 0, 0, 0))
    return pl.pallas_call(
        ffn_second_kernel,
        out_shape=[part] * 2 + [side] * 2 + [turn] * 2,
        grid_spec=pltpu.PrefetchScalarGridSpec(
            num_scalar_prefetch=1,
            grid=(count // 4,),
            in_specs=[whole, whole, units, units] + [weight_spec(slot) for slot in range(4)],
            out_specs=[half] * 2 + [side_block] * 2 + [turn_block] * 2,
        ),
        compiler_params=pltpu.CompilerParams(
            dimension_semantics=("arbitrary",), vmem_limit_bytes=56 * 1024 * 1024
        ),
        cost_estimate=pl.CostEstimate(
            flops=6 * tokens * D * count * rows, transcendentals=0, bytes_accessed=24 * 1024 * 1024
        ),
        name="ffn_second",
    )(order, mixed, cot, act, grad, *([weights] * 4))


def soft(q, k):
    scores = dot_nt(q, k) * (1.0 / math.sqrt(HEAD))
    column = lax.broadcasted_iota(jnp.int32, scores.shape, 1)
    scores = jnp.where(column < SEQ, scores, -1e30)
    exponent = jnp.exp(scores - jnp.max(scores, axis=-1, keepdims=True))
    return exponent / jnp.sum(exponent, axis=-1, keepdims=True)


GROUP = 4


def head_weights(qk_ref, vo_ref):
    qk = [qk_ref[0, head] for head in range(GROUP)]
    v = [vo_ref[0, head, :HEAD] for head in range(GROUP)]
    out = [vo_ref[0, head, HEAD:] for head in range(GROUP)]
    return jnp.concatenate(qk + v, axis=0), jnp.concatenate(out, axis=0)


def head_columns(head):
    first = 2 * HEAD * head
    value = 2 * HEAD * GROUP + HEAD * head
    return (
        slice(first, first + HEAD),
        slice(first + HEAD, first + 2 * HEAD),
        slice(value, value + HEAD),
    )


def attn_forward_kernel(meta_ref, normed_ref, qk_ref, vo_ref, part_a, part_b, qkv_ref, attended_ref):
    step = pl.program_id(0)
    weights, out_weight = head_weights(qk_ref, vo_ref)
    qkv_ref[0] = dot_nt(normed_ref[...], weights).astype(jnp.bfloat16)
    for head in range(GROUP):
        q_at, k_at, v_at = head_columns(head)
        for image in range(2):
            rows = slice(image * PAD, (image + 1) * PAD)
            probs = soft(qkv_ref[0, rows, q_at], qkv_ref[0, rows, k_at]).astype(jnp.bfloat16)
            attended_ref[0, rows, HEAD * head : HEAD * (head + 1)] = dot_nn(
                probs, qkv_ref[0, rows, v_at]
            ).astype(jnp.bfloat16)
    accumulate(step, (part_a, part_b), dot_nn(attended_ref[0], out_weight))


def attn_specs(rows, tokens):
    whole = pl.BlockSpec((tokens, D), lambda s, m: (0, 0))
    half = pl.BlockSpec((tokens // 2, D), lambda s, m: (0, 0))
    qk = pl.BlockSpec((1, GROUP, rows, D), lambda s, m: (m[0], s, 0, 0))
    vo = pl.BlockSpec((1, GROUP, rows, D), lambda s, m: (1 - m[0], s, 0, 0))
    qkv = pl.BlockSpec((1, tokens, 3 * HEAD * GROUP), lambda s, m: (s, 0, 0))
    att = pl.BlockSpec((1, tokens, HEAD * GROUP), lambda s, m: (s, 0, 0))
    return whole, half, qk, vo, qkv, att


def attn_forward(meta, normed, weights):
    heads, rows = weights.shape[1:3]
    tokens = normed.shape[0]
    whole, half, qk, vo, qkv, att = attn_specs(rows, tokens)
    return pl.pallas_call(
        attn_forward_kernel,
        out_shape=[
            jax.ShapeDtypeStruct((tokens // 2, D), jnp.float32),
            jax.ShapeDtypeStruct((tokens // 2, D), jnp.float32),
            jax.ShapeDtypeStruct((heads // GROUP, tokens, 3 * HEAD * GROUP), jnp.bfloat16),
            jax.ShapeDtypeStruct((heads // GROUP, tokens, HEAD * GROUP), jnp.bfloat16),
        ],
        grid_spec=pltpu.PrefetchScalarGridSpec(
            num_scalar_prefetch=1,
            grid=(heads // GROUP,),
            in_specs=[whole, qk, vo],
            out_specs=[half, half, qkv, att],
        ),
        compiler_params=pltpu.CompilerParams(
            dimension_semantics=("arbitrary",), vmem_limit_bytes=48 * 1024 * 1024
        ),
        cost_estimate=pl.CostEstimate(flops=0, transcendentals=0, bytes_accessed=1024 * 1024),
        name="attn_forward",
    )(meta, normed, weights, weights)


def attn_backward_kernel(
    meta_ref,
    normed_ref,
    low_ref,
    qk_ref,
    vo_ref,
    qkv_ref,
    attended_ref,
    part_a,
    part_b,
    own_ref,
    near_ref,
    far_x_ref,
    far_y_ref,
    grads_s,
    out_s,
):
    step = pl.program_id(0)
    normed = normed_ref[...]
    low = low_ref[...]
    weights, out_weight = head_weights(qk_ref, vo_ref)
    out_s[...] = dot_nt(low, out_weight).astype(jnp.bfloat16)
    for head in range(GROUP):
        q_at, k_at, v_at = head_columns(head)
        for image in range(2):
            rows = slice(image * PAD, (image + 1) * PAD)
            q = qkv_ref[0, rows, q_at]
            k = qkv_ref[0, rows, k_at]
            v = qkv_ref[0, rows, v_at]
            grad = out_s[rows, HEAD * head : HEAD * (head + 1)]
            probs = soft(q, k)
            grads_s[rows, v_at] = dot_tn(probs.astype(jnp.bfloat16), grad).astype(jnp.bfloat16)
            grad_probs = dot_nt(grad, v)
            inner = jnp.sum(probs * grad_probs, axis=-1, keepdims=True)
            grad_scores = (probs * (grad_probs - inner) * (1.0 / math.sqrt(HEAD))).astype(
                jnp.bfloat16
            )
            grads_s[rows, q_at] = dot_nn(grad_scores, k).astype(jnp.bfloat16)
            grads_s[rows, k_at] = dot_tn(grad_scores, q).astype(jnp.bfloat16)
    projected = grads_s[...]
    accumulate(step, (part_a, part_b), dot_nn(projected, weights))
    mats = dot_tn(projected, normed)
    outs = dot_tn(attended_ref[0], low)
    first = meta_ref[0] == 0
    for head in range(GROUP):
        q_at, k_at, v_at = head_columns(head)
        query_key = mats[q_at.start : k_at.stop]
        value_out = jnp.concatenate([mats[v_at], outs[HEAD * head : HEAD * (head + 1)]], axis=0)
        own_ref[head] = jnp.where(first, query_key, value_out).astype(jnp.bfloat16)
        other = jnp.where(first, value_out, query_key).astype(jnp.bfloat16)

        @pl.when(step == 0)
        def _():
            near_ref[head] = other

        @pl.when(step == 1)
        def _():
            if head < 2:
                far_x_ref[head] = other
            else:
                far_y_ref[head - 2] = other


def attn_backward(meta, normed, low, weights, qkv_kept, attended):
    heads, rows = weights.shape[1:3]
    tokens = normed.shape[0]
    whole, half, qk, vo, qkv, att = attn_specs(rows, tokens)

    def fixed(size):
        return pl.BlockSpec((size, rows, D), lambda s, m: (0, 0, 0))

    return pl.pallas_call(
        attn_backward_kernel,
        out_shape=[
            jax.ShapeDtypeStruct((tokens // 2, D), jnp.float32),
            jax.ShapeDtypeStruct((tokens // 2, D), jnp.float32),
            jax.ShapeDtypeStruct((heads, rows, D), jnp.bfloat16),
            jax.ShapeDtypeStruct((4, rows, D), jnp.bfloat16),
            jax.ShapeDtypeStruct((2, rows, D), jnp.bfloat16),
            jax.ShapeDtypeStruct((2, rows, D), jnp.bfloat16),
        ],
        grid_spec=pltpu.PrefetchScalarGridSpec(
            num_scalar_prefetch=1,
            grid=(heads // GROUP,),
            in_specs=[whole, whole, qk, vo, qkv, att],
            out_specs=[
                half,
                half,
                pl.BlockSpec((GROUP, rows, D), lambda s, m: (s, 0, 0)),
                fixed(4),
                fixed(2),
                fixed(2),
            ],
            scratch_shapes=[
                pltpu.VMEM((tokens, 3 * HEAD * GROUP), jnp.bfloat16),
                pltpu.VMEM((tokens, HEAD * GROUP), jnp.bfloat16),
            ],
        ),
        compiler_params=pltpu.CompilerParams(
            dimension_semantics=("arbitrary",), vmem_limit_bytes=56 * 1024 * 1024
        ),
        cost_estimate=pl.CostEstimate(
            flops=4 * tokens * D * heads * 2 * rows,
            transcendentals=0,
            bytes_accessed=24 * 1024 * 1024,
        ),
        name="attn_backward",
    )(meta, normed, low, weights, weights, qkv_kept, attended)


def by_narrow(blocks, flag_refs):
    table = [None] * 8
    for place, distance in enumerate((0, 2, 1, 3)):
        for j in range(2):
            table[distance * 2 + j] = blocks[j * 4 + place]
    for number, flag in enumerate(flag_refs):
        bit = 1 << number
        table = [jnp.where(flag == 0, table[i], table[i ^ bit]) for i in range(8)]
    return table


def by_slot(blocks, flag_refs):
    table = list(blocks)
    for number, flag in enumerate(flag_refs):
        bit = 1 << number
        table = [jnp.where(flag == 0, table[i], table[i ^ bit]) for i in range(8)]
    return [table[distance * 2 + j] for j in range(2) for distance in (0, 2, 1, 3)]


def take_kernel(flags_ref, *refs):
    blocks, (mine_ref, give_ref, cot_ref) = refs[:4], refs[4:]
    width = blocks[0].shape[1] // 6
    rows = blocks[0].shape[0]
    first = flags_ref[3] == 0
    for ref in (mine_ref, give_ref, cot_ref):
        ref[rows - 2 :] = jnp.zeros((ref.shape[0] - rows + 2, ref.shape[1]), ref.dtype)
    cots = []
    for j in range(2):
        for place in range(4):
            slot = j * 4 + place
            columns = slice(slot * width, (slot + 1) * width)
            one, two, three = [
                blocks[place][:, (3 * j + kind) * width : (3 * j + kind + 1) * width]
                for kind in range(3)
            ]
            mine_ref[:rows, columns] = jnp.where(first, one, two)
            give_ref[:rows, columns] = jnp.where(first, two, one)
            cots.append(three)
    for number, piece in enumerate(by_narrow(cots, [flags_ref[i] for i in range(3)])):
        cot_ref[:rows, number * width : (number + 1) * width] = piece


def take_tokens(flags, blocks):
    out = jax.ShapeDtypeStruct((PAD, D), jnp.bfloat16)
    full = pl.BlockSpec(memory_space=pltpu.VMEM)
    return pl.pallas_call(
        take_kernel,
        out_shape=[out] * 3,
        in_specs=[pl.BlockSpec(memory_space=pltpu.SMEM)] + [full] * 4,
        out_specs=[full] * 3,
        compiler_params=pltpu.CompilerParams(vmem_limit_bytes=24 * 1024 * 1024),
        cost_estimate=pl.CostEstimate(flops=0, transcendentals=0, bytes_accessed=4 * 1024 * 1024),
        name="take_tokens",
    )(flags, *blocks)


def give_kernel(flags_ref, kept_ref, other_ref, block_ref, near_ref, far_ref):
    rows = near_ref.shape[1]
    width = near_ref.shape[2] // 3
    first = flags_ref[3] == 0
    parts = [block_ref[:rows, n * width : (n + 1) * width] for n in range(8)]
    parts = by_slot(parts, [flags_ref[i] for i in range(3)])
    for slot in range(8):
        columns = slice(slot * width, (slot + 1) * width)
        kept = kept_ref[:rows, columns]
        other = other_ref[:rows, columns]
        target = (near_ref, far_ref)[slot // 4]
        target[slot % 4, :, :width] = jnp.where(first, kept, other)
        target[slot % 4, :, width : 2 * width] = jnp.where(first, other, kept)
        target[slot % 4, :, 2 * width :] = parts[slot]


def give_tokens(flags, kept, other, block):
    out = jax.ShapeDtypeStruct((4, SEQ, 3 * (D // 8)), jnp.bfloat16)
    full = pl.BlockSpec(memory_space=pltpu.VMEM)
    return pl.pallas_call(
        give_kernel,
        out_shape=[out] * 2,
        in_specs=[pl.BlockSpec(memory_space=pltpu.SMEM)] + [full] * 3,
        out_specs=[full] * 2,
        compiler_params=pltpu.CompilerParams(vmem_limit_bytes=24 * 1024 * 1024),
        cost_estimate=pl.CostEstimate(flops=0, transcendentals=0, bytes_accessed=4 * 1024 * 1024),
        name="give_tokens",
    )(flags, kept, other, block)


def join_kernel(near_ref, far_ref, *out_refs):
    width = near_ref.shape[2]
    for place, ref in enumerate(out_refs):
        ref[:, :width] = near_ref[place]
        ref[:, width:] = far_ref[place]


def join_lanes(near, far):
    count, rows, width = near.shape
    full = pl.BlockSpec(memory_space=pltpu.VMEM)
    return pl.pallas_call(
        join_kernel,
        out_shape=[jax.ShapeDtypeStruct((rows, 2 * width), near.dtype)] * count,
        in_specs=[full] * 2,
        out_specs=[full] * count,
        compiler_params=pltpu.CompilerParams(vmem_limit_bytes=24 * 1024 * 1024),
        cost_estimate=pl.CostEstimate(flops=0, transcendentals=0, bytes_accessed=4 * 1024 * 1024),
        name="join_lanes",
    )(near, far)
def pack_kernel(flags_ref, stream_ref, skip_ref, cot_ref, near_ref, give_ref):
    rows = near_ref.shape[1]
    pieces = []
    for number in range(8):
        at = slice(number * rows, (number + 1) * rows)
        piece = jnp.concatenate([stream_ref[:, at], skip_ref[:, at], cot_ref[:, at]], axis=0)
        pieces.append(piece.T)
    pieces = by_slot(pieces, [flags_ref[i] for i in range(3)])
    for place in range(4):
        near_ref[place] = pieces[place]
        give_ref[place] = pieces[4 + place]


def pack_tokens(flags, stream, skip_in, cotangent):
    out = jax.ShapeDtypeStruct((4, SEQ, 3 * stream.shape[0]), stream.dtype)
    full = pl.BlockSpec(memory_space=pltpu.VMEM)
    return pl.pallas_call(
        pack_kernel,
        out_shape=[out] * 2,
        in_specs=[pl.BlockSpec(memory_space=pltpu.SMEM)] + [full] * 3,
        out_specs=[full] * 2,
        compiler_params=pltpu.CompilerParams(vmem_limit_bytes=24 * 1024 * 1024),
        cost_estimate=pl.CostEstimate(flops=0, transcendentals=0, bytes_accessed=4 * 1024 * 1024),
        name="pack_tokens",
    )(flags, stream, skip_in, cotangent)


def back_kernel(flags_ref, *refs):
    blocks, (stream_ref, skip_ref, block_ref) = refs[:4], refs[4:]
    width = stream_ref.shape[0]
    rows = blocks[0].shape[0]
    pieces = [
        blocks[place][:, 3 * j * width : 3 * (j + 1) * width] for j in range(2) for place in range(4)
    ]
    for number, piece in enumerate(by_narrow(pieces, [flags_ref[i] for i in range(3)])):
        at = slice(number * rows, (number + 1) * rows)
        turned = piece.T
        stream_ref[:, at] = turned[:width].astype(jnp.float32)
        skip_ref[:, at] = turned[width : 2 * width].astype(jnp.float32)
        block_ref[:, at] = turned[2 * width :]


def back_tokens(flags, blocks):
    rows, width = blocks[0].shape
    shape = (width // 6, 8 * rows)
    full = pl.BlockSpec(memory_space=pltpu.VMEM)
    return pl.pallas_call(
        back_kernel,
        out_shape=[
            jax.ShapeDtypeStruct(shape, jnp.float32),
            jax.ShapeDtypeStruct(shape, jnp.float32),
            jax.ShapeDtypeStruct(shape, jnp.bfloat16),
        ],
        in_specs=[pl.BlockSpec(memory_space=pltpu.SMEM)] + [full] * 4,
        out_specs=[full] * 3,
        compiler_params=pltpu.CompilerParams(vmem_limit_bytes=24 * 1024 * 1024),
        cost_estimate=pl.CostEstimate(flops=0, transcendentals=0, bytes_accessed=8 * 1024 * 1024),
        name="back_tokens",
    )(flags, *blocks)


def chips(
    stream,
    skip_in,
    cotangent,
    skip_weight,
    qkv_weight,
    out_weight,
    up_weight,
    down_weight,
    norm_gain,
    norm_bias,
    row_skip,
    col_skip,
    row_qkv,
    col_qkv,
    row_out,
    col_out,
    row_up,
    col_up,
    row_down,
    col_down,
    second_gain,
    second_bias,
):
    bf16 = jnp.bfloat16
    f32 = jnp.float32
    axes = ("wide", "narrow")
    wide_count = lax.axis_size("wide")
    narrow_count = lax.axis_size("narrow")
    ZS, YS = narrow_count // 2, 2
    wide_index = lax.axis_index("wide")
    narrow_index = lax.axis_index("narrow")
    xi = wide_index // 2
    ci = wide_index % 2
    zi = narrow_index // 2
    yi = narrow_index % 2
    rows_local, feat = stream.shape
    half_head = feat // 2
    hidden = up_weight.shape[1]
    quarter = hidden // 4
    scale_factor = 1.0 / math.sqrt(HEAD)

    def perm(move):
        pairs = []
        for wide in range(wide_count):
            for narrow in range(narrow_count):
                x, c, z, y = move(wide // 2, wide % 2, narrow // 2, narrow % 2)
                target = (x * 2 + c) * narrow_count + z * 2 + y
                pairs.append((wide * narrow_count + narrow, target))
        return pairs

    def send(value, move):
        return lax.ppermute(value, axes, perm(move))

    def core(value):
        return send(value, lambda x, c, z, y: (x, 1 - c, z, y))

    def over_x(value):
        return send(value, lambda x, c, z, y: (1 - x, c, z, y))

    def over_y(value):
        return send(value, lambda x, c, z, y: (x, c, z, 1 - y))

    def xor_z(value, bit):
        return send(value, lambda x, c, z, y: (x, c, z ^ bit, y))

    def tie(*values):
        return lax.optimization_barrier(values)

    def tie(*values):
        return lax.optimization_barrier(values)

    def add_low(left, right):
        return (left.astype(f32) + right.astype(f32)).astype(bf16)

    def padded(own):
        return jnp.pad(own, ((0, PAD - SEQ), (0, 0)))

    distances = [0]
    bit = ZS // 2
    while bit:
        distances += [distance ^ bit for distance in distances]
        bit //= 2

    def gather_z(block):
        line = block[None]
        bit = ZS // 2
        while bit:
            line = jnp.concatenate([line, xor_z(line, bit)])
            bit //= 2
        return line

    order = jnp.stack(
        [(zi ^ distance) * 2 + (yi ^ j) for j in range(2) for distance in distances]
    ).astype(jnp.int32)

    def canonical(blocks):
        def exchange(table, flag, bit, width):
            return [
                jnp.where(flag == 0, table[index], table[index ^ bit]) for index in range(width)
            ]

        table = [None] * narrow_count
        for place, distance in enumerate(distances):
            for j in range(2):
                table[distance * 2 + j] = blocks[j * ZS + place]
        bit = 1
        while bit < narrow_count:
            table = exchange(table, (narrow_index // bit) % 2, bit, narrow_count)
            bit *= 2
        return table

    def split_y(array):
        grid = array.reshape((ZS, YS) + array.shape[1:])
        return pick(grid, yi, 1), pick(grid, 1 - yi, 1)

    def z_pieces(near, far):
        return [
            jnp.concatenate([pick(near, zi ^ distance, 0), pick(far, zi ^ distance, 0)], axis=-1)
            for distance in distances
        ]

    def z_line(pieces):
        return [pieces[0]] + [
            xor_z(piece, distance) for piece, distance in zip(pieces[1:], distances[1:])
        ]

    def halves_z(total):
        return total[: ZS // 2], total[ZS // 2 :]

    half = ZS // 2
    meta = xi.astype(jnp.int32)[None]
    is_first = ci == 0

    def in_order(pair, other_core):
        four = jnp.stack([pair, other_core])
        return jnp.stack(
            [pick(pick(four, c ^ ci, 0), x ^ xi, 0) for c in range(2) for x in range(2)]
        )

    def all_narrow(value):
        value = value + over_y(value)
        bit = 1
        while bit < ZS:
            value = value + xor_z(value, bit)
            bit *= 2
        return value

    def columns(array):
        size = D // wide_count
        return lax.dynamic_slice_in_dim(array, wide_index * size, size, array.ndim - 1).astype(f32)

    def statistics(grad, old):
        grad = grad.astype(f32)
        squares = grad * grad + EPS_SQUARE
        new = DECAY * old + (1.0 - DECAY) * (jnp.sum(squares, axis=1) / D)
        return new, jnp.sum(squares, axis=0), jnp.sum(grad * grad * (1.0 / new)[:, None], axis=0)

    def step_of(grad, new, scale):
        return grad.astype(f32) * lax.rsqrt(new)[:, None] * scale[None, :]

    old_wide = jnp.stack([col_skip, row_qkv, col_out, row_up, col_down])
    lane = lax.broadcasted_iota(jnp.int32, (1, D), 1)
    old_sums = (
        jnp.where(lane == 0, jnp.sum(row_skip), 0.0)
        + jnp.where(lane == 2, jnp.sum(row_out), 0.0)
        + jnp.where(lane == 4, jnp.sum(row_down), 0.0)
    )
    rows_all = jnp.array([[2 * D], [3 * D], [D], [FF], [FF]], f32)
    along_wide = jnp.array([[False], [True], [False], [True], [False]])

    flags = jnp.stack([yi, zi % 2, zi // 2, ci]).astype(jnp.int32)
    token_near, token_give = pack_tokens(flags, stream.T, skip_in.T, cotangent.T)
    skip_block = pick(pick(skip_weight, ci, 0).reshape(2, feat // 2, D), xi, 0)
    attn_rows = jnp.concatenate(
        [
            pick(qkv_weight.transpose(1, 2, 0).reshape(3, 2, half_head, D), ci, 1),
            pick(out_weight.reshape(2, half_head, D), ci, 0)[None],
        ]
    ).reshape(2, 2 * half_head, D)
    attn_block = pick(attn_rows, xi, 0)
    skip_block, attn_block, token_give = tie(skip_block, attn_block, token_give)
    token_far = over_y(token_give)
    skip_two = xor_z(skip_block, 2)
    attn_two = xor_z(attn_block, 2)
    skip_line = jnp.stack([skip_block, skip_two])
    attn_line = jnp.stack([attn_block, attn_two])
    skip_line = jnp.concatenate([skip_line, xor_z(skip_line, 1)])
    attn_line = jnp.concatenate([attn_line, xor_z(attn_line, 1)])

    token_far, up_weight, down_weight = tie(token_far, up_weight, down_weight)
    token_blocks = z_line(join_lanes(token_near, token_far))
    skip_beside = over_y(skip_line)
    skip_across = over_x(skip_line)
    ffn_block = jnp.stack(
        [
            lax.dynamic_slice_in_dim(up_weight, (ci * 2 + xi) * quarter, quarter, 1).T,
            lax.dynamic_slice_in_dim(down_weight, (ci * 2 + xi) * quarter, quarter, 0),
        ]
    )

    skip_beside, skip_across, attn_line = tie(skip_beside, skip_across, attn_line)
    skip_corner = jnp.concatenate([over_x(skip_beside[:half]), over_y(skip_across[half:])])
    attn_beside = over_y(attn_line)
    attn_across = over_x(attn_line)

    ffn_full = lax.all_gather(ffn_block[None], "narrow", tiled=True)
    mine, give, cot_pad = take_tokens(flags, token_blocks)
    flat = jnp.concatenate([mine, core(give)])
    cot_own = cot_pad[:SEQ]
    attn_corner_x = over_x(attn_beside[:half])
    attn_corner_y = over_y(attn_across[half:])
    skip_near = jnp.concatenate([skip_line, skip_beside])
    skip_away = jnp.concatenate([skip_across, skip_corner])
    skip_mat = jnp.where(
        xi == 0,
        jnp.stack([skip_near, skip_away], axis=1),
        jnp.stack([skip_away, skip_near], axis=1),
    ).reshape(D, D)

    def both_images(own):
        own = padded(own)
        return jnp.concatenate([own, core(own)])

    def core_sum(kept, given):
        return (kept + core(given))[:SEQ]

    skip_part = matmul(flat, skip_mat, "rc,cd->rd")
    hidden_in = core_sum(skip_part[:PAD], skip_part[PAD:])
    unit_one, inverse_one = unit_parts(hidden_in)
    normed = both_images((unit_one * norm_gain[0] + norm_bias[0]).astype(bf16))

    attn_corner = jnp.concatenate([attn_corner_x, attn_corner_y])
    normed, cot_pad, attn_corner = tie(normed, cot_pad, attn_corner)
    cot_pair = jnp.concatenate([cot_pad, over_x(cot_pad)])
    attn_full = jnp.stack(
        [
            jnp.concatenate([attn_line, attn_beside]),
            jnp.concatenate([attn_across, attn_corner]),
        ]
    )
    attn_a, attn_b, qkv_kept, attended = attn_forward(meta, normed, attn_full)
    attn_b, cot_pair = tie(attn_b, cot_pair)
    middle = hidden_in + core_sum(attn_a, attn_b)
    unit_two, inverse_two = unit_parts(middle)
    mixed_own = padded((unit_two * norm_gain[1] + norm_bias[1]).astype(bf16))
    mixed_pair = jnp.concatenate([mixed_own, over_x(mixed_own)])
    mixed = jnp.concatenate([mixed_pair, core(mixed_pair)])
    cot = jnp.concatenate([cot_pair, core(cot_pair)])

    mixed_a, mixed_b, act, act_grad = ffn_first(order, mixed, cot, ffn_full)
    mixed_sum = mixed_a + core(mixed_b)
    mixed_far = over_x(mixed_sum[PAD:].astype(bf16))
    mixed_sum, act = tie(mixed_sum, act)
    down_a, down_b, up_near, up_give, down_near, down_give = ffn_second(
        order, mixed, cot, act, act_grad, ffn_full
    )
    ffn_far_up = over_y(up_give)
    ffn_down_one = xor_z(down_give, 1)

    mixed_far, down_b = tie(mixed_far, down_b)
    down_sum = down_a + core(down_b)
    down_far = over_x(down_sum[PAD:].astype(bf16))
    back_middle, gain_two, bias_two = norm_back_own(
        unit_two,
        inverse_two,
        (mixed_sum[:PAD] + mixed_far.astype(f32))[:SEQ],
        norm_gain[1],
    )
    grad_middle = cot_own.astype(f32) + back_middle
    middle_low = both_images(grad_middle.astype(bf16))
    normed_a, normed_b, own, other_near, other_x, other_y = attn_backward(
        meta, normed, middle_low, attn_full, qkv_kept, attended
    )

    normed_b, ffn_far_up, ffn_down_one, down_far, other_x, other_y = tie(
        normed_b, ffn_far_up, ffn_down_one, down_far, other_x, other_y
    )
    attn_from_x = over_x(other_x)
    attn_from_y = over_y(other_y)
    ffn_down = add_low(down_near, ffn_down_one)
    ffn_down_far = over_y(ffn_down[1])
    ffn_up, ffn_up_give = halves_z(add_low(up_near, ffn_far_up))
    ffn_up_one = xor_z(ffn_up_give, 1)
    block_own = (middle + (down_sum[:PAD] + down_far.astype(f32))[:SEQ]).astype(bf16)
    back_hidden, gain_one, bias_one = norm_back_own(
        unit_one, inverse_one, core_sum(normed_a, normed_b), norm_gain[0]
    )
    hidden_low = both_images((grad_middle + back_hidden).astype(bf16))
    hidden_low, attn_from_x, attn_from_y = tie(hidden_low, attn_from_x, attn_from_y)
    token_grad = matmul(hidden_low, skip_mat, "rd,cd->rc").astype(bf16)
    back_near, back_give = give_tokens(
        flags, token_grad[:PAD], core(token_grad[PAD:]), padded(block_own)
    )
    grad_skip = matmul(flat, hidden_low, "rc,rd->cd").astype(bf16)
    grad_skip = grad_skip.reshape(narrow_count, 2, feat // 2, D)
    skip_own, skip_other = pick(grad_skip, xi, 1), pick(grad_skip, 1 - xi, 1)

    attn_from_x, attn_from_y, ffn_down_far, ffn_up_one, back_give, skip_own, skip_other = tie(
        attn_from_x, attn_from_y, ffn_down_far, ffn_up_one, back_give, skip_own, skip_other
    )
    back_far = over_y(back_give)
    skip_from_x = over_x(skip_other[ZS : ZS + half])
    skip_from_y = over_y(skip_other[ZS + half :])
    attn_across = over_x(
        jnp.concatenate([other_near[:half], add_low(other_near[half:], attn_from_y)])
    )
    attn_far = jnp.concatenate([add_low(own[ZS : ZS + half], attn_from_x), own[ZS + half :]])
    ffn_both = jnp.stack([add_low(ffn_up, ffn_up_one), add_low(ffn_down[0], ffn_down_far)])
    ffn_two = xor_z(ffn_both[:, 1], 2)

    back_far, skip_from_x, skip_from_y, attn_across, ffn_two, attn_far = tie(
        back_far, skip_from_x, skip_from_y, attn_across, ffn_two, attn_far
    )
    attn_beside = over_y(attn_far)
    back_blocks = z_line(join_lanes(back_near, back_far))
    ffn_own = add_low(ffn_both[:, 0], ffn_two)
    ffn_x = over_x(ffn_own)
    skip_give_x = jnp.concatenate([skip_other[:half], add_low(skip_other[half:ZS], skip_from_y)])
    skip_give_y = jnp.concatenate(
        [add_low(skip_own[ZS : ZS + half], skip_from_x), skip_own[ZS + half :]]
    )

    attn_beside, back_blocks, ffn_x, skip_give_x, skip_give_y = tie(
        attn_beside, back_blocks, ffn_x, skip_give_x, skip_give_y
    )
    attn_total, attn_give = halves_z(
        (own[:ZS].astype(f32) + attn_beside.astype(f32) + attn_across.astype(f32)).astype(bf16)
    )
    attn_one = xor_z(attn_give, 1)
    skip_across = over_x(skip_give_x)
    skip_beside = over_y(skip_give_y)
    ffn_pair = jnp.stack([ffn_own, ffn_x])
    ffn_core = core(ffn_pair)
    back_out = back_tokens(flags, back_blocks)
    (ffn_all,) = tie(in_order(ffn_pair, ffn_core))
    grad_up_rows = ffn_all[:, 0].reshape(hidden, D)
    grad_down = ffn_all[:, 1].reshape(hidden, D)
    new_col_up, *up_sums = statistics(grad_up_rows, col_up)
    new_row_down, *down_sums = statistics(grad_down, row_down)
    ffn_sums = list(up_sums) + list(down_sums)

    attn_one, skip_across, skip_beside, ffn_sums, back_out = tie(
        attn_one, skip_across, skip_beside, ffn_sums, back_out
    )
    attn_total = add_low(attn_total, attn_one)
    attn_two = xor_z(attn_total[1], 2)
    skip_total, skip_give = halves_z(
        (skip_own[:ZS].astype(f32) + skip_beside.astype(f32) + skip_across.astype(f32)).astype(
            bf16
        )
    )
    skip_one = xor_z(skip_give, 1)
    grad_stream, grad_skip_in, block_out = [part.T for part in back_out]

    attn_two, skip_one = tie(attn_two, skip_one)
    attn_own = add_low(attn_total[0], attn_two)
    attn_x = over_x(attn_own)
    skip_total = add_low(skip_total, skip_one)
    skip_two = xor_z(skip_total[1], 2)
    grad_up_out = columns(grad_up_rows).T
    grad_down_out = columns(grad_down)

    attn_x, skip_two, grad_up_out, grad_down_out = tie(
        attn_x, skip_two, grad_up_out, grad_down_out
    )
    skip_last = add_low(skip_total[0], skip_two)
    skip_x = over_x(skip_last)
    attn_pair = jnp.stack([attn_own, attn_x])
    (attn_all,) = tie(in_order(attn_pair, core(attn_pair)))
    attn_all = attn_all.reshape(2, 4, half_head, D)
    grad_qkv_rows = attn_all[:, :3].transpose(1, 0, 2, 3).reshape(3 * feat, D)
    grad_out = attn_all[:, 3].reshape(feat, D)
    new_col_qkv, *qkv_sums = statistics(grad_qkv_rows, col_qkv.reshape(-1))
    new_row_out, *out_sums = statistics(grad_out, row_out)

    skip_x, *sums = tie(skip_x, *qkv_sums, *out_sums)
    skip_pair = jnp.stack([skip_last, skip_x])
    (skip_all,) = tie(in_order(skip_pair, core(skip_pair)))
    grad_skip_rows = skip_all.reshape(2 * feat, D)

    norm_sums = jnp.stack([gain_one, gain_two, bias_one, bias_two])
    norm_sums = norm_sums + core(norm_sums)
    norm_sums = norm_sums + over_x(norm_sums)
    new_row_skip, *skip_sums = statistics(grad_skip_rows, row_skip.reshape(-1))
    sums = list(skip_sums) + sums + list(ffn_sums)
    totals = all_narrow(
        jnp.concatenate([jnp.stack(sums[0::2] + sums[1::2]), norm_sums, old_sums])
    )
    gain_total = totals[10:12]
    bias_total = totals[12:14]
    wide_mean = totals[:5] / rows_all
    new_wide = DECAY * old_wide + (1.0 - DECAY) * wide_mean
    row_mean = jnp.where(
        along_wide,
        jnp.mean(new_wide, axis=1, keepdims=True),
        DECAY * (totals[14, :5].reshape(5, 1) / rows_all)
        + (1.0 - DECAY) * jnp.mean(wide_mean, axis=1, keepdims=True),
    )
    square_total = jnp.sum(totals[5:10] / new_wide, axis=1, keepdims=True) * row_mean
    ratios = jnp.sqrt(square_total / (rows_all * D)) / CLIP_LEVEL
    scales = lax.rsqrt(new_wide) * (-(STEP_RATE * jnp.sqrt(row_mean) / jnp.maximum(1.0, ratios)))
    new_col_skip, new_row_qkv, new_col_out, new_row_up, new_col_down = new_wide
    clip_ratio = ratios[:, 0]
    step_skip = step_of(grad_skip_rows, new_row_skip, scales[0])
    step_qkv = step_of(grad_qkv_rows, new_col_qkv, scales[1])
    step_out = step_of(grad_out, new_row_out, scales[2])
    step_up = step_of(grad_up_rows, new_col_up, scales[3])
    step_down = step_of(grad_down, new_row_down, scales[4])
    new_up = up_weight.astype(f32) + step_up.T
    new_down = down_weight.astype(f32) + step_down
    new_skip = skip_weight.astype(f32) + step_skip.reshape(2, feat, D)
    new_qkv = qkv_weight.astype(f32) + step_qkv.reshape(3, feat, D).transpose(2, 0, 1)
    new_second_gain, gain_step = plain_update(gain_total, second_gain)
    new_second_bias, bias_step = plain_update(bias_total, second_bias)
    return (
        block_out,
        grad_stream,
        grad_skip_in,
        columns(grad_skip_rows).reshape(2, feat, -1),
        columns(grad_qkv_rows).reshape(3, feat, -1).transpose(2, 0, 1),
        columns(grad_out),
        grad_up_out,
        grad_down_out,
        gain_total,
        bias_total,
        new_row_skip.reshape(2, feat),
        new_col_skip,
        new_row_qkv,
        new_col_qkv.reshape(3, feat),
        new_row_out,
        new_col_out,
        new_row_up,
        new_col_up,
        new_row_down,
        new_col_down,
        new_second_gain,
        new_second_bias[0],
        new_second_bias[1],
        new_skip,
        new_qkv,
        step_out,
        new_up,
        new_down,
        gain_step,
        bias_step,
        clip_ratio,
    )


def solution(mesh):
    wide, narrow = mesh.shape["wide"], mesh.shape["narrow"]
    body = chips if (wide == 4 and narrow == 8) else local
    in_specs = (
        P("wide", "narrow"),
        P("wide", "narrow"),
        P("wide", "narrow"),
        P(None, "narrow", None),
        P(None, None, "narrow"),
        P("narrow", None),
        P(None, "narrow"),
        P("narrow", None),
        P(),
        P(),
        P(None, "narrow"),
        P(),
        P(),
        P(None, "narrow"),
        P("narrow"),
        P(),
        P(),
        P("narrow"),
        P("narrow"),
        P(),
        P(),
        P(),
    )
    out_specs = (
        P("wide", "narrow"),
        P("wide", "narrow"),
        P("wide", "narrow"),
        P(None, "narrow", "wide"),
        P("wide", None, "narrow"),
        P("narrow", "wide"),
        P("wide", "narrow"),
        P("narrow", "wide"),
        P(),
        P(),
        P(None, "narrow"),
        P(),
        P(),
        P(None, "narrow"),
        P("narrow"),
        P(),
        P(),
        P("narrow"),
        P("narrow"),
        P(),
        P(),
        P(),
        P(),
        P(None, "narrow", None),
        P(None, None, "narrow"),
        P("narrow", None),
        P(None, "narrow"),
        P("narrow", None),
        P(),
        P(),
        P(),
    )
    return jax.shard_map(body, mesh=mesh, in_specs=in_specs, out_specs=out_specs, check_vma=False)
```

```python
import math

import jax
import jax.numpy as jnp
from jax import lax
from jax.experimental import pallas as pl
from jax.experimental.pallas import tpu as pltpu
from jax.sharding import PartitionSpec as P

D = 1152
FF = 4608
SEQ = 258
HEAD = 72


NORM_EPS = 1e-05
EPS_SQUARE = 1e-30
DECAY = 0.5
STEP_RATE = 0.05
CLIP_LEVEL = 0.25


def layer_norm(values, gain, shift):
    average = jnp.mean(values, axis=-1, keepdims=True)
    centered = values - average
    variance = jnp.mean(centered * centered, axis=-1, keepdims=True)
    return centered * lax.rsqrt(variance + NORM_EPS) * gain + shift


def norm_back(values, grad, gain, own_rows):
    average = jnp.mean(values, axis=-1, keepdims=True)
    centered = values - average
    variance = jnp.mean(centered * centered, axis=-1, keepdims=True)
    inverse = lax.rsqrt(variance + NORM_EPS)
    unit = centered * inverse
    scaled = grad * gain
    inner = (
        scaled
        - jnp.mean(scaled, axis=-1, keepdims=True)
        - unit * jnp.mean(scaled * unit, axis=-1, keepdims=True)
    )
    weighted = grad * own_rows
    return (inner * inverse, jnp.sum(weighted * unit, axis=0), jnp.sum(weighted, axis=0))


def gelu_exact(inputs):
    return jax.nn.gelu(inputs, approximate=False)


def matmul(left, right, form):
    return jnp.einsum(form, left, right, preferred_element_type=jnp.float32)


def plain_update(grad, second_old):
    second_new = DECAY * second_old + (1.0 - DECAY) * (grad * grad + EPS_SQUARE)
    update = grad * lax.rsqrt(second_new)
    spread = jnp.sqrt(jnp.mean(update * update))
    update = update / jnp.maximum(1.0, spread / CLIP_LEVEL)
    return (second_new, -(STEP_RATE * update))


def wide_slice(array, dim_index, count, wide_index):
    piece_size = array.shape[dim_index] // count
    return lax.dynamic_slice_in_dim(array, wide_index * piece_size, piece_size, dim_index)


def local(
    stream,
    skip_in,
    cotangent,
    skip_weight,
    qkv_weight,
    out_weight,
    up_weight,
    down_weight,
    norm_gain,
    norm_bias,
    row_skip,
    col_skip,
    row_qkv,
    col_qkv,
    row_out,
    col_out,
    row_up,
    col_up,
    row_down,
    col_down,
    second_gain,
    second_bias,
):
    rows_local, feat_local = stream.shape
    images = rows_local // SEQ
    heads_local = feat_local // HEAD
    scale_factor = 1.0 / math.sqrt(HEAD)
    split_shape = (images, SEQ, heads_local, HEAD)
    narrow_count = lax.axis_size("narrow")
    narrow_index = lax.axis_index("narrow")
    share_rows = -(-rows_local // narrow_count)
    row_start = narrow_index * share_rows
    row_ids = lax.broadcasted_iota(jnp.int32, (rows_local, 1), 0)
    own_mask = ((row_ids >= row_start) & (row_ids < row_start + share_rows)).astype(jnp.float32)

    def full_sum(values):
        return lax.psum(values, "narrow")

    partial_in = matmul(stream, skip_weight[0], "rc,cd->rd") + matmul(
        skip_in, skip_weight[1], "rc,cd->rd"
    )
    hidden_in = full_sum(partial_in)
    normed = layer_norm(hidden_in, norm_gain[0], norm_bias[0]).astype(jnp.bfloat16)
    projected = matmul(normed, qkv_weight, "rd,dtc->rtc").astype(jnp.bfloat16)
    queries = projected[:, 0].reshape(split_shape)
    key_vectors = projected[:, 1].reshape(split_shape)
    value_vectors = projected[:, 2].reshape(split_shape)
    scores = matmul(queries, key_vectors, "bqhe,bkhe->bhqk") * scale_factor
    row_max = jnp.max(scores, axis=-1, keepdims=True)
    exponent = jnp.exp(scores - row_max)
    row_total = jnp.sum(exponent, axis=-1, keepdims=True)
    log_total = row_max + jnp.log(row_total)
    probs_low = (exponent / row_total).astype(jnp.bfloat16)
    attended = (
        matmul(probs_low, value_vectors, "bhqk,bkhe->bqhe")
        .reshape(rows_local, feat_local)
        .astype(jnp.bfloat16)
    )
    attn_part = matmul(attended, out_weight, "rc,cd->rd")
    middle = hidden_in + full_sum(attn_part)
    mixed_in = layer_norm(middle, norm_gain[1], norm_bias[1]).astype(jnp.bfloat16)
    middle_own = lax.dynamic_slice_in_dim(middle, narrow_index * feat_local, feat_local, 1)
    up_input = matmul(mixed_in, up_weight, "rd,df->rf")
    activation = gelu_exact(up_input).astype(jnp.bfloat16)
    down_part = matmul(activation, down_weight, "rf,fd->rd")
    block_out = (
        middle_own + lax.psum_scatter(down_part, "narrow", scatter_dimension=1, tiled=True)
    ).astype(jnp.bfloat16)
    grad_full = lax.all_gather(cotangent, "narrow", axis=1, tiled=True)
    grad_down = matmul(activation, grad_full, "rf,rd->fd")
    grad_act = matmul(grad_full, down_weight, "rd,fd->rf")
    gelu_value, gelu_back = jax.vjp(gelu_exact, up_input)
    grad_up_in = gelu_back(grad_act)[0].astype(jnp.bfloat16)
    grad_up = matmul(mixed_in, grad_up_in, "rd,rf->df")
    mixed_part = matmul(grad_up_in, up_weight, "rf,df->rd")
    grad_mixed = full_sum(mixed_part)
    back_middle, back_gain_two, back_bias_two = norm_back(
        middle, grad_mixed, norm_gain[1], own_mask
    )
    grad_middle = grad_full.astype(jnp.float32) + back_middle
    middle_low = grad_middle.astype(jnp.bfloat16)
    grad_out = matmul(attended, middle_low, "rc,rd->cd")
    grad_attended = (
        matmul(middle_low, out_weight, "rd,cd->rc").astype(jnp.bfloat16).reshape(split_shape)
    )
    scores_again = matmul(queries, key_vectors, "bqhe,bkhe->bhqk") * scale_factor
    probs = jnp.exp(scores_again - log_total)
    probs_again = probs.astype(jnp.bfloat16)
    grad_values = matmul(probs_again, grad_attended, "bhqk,bqhe->bkhe")
    grad_probs = matmul(grad_attended, value_vectors, "bqhe,bkhe->bhqk")
    inner_sum = jnp.sum(probs * grad_probs, axis=-1, keepdims=True)
    grad_scores = (probs * (grad_probs - inner_sum) * scale_factor).astype(jnp.bfloat16)
    grad_queries = matmul(grad_scores, key_vectors, "bhqk,bkhe->bqhe")
    grad_keys = matmul(grad_scores, queries, "bhqk,bqhe->bkhe")
    grad_projected = jnp.stack(
        [
            grad_queries.reshape(rows_local, feat_local),
            grad_keys.reshape(rows_local, feat_local),
            grad_values.reshape(rows_local, feat_local),
        ],
        axis=1,
    ).astype(jnp.bfloat16)
    grad_qkv = matmul(normed, grad_projected, "rd,rtc->dtc")
    normed_part = matmul(grad_projected, qkv_weight, "rtc,dtc->rd")
    grad_normed = full_sum(normed_part)
    back_hidden, back_gain_one, back_bias_one = norm_back(
        hidden_in, grad_normed, norm_gain[0], own_mask
    )
    hidden_low = (grad_middle + back_hidden).astype(jnp.bfloat16)
    grad_skip = jnp.stack(
        [matmul(stream, hidden_low, "rc,rd->cd"), matmul(skip_in, hidden_low, "rc,rd->cd")]
    )
    grad_stream = matmul(hidden_low, skip_weight[0], "rd,cd->rc")
    grad_skip_in = matmul(hidden_low, skip_weight[1], "rd,cd->rc")
    gain_grads = jnp.stack([back_gain_one, back_gain_two])
    bias_grads = jnp.stack([back_bias_one, back_bias_two])
    wide_count = lax.axis_size("wide")
    wide_index = lax.axis_index("wide")
    wide_dims = (2, 0, 1, 0, 1)
    wide_axes = ((0, 1), (1, 2), (0,), (1,), (0,))
    narrow_axes = ((2,), (0,), (1,), (0,), (1,))
    wide_counts = (2 * D, 3 * D, D, FF, FF)
    row_along_wide = (False, True, False, True, False)
    entry_counts = (2 * D * D, 3 * D * D, D * D, D * FF, FF * D)
    old_slots = (0, 0, 1, 0, 2)
    weights = (skip_weight, qkv_weight, out_weight, up_weight, down_weight)
    old_wide = (col_skip, row_qkv, col_out, row_up, col_down)
    old_narrow = (row_skip, col_qkv, row_out, col_up, row_down)
    summed = lax.psum(
        (grad_skip, grad_qkv, grad_out, grad_up, grad_down, gain_grads, bias_grads), "wide"
    )
    pieces = summed[:5]
    gain_section = summed[5]
    bias_section = summed[6]
    squares = [piece * piece + EPS_SQUARE for piece in pieces]
    wide_parts = [jnp.sum(squares[number], axis=wide_axes[number]) for number in range(5)]
    narrow_parts = [jnp.sum(squares[number], axis=narrow_axes[number]) for number in range(5)]
    old_sums = jnp.stack([jnp.sum(row_skip), jnp.sum(row_out), jnp.sum(row_down)])
    stat_total = lax.psum(
        (
            wide_parts[0],
            wide_parts[1],
            wide_parts[2],
            wide_parts[3],
            wide_parts[4],
            old_sums,
            gain_section,
            bias_section,
        ),
        "narrow",
    )
    old_row_means = (stat_total[5][0] / (2 * D), stat_total[5][1] / D, stat_total[5][2] / FF)
    wide_stats = stat_total[:5]
    gain_total = stat_total[6]
    bias_total = stat_total[7]
    new_wide = []
    new_narrow = []
    updates = []
    for number in range(5):
        wide_mean = wide_stats[number] / wide_counts[number]
        wide_new = DECAY * old_wide[number] + (1.0 - DECAY) * wide_mean
        narrow_new = DECAY * old_narrow[number] + (1.0 - DECAY) * narrow_parts[number] / D
        if row_along_wide[number]:
            row_mean = jnp.mean(wide_new)
        else:
            row_mean = DECAY * old_row_means[old_slots[number]] + (1.0 - DECAY) * jnp.mean(
                wide_mean
            )
        dim_index = wide_dims[number]
        piece_size = pieces[number].shape[dim_index]
        broadcast_shape = [1] * pieces[number].ndim
        broadcast_shape[dim_index] = piece_size
        second = (
            jnp.expand_dims(narrow_new, dim_index) * wide_new.reshape(broadcast_shape) / row_mean
        )
        updates.append(pieces[number] * lax.rsqrt(second))
        new_wide.append(wide_new)
        new_narrow.append(narrow_new)
    update_squares = jnp.stack([jnp.sum(update * update) for update in updates])
    square_totals = lax.psum(update_squares, "narrow")
    counts_array = jnp.array(entry_counts, jnp.float32)
    clip_ratio = jnp.sqrt(square_totals / counts_array) / CLIP_LEVEL
    new_pieces = []
    for number in range(5):
        spread = jnp.sqrt(square_totals[number] / entry_counts[number])
        step_piece = -(STEP_RATE * (updates[number] / jnp.maximum(1.0, spread / CLIP_LEVEL)))
        if number == 2:
            new_pieces.append(step_piece)
        else:
            weight_piece = weights[number]
            new_pieces.append(weight_piece.astype(jnp.float32) + step_piece)
    grad_outs = [
        wide_slice(pieces[number], wide_dims[number], wide_count, wide_index) for number in range(5)
    ]
    new_second_gain, gain_step = plain_update(gain_total, second_gain)
    new_second_bias, bias_step = plain_update(bias_total, second_bias)
    return (
        block_out,
        grad_stream,
        grad_skip_in,
        grad_outs[0],
        grad_outs[1],
        grad_outs[2],
        grad_outs[3],
        grad_outs[4],
        gain_total,
        bias_total,
        new_narrow[0],
        new_wide[0],
        new_wide[1],
        new_narrow[1],
        new_narrow[2],
        new_wide[2],
        new_wide[3],
        new_narrow[3],
        new_narrow[4],
        new_wide[4],
        new_second_gain,
        new_second_bias[0],
        new_second_bias[1],
        new_pieces[0],
        new_pieces[1],
        new_pieces[2],
        new_pieces[3],
        new_pieces[4],
        gain_step,
        bias_step,
        clip_ratio,
    )


def unit_parts(values):
    average = jnp.mean(values, axis=-1, keepdims=True)
    centered = values - average
    variance = jnp.mean(centered * centered, axis=-1, keepdims=True)
    inverse = lax.rsqrt(variance + NORM_EPS)
    return centered * inverse, inverse


def norm_back_own(unit, inverse, grad, gain):
    scaled = grad * gain
    inner = (
        scaled
        - jnp.mean(scaled, axis=-1, keepdims=True)
        - unit * jnp.mean(scaled * unit, axis=-1, keepdims=True)
    )
    rows = tuple(range(grad.ndim - 1))
    return inner * inverse, jnp.sum(grad * unit, axis=rows), jnp.sum(grad, axis=rows)


def pick(array, index, axis):
    return lax.dynamic_index_in_dim(array, index, axis, keepdims=False)


PAD = 272


def dot_nt(left, right):
    return lax.dot_general(left, right, (((1,), (1,)), ((), ())), preferred_element_type=jnp.float32)


def dot_nn(left, right):
    return lax.dot_general(left, right, (((1,), (0,)), ((), ())), preferred_element_type=jnp.float32)


def dot_tn(left, right):
    return lax.dot_general(left, right, (((0,), (0,)), ((), ())), preferred_element_type=jnp.float32)


def accumulate(step, refs, value):
    size = refs[0].shape[0]

    @pl.when(step == 0)
    def _():
        for number, ref in enumerate(refs):
            ref[...] = value[number * size : (number + 1) * size]

    @pl.when(step > 0)
    def _():
        for number, ref in enumerate(refs):
            ref[...] += value[number * size : (number + 1) * size]


def all_four(refs):
    return jnp.concatenate([ref[...] for ref in refs], axis=0)


def ffn_first_kernel(order_ref, *refs):
    mixed, cot, weights, parts, (act_ref, grad_ref) = (
        all_four(refs[:4]),
        all_four(refs[4:8]),
        refs[8:12],
        refs[12:16],
        refs[16:],
    )
    up = jnp.concatenate([ref[0, 0] for ref in weights], axis=0)
    down = jnp.concatenate([ref[0, 1] for ref in weights], axis=0)
    up_input = dot_nt(mixed, up)
    gate = 0.5 * (1.0 + lax.erf(up_input * (1.0 / math.sqrt(2.0))))
    act_ref[0] = (up_input * gate).astype(jnp.bfloat16)
    slope = gate + up_input * (jnp.exp(-0.5 * up_input * up_input) * (1.0 / math.sqrt(2.0 * math.pi)))
    grad = (dot_nt(cot, down) * slope).astype(jnp.bfloat16)
    grad_ref[0] = grad
    accumulate(pl.program_id(0), parts, dot_nn(grad, up))


def ffn_second_kernel(order_ref, *refs):
    mixed, cot, (act_ref, grad_ref), weights, parts, (up_near, up_far, down_near, down_far) = (
        all_four(refs[:4]),
        all_four(refs[4:8]),
        refs[8:10],
        refs[10:14],
        refs[14:18],
        refs[18:],
    )
    step = pl.program_id(0)
    down = jnp.concatenate([ref[0, 0] for ref in weights], axis=0)
    grad_up = dot_tn(grad_ref[0], mixed).astype(jnp.bfloat16)
    grad_down = dot_tn(act_ref[0], cot).astype(jnp.bfloat16)
    for j, ref in enumerate((up_near, up_far)):

        @pl.when(step == j)
        def _():
            ref[...] = grad_up.reshape(ref.shape)

    halves = grad_down.reshape((2,) + down_near.shape[1:])
    down_near[0] = halves[0]
    down_far[0] = halves[1]
    accumulate(step, parts, dot_nn(act_ref[0], down))


def ffn_specs(tokens, rows):
    image = pl.BlockSpec((tokens // 4, D), lambda t, m: (0, 0))
    units = pl.BlockSpec((1, tokens, 4 * rows), lambda t, m: (t, 0, 0))
    return image, units


def ffn_first(order, mixed, cot, weights):
    count, _, rows, _ = weights.shape
    tokens = 4 * mixed[0].shape[0]
    image, units = ffn_specs(tokens, rows)

    def weight_spec(slot):
        return pl.BlockSpec((1, 2, rows, D), lambda t, m: (m[4 * t + slot], 0, 0, 0))

    part = jax.ShapeDtypeStruct((tokens // 4, D), jnp.float32)
    hidden = jax.ShapeDtypeStruct((count // 4, tokens, 4 * rows), jnp.bfloat16)
    *parts, act, grad = pl.pallas_call(
        ffn_first_kernel,
        out_shape=[part] * 4 + [hidden] * 2,
        grid_spec=pltpu.PrefetchScalarGridSpec(
            num_scalar_prefetch=1,
            grid=(count // 4,),
            in_specs=[image] * 8 + [weight_spec(slot) for slot in range(4)],
            out_specs=[image] * 4 + [units] * 2,
        ),
        compiler_params=pltpu.CompilerParams(
            dimension_semantics=("arbitrary",), vmem_limit_bytes=56 * 1024 * 1024
        ),
        cost_estimate=pl.CostEstimate(
            flops=6 * tokens * D * count * rows, transcendentals=0, bytes_accessed=24 * 1024 * 1024
        ),
        name="ffn_first",
    )(order, *mixed, *cot, *([weights] * 4))
    return parts, act, grad


def ffn_second(order, mixed, cot, act, grad, weights):
    count, _, rows, _ = weights.shape
    tokens = 4 * mixed[0].shape[0]
    image, units = ffn_specs(tokens, rows)

    def weight_spec(slot):
        return pl.BlockSpec((1, 1, rows, D), lambda t, m: (m[4 * t + slot], 1, 0, 0))

    part = jax.ShapeDtypeStruct((tokens // 4, D), jnp.float32)
    side = jax.ShapeDtypeStruct((4, rows, D), jnp.bfloat16)
    turn = jax.ShapeDtypeStruct((2, 2, rows, D), jnp.bfloat16)
    side_block = pl.BlockSpec((4, rows, D), lambda t, m: (0, 0, 0))
    turn_block = pl.BlockSpec((1, 2, rows, D), lambda t, m: (t, 0, 0, 0))
    *outs, up_near, up_far, down_near, down_far = pl.pallas_call(
        ffn_second_kernel,
        out_shape=[part] * 4 + [side] * 2 + [turn] * 2,
        grid_spec=pltpu.PrefetchScalarGridSpec(
            num_scalar_prefetch=1,
            grid=(count // 4,),
            in_specs=[image] * 8 + [units, units] + [weight_spec(slot) for slot in range(4)],
            out_specs=[image] * 4 + [side_block] * 2 + [turn_block] * 2,
        ),
        compiler_params=pltpu.CompilerParams(
            dimension_semantics=("arbitrary",), vmem_limit_bytes=56 * 1024 * 1024
        ),
        cost_estimate=pl.CostEstimate(
            flops=6 * tokens * D * count * rows, transcendentals=0, bytes_accessed=24 * 1024 * 1024
        ),
        name="ffn_second",
    )(order, *mixed, *cot, act, grad, *([weights] * 4))
    return outs, up_near, up_far, down_near, down_far


def soft(q, k):
    scores = dot_nt(q, k) * (1.0 / math.sqrt(HEAD))
    column = lax.broadcasted_iota(jnp.int32, scores.shape, 1)
    scores = jnp.where(column < SEQ, scores, -1e30)
    exponent = jnp.exp(scores - jnp.max(scores, axis=-1, keepdims=True))
    return exponent / jnp.sum(exponent, axis=-1, keepdims=True)


GROUP = 4


def head_weights(qk_ref, vo_ref):
    qk = [qk_ref[0, head] for head in range(GROUP)]
    v = [vo_ref[0, head, :HEAD] for head in range(GROUP)]
    out = [vo_ref[0, head, HEAD:] for head in range(GROUP)]
    return jnp.concatenate(qk + v, axis=0), jnp.concatenate(out, axis=0)


def head_columns(head):
    first = 2 * HEAD * head
    value = 2 * HEAD * GROUP + HEAD * head
    return (
        slice(first, first + HEAD),
        slice(first + HEAD, first + 2 * HEAD),
        slice(value, value + HEAD),
    )


def both(first_ref, second_ref):
    return jnp.concatenate([first_ref[...], second_ref[...]], axis=0)


def attn_forward_kernel(
    meta_ref, normed_a, normed_b, qk_ref, vo_ref, part_a, part_b, qkv_ref, attended_ref
):
    step = pl.program_id(0)
    weights, out_weight = head_weights(qk_ref, vo_ref)
    qkv_ref[0] = dot_nt(both(normed_a, normed_b), weights).astype(jnp.bfloat16)
    for head in range(GROUP):
        q_at, k_at, v_at = head_columns(head)
        for image in range(2):
            rows = slice(image * PAD, (image + 1) * PAD)
            probs = soft(qkv_ref[0, rows, q_at], qkv_ref[0, rows, k_at]).astype(jnp.bfloat16)
            attended_ref[0, rows, HEAD * head : HEAD * (head + 1)] = dot_nn(
                probs, qkv_ref[0, rows, v_at]
            ).astype(jnp.bfloat16)
    accumulate(step, (part_a, part_b), dot_nn(attended_ref[0], out_weight))


def attn_specs(rows, tokens):
    whole = pl.BlockSpec((tokens, D), lambda s, m: (0, 0))
    half = pl.BlockSpec((tokens // 2, D), lambda s, m: (0, 0))
    qk = pl.BlockSpec((1, GROUP, rows, D), lambda s, m: (m[0], s, 0, 0))
    vo = pl.BlockSpec((1, GROUP, rows, D), lambda s, m: (1 - m[0], s, 0, 0))
    qkv = pl.BlockSpec((1, tokens, 3 * HEAD * GROUP), lambda s, m: (s, 0, 0))
    att = pl.BlockSpec((1, tokens, HEAD * GROUP), lambda s, m: (s, 0, 0))
    return whole, half, qk, vo, qkv, att


def attn_forward(meta, normed, weights):
    heads, rows = weights.shape[1:3]
    tokens = 2 * normed[0].shape[0]
    whole, half, qk, vo, qkv, att = attn_specs(rows, tokens)
    return pl.pallas_call(
        attn_forward_kernel,
        out_shape=[
            jax.ShapeDtypeStruct((tokens // 2, D), jnp.float32),
            jax.ShapeDtypeStruct((tokens // 2, D), jnp.float32),
            jax.ShapeDtypeStruct((heads // GROUP, tokens, 3 * HEAD * GROUP), jnp.bfloat16),
            jax.ShapeDtypeStruct((heads // GROUP, tokens, HEAD * GROUP), jnp.bfloat16),
        ],
        grid_spec=pltpu.PrefetchScalarGridSpec(
            num_scalar_prefetch=1,
            grid=(heads // GROUP,),
            in_specs=[half, half, qk, vo],
            out_specs=[half, half, qkv, att],
        ),
        compiler_params=pltpu.CompilerParams(
            dimension_semantics=("arbitrary",), vmem_limit_bytes=48 * 1024 * 1024
        ),
        cost_estimate=pl.CostEstimate(flops=0, transcendentals=0, bytes_accessed=1024 * 1024),
        name="attn_forward",
    )(meta, *normed, weights, weights)


def attn_backward_kernel(
    meta_ref,
    normed_first,
    normed_second,
    low_first,
    low_second,
    qk_ref,
    vo_ref,
    qkv_ref,
    attended_ref,
    part_a,
    part_b,
    own_ref,
    near_ref,
    far_x_ref,
    far_y_ref,
    grads_s,
    out_s,
):
    step = pl.program_id(0)
    normed = both(normed_first, normed_second)
    low = both(low_first, low_second)
    weights, out_weight = head_weights(qk_ref, vo_ref)
    out_s[...] = dot_nt(low, out_weight).astype(jnp.bfloat16)
    for head in range(GROUP):
        q_at, k_at, v_at = head_columns(head)
        for image in range(2):
            rows = slice(image * PAD, (image + 1) * PAD)
            q = qkv_ref[0, rows, q_at]
            k = qkv_ref[0, rows, k_at]
            v = qkv_ref[0, rows, v_at]
            grad = out_s[rows, HEAD * head : HEAD * (head + 1)]
            probs = soft(q, k)
            grads_s[rows, v_at] = dot_tn(probs.astype(jnp.bfloat16), grad).astype(jnp.bfloat16)
            grad_probs = dot_nt(grad, v)
            inner = jnp.sum(probs * grad_probs, axis=-1, keepdims=True)
            grad_scores = (probs * (grad_probs - inner) * (1.0 / math.sqrt(HEAD))).astype(
                jnp.bfloat16
            )
            grads_s[rows, q_at] = dot_nn(grad_scores, k).astype(jnp.bfloat16)
            grads_s[rows, k_at] = dot_tn(grad_scores, q).astype(jnp.bfloat16)
    projected = grads_s[...]
    accumulate(step, (part_a, part_b), dot_nn(projected, weights))
    mats = dot_tn(projected, normed)
    outs = dot_tn(attended_ref[0], low)
    first = meta_ref[0] == 0
    for head in range(GROUP):
        q_at, k_at, v_at = head_columns(head)
        query_key = mats[q_at.start : k_at.stop]
        value_out = jnp.concatenate([mats[v_at], outs[HEAD * head : HEAD * (head + 1)]], axis=0)
        own_ref[head] = jnp.where(first, query_key, value_out).astype(jnp.bfloat16)
        other = jnp.where(first, value_out, query_key).astype(jnp.bfloat16)

        @pl.when(step == 0)
        def _():
            near_ref[head] = other

        @pl.when(step == 1)
        def _():
            if head < 2:
                far_x_ref[head] = other
            else:
                far_y_ref[head - 2] = other


def attn_backward(meta, normed, low, weights, qkv_kept, attended):
    heads, rows = weights.shape[1:3]
    tokens = 2 * normed[0].shape[0]
    whole, half, qk, vo, qkv, att = attn_specs(rows, tokens)

    def fixed(size):
        return pl.BlockSpec((size, rows, D), lambda s, m: (0, 0, 0))

    return pl.pallas_call(
        attn_backward_kernel,
        out_shape=[
            jax.ShapeDtypeStruct((tokens // 2, D), jnp.float32),
            jax.ShapeDtypeStruct((tokens // 2, D), jnp.float32),
            jax.ShapeDtypeStruct((heads, rows, D), jnp.bfloat16),
            jax.ShapeDtypeStruct((4, rows, D), jnp.bfloat16),
            jax.ShapeDtypeStruct((2, rows, D), jnp.bfloat16),
            jax.ShapeDtypeStruct((2, rows, D), jnp.bfloat16),
        ],
        grid_spec=pltpu.PrefetchScalarGridSpec(
            num_scalar_prefetch=1,
            grid=(heads // GROUP,),
            in_specs=[half, half, half, half, qk, vo, qkv, att],
            out_specs=[
                half,
                half,
                pl.BlockSpec((GROUP, rows, D), lambda s, m: (s, 0, 0)),
                fixed(4),
                fixed(2),
                fixed(2),
            ],
            scratch_shapes=[
                pltpu.VMEM((tokens, 3 * HEAD * GROUP), jnp.bfloat16),
                pltpu.VMEM((tokens, HEAD * GROUP), jnp.bfloat16),
            ],
        ),
        compiler_params=pltpu.CompilerParams(
            dimension_semantics=("arbitrary",), vmem_limit_bytes=56 * 1024 * 1024
        ),
        cost_estimate=pl.CostEstimate(
            flops=4 * tokens * D * heads * 2 * rows,
            transcendentals=0,
            bytes_accessed=24 * 1024 * 1024,
        ),
        name="attn_backward",
    )(meta, *normed, *low, weights, weights, qkv_kept, attended)


def by_narrow(blocks, flag_refs):
    table = [None] * 8
    for place, distance in enumerate((0, 2, 1, 3)):
        for j in range(2):
            table[distance * 2 + j] = blocks[j * 4 + place]
    for number, flag in enumerate(flag_refs):
        bit = 1 << number
        table = [jnp.where(flag == 0, table[i], table[i ^ bit]) for i in range(8)]
    return table


def by_slot(blocks, flag_refs):
    table = list(blocks)
    for number, flag in enumerate(flag_refs):
        bit = 1 << number
        table = [jnp.where(flag == 0, table[i], table[i ^ bit]) for i in range(8)]
    return [table[distance * 2 + j] for j in range(2) for distance in (0, 2, 1, 3)]


def take_kernel(flags_ref, *refs):
    blocks, (mine_ref, give_ref, cot_ref) = refs[:4], refs[4:]
    width = blocks[0].shape[1] // 6
    rows = blocks[0].shape[0]
    first = flags_ref[3] == 0
    for ref in (mine_ref, give_ref, cot_ref):
        ref[rows - 2 :] = jnp.zeros((ref.shape[0] - rows + 2, ref.shape[1]), ref.dtype)
    cots = []
    for j in range(2):
        for place in range(4):
            slot = j * 4 + place
            columns = slice(slot * width, (slot + 1) * width)
            one, two, three = [
                blocks[place][:, (3 * j + kind) * width : (3 * j + kind + 1) * width]
                for kind in range(3)
            ]
            mine_ref[:rows, columns] = jnp.where(first, one, two)
            give_ref[:rows, columns] = jnp.where(first, two, one)
            cots.append(three)
    for number, piece in enumerate(by_narrow(cots, [flags_ref[i] for i in range(3)])):
        cot_ref[:rows, number * width : (number + 1) * width] = piece


def take_tokens(flags, blocks):
    out = jax.ShapeDtypeStruct((PAD, D), jnp.bfloat16)
    full = pl.BlockSpec(memory_space=pltpu.VMEM)
    return pl.pallas_call(
        take_kernel,
        out_shape=[out] * 3,
        in_specs=[pl.BlockSpec(memory_space=pltpu.SMEM)] + [full] * 4,
        out_specs=[full] * 3,
        compiler_params=pltpu.CompilerParams(vmem_limit_bytes=24 * 1024 * 1024),
        cost_estimate=pl.CostEstimate(flops=0, transcendentals=0, bytes_accessed=4 * 1024 * 1024),
        name="take_tokens",
    )(flags, *blocks)


def give_kernel(flags_ref, kept_ref, other_ref, block_ref, near_ref, far_ref):
    rows = near_ref.shape[1]
    width = near_ref.shape[2] // 3
    first = flags_ref[3] == 0
    parts = [block_ref[:rows, n * width : (n + 1) * width] for n in range(8)]
    parts = by_slot(parts, [flags_ref[i] for i in range(3)])
    for slot in range(8):
        columns = slice(slot * width, (slot + 1) * width)
        kept = kept_ref[:rows, columns]
        other = other_ref[:rows, columns]
        target = (near_ref, far_ref)[slot // 4]
        target[slot % 4, :, :width] = jnp.where(first, kept, other)
        target[slot % 4, :, width : 2 * width] = jnp.where(first, other, kept)
        target[slot % 4, :, 2 * width :] = parts[slot]


def give_tokens(flags, kept, other, block):
    out = jax.ShapeDtypeStruct((4, SEQ, 3 * (D // 8)), jnp.bfloat16)
    full = pl.BlockSpec(memory_space=pltpu.VMEM)
    return pl.pallas_call(
        give_kernel,
        out_shape=[out] * 2,
        in_specs=[pl.BlockSpec(memory_space=pltpu.SMEM)] + [full] * 3,
        out_specs=[full] * 2,
        compiler_params=pltpu.CompilerParams(vmem_limit_bytes=24 * 1024 * 1024),
        cost_estimate=pl.CostEstimate(flops=0, transcendentals=0, bytes_accessed=4 * 1024 * 1024),
        name="give_tokens",
    )(flags, kept, other, block)


def join_kernel(near_ref, far_ref, *out_refs):
    width = near_ref.shape[2]
    for place, ref in enumerate(out_refs):
        ref[:, :width] = near_ref[place]
        ref[:, width:] = far_ref[place]


def join_lanes(near, far):
    count, rows, width = near.shape
    full = pl.BlockSpec(memory_space=pltpu.VMEM)
    return pl.pallas_call(
        join_kernel,
        out_shape=[jax.ShapeDtypeStruct((rows, 2 * width), near.dtype)] * count,
        in_specs=[full] * 2,
        out_specs=[full] * count,
        compiler_params=pltpu.CompilerParams(vmem_limit_bytes=24 * 1024 * 1024),
        cost_estimate=pl.CostEstimate(flops=0, transcendentals=0, bytes_accessed=4 * 1024 * 1024),
        name="join_lanes",
    )(near, far)
def pack_kernel(flags_ref, stream_ref, skip_ref, cot_ref, near_ref, give_ref):
    rows = near_ref.shape[1]
    pieces = []
    for number in range(8):
        at = slice(number * rows, (number + 1) * rows)
        piece = jnp.concatenate([stream_ref[:, at], skip_ref[:, at], cot_ref[:, at]], axis=0)
        pieces.append(piece.T)
    pieces = by_slot(pieces, [flags_ref[i] for i in range(3)])
    for place in range(4):
        near_ref[place] = pieces[place]
        give_ref[place] = pieces[4 + place]


def pack_tokens(flags, stream, skip_in, cotangent):
    out = jax.ShapeDtypeStruct((4, SEQ, 3 * stream.shape[0]), stream.dtype)
    full = pl.BlockSpec(memory_space=pltpu.VMEM)
    return pl.pallas_call(
        pack_kernel,
        out_shape=[out] * 2,
        in_specs=[pl.BlockSpec(memory_space=pltpu.SMEM)] + [full] * 3,
        out_specs=[full] * 2,
        compiler_params=pltpu.CompilerParams(vmem_limit_bytes=24 * 1024 * 1024),
        cost_estimate=pl.CostEstimate(flops=0, transcendentals=0, bytes_accessed=4 * 1024 * 1024),
        name="pack_tokens",
    )(flags, stream, skip_in, cotangent)


def back_kernel(flags_ref, *refs):
    blocks, (stream_ref, skip_ref, block_ref) = refs[:4], refs[4:]
    width = stream_ref.shape[0]
    rows = blocks[0].shape[0]
    pieces = [
        blocks[place][:, 3 * j * width : 3 * (j + 1) * width] for j in range(2) for place in range(4)
    ]
    for number, piece in enumerate(by_narrow(pieces, [flags_ref[i] for i in range(3)])):
        at = slice(number * rows, (number + 1) * rows)
        turned = piece.T
        stream_ref[:, at] = turned[:width].astype(jnp.float32)
        skip_ref[:, at] = turned[width : 2 * width].astype(jnp.float32)
        block_ref[:, at] = turned[2 * width :]


def back_tokens(flags, blocks):
    rows, width = blocks[0].shape
    shape = (width // 6, 8 * rows)
    full = pl.BlockSpec(memory_space=pltpu.VMEM)
    return pl.pallas_call(
        back_kernel,
        out_shape=[
            jax.ShapeDtypeStruct(shape, jnp.float32),
            jax.ShapeDtypeStruct(shape, jnp.float32),
            jax.ShapeDtypeStruct(shape, jnp.bfloat16),
        ],
        in_specs=[pl.BlockSpec(memory_space=pltpu.SMEM)] + [full] * 4,
        out_specs=[full] * 3,
        compiler_params=pltpu.CompilerParams(vmem_limit_bytes=24 * 1024 * 1024),
        cost_estimate=pl.CostEstimate(flops=0, transcendentals=0, bytes_accessed=8 * 1024 * 1024),
        name="back_tokens",
    )(flags, *blocks)


def chips(
    stream,
    skip_in,
    cotangent,
    skip_weight,
    qkv_weight,
    out_weight,
    up_weight,
    down_weight,
    norm_gain,
    norm_bias,
    row_skip,
    col_skip,
    row_qkv,
    col_qkv,
    row_out,
    col_out,
    row_up,
    col_up,
    row_down,
    col_down,
    second_gain,
    second_bias,
):
    bf16 = jnp.bfloat16
    f32 = jnp.float32
    axes = ("wide", "narrow")
    wide_count = lax.axis_size("wide")
    narrow_count = lax.axis_size("narrow")
    ZS, YS = narrow_count // 2, 2
    wide_index = lax.axis_index("wide")
    narrow_index = lax.axis_index("narrow")
    xi = wide_index // 2
    ci = wide_index % 2
    zi = narrow_index // 2
    yi = narrow_index % 2
    rows_local, feat = stream.shape
    half_head = feat // 2
    hidden = up_weight.shape[1]
    quarter = hidden // 4
    scale_factor = 1.0 / math.sqrt(HEAD)

    def perm(move):
        pairs = []
        for wide in range(wide_count):
            for narrow in range(narrow_count):
                x, c, z, y = move(wide // 2, wide % 2, narrow // 2, narrow % 2)
                target = (x * 2 + c) * narrow_count + z * 2 + y
                pairs.append((wide * narrow_count + narrow, target))
        return pairs

    def send(value, move):
        return lax.ppermute(value, axes, perm(move))

    def core(value):
        return send(value, lambda x, c, z, y: (x, 1 - c, z, y))

    def over_x(value):
        return send(value, lambda x, c, z, y: (1 - x, c, z, y))

    def over_y(value):
        return send(value, lambda x, c, z, y: (x, c, z, 1 - y))

    def xor_z(value, bit):
        return send(value, lambda x, c, z, y: (x, c, z ^ bit, y))

    def tie(*values):
        return lax.optimization_barrier(values)

    def tie(*values):
        return lax.optimization_barrier(values)

    def add_low(left, right):
        return (left.astype(f32) + right.astype(f32)).astype(bf16)

    def padded(own):
        return jnp.pad(own, ((0, PAD - SEQ), (0, 0)))

    distances = [0]
    bit = ZS // 2
    while bit:
        distances += [distance ^ bit for distance in distances]
        bit //= 2

    def gather_z(block):
        line = block[None]
        bit = ZS // 2
        while bit:
            line = jnp.concatenate([line, xor_z(line, bit)])
            bit //= 2
        return line

    order = jnp.stack(
        [(zi ^ distance) * 2 + (yi ^ j) for j in range(2) for distance in distances]
    ).astype(jnp.int32)

    def canonical(blocks):
        def exchange(table, flag, bit, width):
            return [
                jnp.where(flag == 0, table[index], table[index ^ bit]) for index in range(width)
            ]

        table = [None] * narrow_count
        for place, distance in enumerate(distances):
            for j in range(2):
                table[distance * 2 + j] = blocks[j * ZS + place]
        bit = 1
        while bit < narrow_count:
            table = exchange(table, (narrow_index // bit) % 2, bit, narrow_count)
            bit *= 2
        return table

    def split_y(array):
        grid = array.reshape((ZS, YS) + array.shape[1:])
        return pick(grid, yi, 1), pick(grid, 1 - yi, 1)

    def z_pieces(near, far):
        return [
            jnp.concatenate([pick(near, zi ^ distance, 0), pick(far, zi ^ distance, 0)], axis=-1)
            for distance in distances
        ]

    def z_line(pieces):
        return [pieces[0]] + [
            xor_z(piece, distance) for piece, distance in zip(pieces[1:], distances[1:])
        ]

    def halves_z(total):
        return total[: ZS // 2], total[ZS // 2 :]

    half = ZS // 2
    meta = xi.astype(jnp.int32)[None]
    is_first = ci == 0

    def in_order(pair, other_core):
        four = jnp.stack([pair, other_core])
        return jnp.stack(
            [pick(pick(four, c ^ ci, 0), x ^ xi, 0) for c in range(2) for x in range(2)]
        )

    def all_narrow(value):
        value = value + over_y(value)
        bit = 1
        while bit < ZS:
            value = value + xor_z(value, bit)
            bit *= 2
        return value

    def columns(array):
        size = D // wide_count
        return lax.dynamic_slice_in_dim(array, wide_index * size, size, array.ndim - 1).astype(f32)

    def statistics(grad, old):
        grad = grad.astype(f32)
        squares = grad * grad + EPS_SQUARE
        new = DECAY * old + (1.0 - DECAY) * (jnp.sum(squares, axis=1) / D)
        return new, jnp.sum(squares, axis=0), jnp.sum(grad * grad * (1.0 / new)[:, None], axis=0)

    def step_of(grad, new, scale):
        return grad.astype(f32) * lax.rsqrt(new)[:, None] * scale[None, :]

    old_wide = jnp.stack([col_skip, row_qkv, col_out, row_up, col_down])
    lane = lax.broadcasted_iota(jnp.int32, (1, D), 1)
    old_sums = (
        jnp.where(lane == 0, jnp.sum(row_skip), 0.0)
        + jnp.where(lane == 2, jnp.sum(row_out), 0.0)
        + jnp.where(lane == 4, jnp.sum(row_down), 0.0)
    )
    rows_all = jnp.array([[2 * D], [3 * D], [D], [FF], [FF]], f32)
    along_wide = jnp.array([[False], [True], [False], [True], [False]])

    flags = jnp.stack([yi, zi % 2, zi // 2, ci]).astype(jnp.int32)
    token_near, token_give = pack_tokens(flags, stream.T, skip_in.T, cotangent.T)
    skip_block = pick(pick(skip_weight, ci, 0).reshape(2, feat // 2, D), xi, 0)
    attn_rows = jnp.concatenate(
        [
            pick(qkv_weight.transpose(1, 2, 0).reshape(3, 2, half_head, D), ci, 1),
            pick(out_weight.reshape(2, half_head, D), ci, 0)[None],
        ]
    ).reshape(2, 2 * half_head, D)
    attn_block = pick(attn_rows, xi, 0)
    skip_block, attn_block, token_give = tie(skip_block, attn_block, token_give)
    token_far = over_y(token_give)
    skip_two = xor_z(skip_block, 2)
    attn_two = xor_z(attn_block, 2)
    skip_line = jnp.stack([skip_block, skip_two])
    attn_line = jnp.stack([attn_block, attn_two])
    skip_line = jnp.concatenate([skip_line, xor_z(skip_line, 1)])
    attn_line = jnp.concatenate([attn_line, xor_z(attn_line, 1)])

    token_far, up_weight, down_weight = tie(token_far, up_weight, down_weight)
    token_blocks = z_line(join_lanes(token_near, token_far))
    skip_beside = over_y(skip_line)
    skip_across = over_x(skip_line)
    ffn_block = jnp.stack(
        [
            lax.dynamic_slice_in_dim(up_weight, (ci * 2 + xi) * quarter, quarter, 1).T,
            lax.dynamic_slice_in_dim(down_weight, (ci * 2 + xi) * quarter, quarter, 0),
        ]
    )

    skip_beside, skip_across, attn_line = tie(skip_beside, skip_across, attn_line)
    skip_corner = jnp.concatenate([over_x(skip_beside[:half]), over_y(skip_across[half:])])
    attn_beside = over_y(attn_line)
    attn_across = over_x(attn_line)

    token_blocks, ffn_block = tie(token_blocks, ffn_block)
    ffn_full = lax.all_gather(ffn_block[None], "narrow", tiled=True)
    mine, give, cot_pad = take_tokens(flags, token_blocks)
    flat = (mine, core(give))
    cot_own = cot_pad[:SEQ]
    attn_corner_x = over_x(attn_beside[:half])
    attn_corner_y = over_y(attn_across[half:])
    skip_near = jnp.concatenate([skip_line, skip_beside])
    skip_away = jnp.concatenate([skip_across, skip_corner])
    skip_mat = jnp.where(
        xi == 0,
        jnp.stack([skip_near, skip_away], axis=1),
        jnp.stack([skip_away, skip_near], axis=1),
    ).reshape(D, D)

    def both_images(own):
        own = padded(own)
        return own, core(own)

    def core_sum(kept, given):
        return (kept + core(given))[:SEQ]

    skip_give = matmul(flat[1], skip_mat, "rc,cd->rd")
    hidden_in = core_sum(matmul(flat[0], skip_mat, "rc,cd->rd"), skip_give)
    unit_one, inverse_one = unit_parts(hidden_in)
    normed = both_images((unit_one * norm_gain[0] + norm_bias[0]).astype(bf16))

    attn_corner = jnp.concatenate([attn_corner_x, attn_corner_y])
    normed, cot_pad, attn_corner = tie(normed, cot_pad, attn_corner)
    cot_pair = (cot_pad, over_x(cot_pad))
    attn_full = jnp.stack(
        [
            jnp.concatenate([attn_line, attn_beside]),
            jnp.concatenate([attn_across, attn_corner]),
        ]
    )
    attn_a, attn_b, qkv_kept, attended = attn_forward(meta, normed, attn_full)
    attn_b, cot_pair = tie(attn_b, cot_pair)
    middle = hidden_in + core_sum(attn_a, attn_b)
    unit_two, inverse_two = unit_parts(middle)
    mixed_own = padded((unit_two * norm_gain[1] + norm_bias[1]).astype(bf16))
    mixed_far = over_x(mixed_own)
    mixed = (mixed_own, mixed_far, core(mixed_own), core(mixed_far))
    cot = (*cot_pair, core(cot_pair[0]), core(cot_pair[1]))

    mixed_parts, act, act_grad = ffn_first(order, mixed, cot, ffn_full)
    mixed_far = mixed_parts[1] + core(mixed_parts[3])
    mixed_far, act = tie(mixed_far, act)
    mixed_far = over_x(mixed_far.astype(bf16))
    mixed_sum = mixed_parts[0] + core(mixed_parts[2])
    down_parts, up_near, up_give, down_near, down_give = ffn_second(
        order, mixed, cot, act, act_grad, ffn_full
    )
    ffn_far_up = over_y(up_give)
    ffn_down_one = xor_z(down_give, 1)

    mixed_far, down_parts = tie(mixed_far, down_parts)
    down_far = over_x((down_parts[1] + core(down_parts[3])).astype(bf16))
    down_sum = down_parts[0] + core(down_parts[2])
    back_middle, gain_two, bias_two = norm_back_own(
        unit_two,
        inverse_two,
        (mixed_sum + mixed_far.astype(f32))[:SEQ],
        norm_gain[1],
    )
    grad_middle = cot_own.astype(f32) + back_middle
    middle_low = both_images(grad_middle.astype(bf16))
    normed_a, normed_b, own, other_near, other_x, other_y = attn_backward(
        meta, normed, middle_low, attn_full, qkv_kept, attended
    )

    normed_b, ffn_far_up, ffn_down_one, down_far, other_x, other_y = tie(
        normed_b, ffn_far_up, ffn_down_one, down_far, other_x, other_y
    )
    attn_from_x = over_x(other_x)
    attn_from_y = over_y(other_y)
    ffn_down = add_low(down_near, ffn_down_one)
    ffn_down_far = over_y(ffn_down[1])
    ffn_up, ffn_up_give = halves_z(add_low(up_near, ffn_far_up))
    ffn_up_one = xor_z(ffn_up_give, 1)
    block_own = (middle + (down_sum + down_far.astype(f32))[:SEQ]).astype(bf16)
    back_hidden, gain_one, bias_one = norm_back_own(
        unit_one, inverse_one, core_sum(normed_a, normed_b), norm_gain[0]
    )
    hidden_low = both_images((grad_middle + back_hidden).astype(bf16))
    hidden_low, attn_from_x = tie(hidden_low, attn_from_x)
    token_grads = [matmul(low, skip_mat, "rd,cd->rc").astype(bf16) for low in hidden_low]
    back_near, back_give = give_tokens(
        flags, token_grads[0], core(token_grads[1]), padded(block_own)
    )
    grad_skip = matmul(
        jnp.concatenate(flat), jnp.concatenate(hidden_low), "rc,rd->cd"
    ).astype(bf16)
    grad_skip = grad_skip.reshape(narrow_count, 2, feat // 2, D)
    skip_own, skip_other = pick(grad_skip, xi, 1), pick(grad_skip, 1 - xi, 1)

    norm_sums = jnp.stack([gain_one, gain_two, bias_one, bias_two])
    norm_sums = norm_sums + core(norm_sums)

    attn_from_y, ffn_down_far, ffn_up_one, back_give, skip_own, skip_other, norm_sums = tie(
        attn_from_y, ffn_down_far, ffn_up_one, back_give, skip_own, skip_other, norm_sums
    )
    back_far = over_y(back_give)
    skip_from_x = over_x(skip_other[ZS : ZS + half])
    skip_from_y = over_y(skip_other[ZS + half :])
    attn_across = over_x(
        jnp.concatenate([other_near[:half], add_low(other_near[half:], attn_from_y)])
    )
    attn_far = jnp.concatenate([add_low(own[ZS : ZS + half], attn_from_x), own[ZS + half :]])
    ffn_both = jnp.stack([add_low(ffn_up, ffn_up_one), add_low(ffn_down[0], ffn_down_far)])
    ffn_two = xor_z(ffn_both[:, 1], 2)

    back_far, skip_from_x, skip_from_y, attn_across, ffn_two, attn_far = tie(
        back_far, skip_from_x, skip_from_y, attn_across, ffn_two, attn_far
    )
    attn_beside = over_y(attn_far)
    back_blocks = z_line(join_lanes(back_near, back_far))
    ffn_own = add_low(ffn_both[:, 0], ffn_two)
    ffn_x = over_x(ffn_own)
    skip_give_x = jnp.concatenate([skip_other[:half], add_low(skip_other[half:ZS], skip_from_y)])
    skip_give_y = jnp.concatenate(
        [add_low(skip_own[ZS : ZS + half], skip_from_x), skip_own[ZS + half :]]
    )

    attn_beside, back_blocks, ffn_x, skip_give_x, skip_give_y = tie(
        attn_beside, back_blocks, ffn_x, skip_give_x, skip_give_y
    )
    attn_total, attn_give = halves_z(
        (own[:ZS].astype(f32) + attn_beside.astype(f32) + attn_across.astype(f32)).astype(bf16)
    )
    attn_one = xor_z(attn_give, 1)
    skip_across = over_x(skip_give_x)
    skip_beside = over_y(skip_give_y)
    ffn_pair = jnp.stack([ffn_own, ffn_x])
    ffn_core = core(ffn_pair)
    back_out = back_tokens(flags, back_blocks)
    (ffn_all,) = tie(in_order(ffn_pair, ffn_core))
    grad_up_rows = ffn_all[:, 0].reshape(hidden, D)
    grad_down = ffn_all[:, 1].reshape(hidden, D)
    new_col_up, *up_sums = statistics(grad_up_rows, col_up)
    new_row_down, *down_sums = statistics(grad_down, row_down)
    ffn_sums = list(up_sums) + list(down_sums)

    attn_one, skip_across, skip_beside, ffn_sums, back_out = tie(
        attn_one, skip_across, skip_beside, ffn_sums, back_out
    )
    attn_total = add_low(attn_total, attn_one)
    attn_two = xor_z(attn_total[1], 2)
    skip_total, skip_give = halves_z(
        (skip_own[:ZS].astype(f32) + skip_beside.astype(f32) + skip_across.astype(f32)).astype(
            bf16
        )
    )
    skip_one = xor_z(skip_give, 1)
    grad_stream, grad_skip_in, block_out = [part.T for part in back_out]

    norm_far = over_x(norm_sums)

    attn_two, skip_one, norm_far = tie(attn_two, skip_one, norm_far)
    norm_sums = norm_sums + norm_far
    attn_own = add_low(attn_total[0], attn_two)
    attn_x = over_x(attn_own)
    skip_total = add_low(skip_total, skip_one)
    skip_two = xor_z(skip_total[1], 2)
    grad_up_out = columns(grad_up_rows).T
    grad_down_out = columns(grad_down)

    attn_x, skip_two, grad_up_out, grad_down_out = tie(
        attn_x, skip_two, grad_up_out, grad_down_out
    )
    skip_last = add_low(skip_total[0], skip_two)
    skip_x = over_x(skip_last)
    attn_pair = jnp.stack([attn_own, attn_x])
    (attn_all,) = tie(in_order(attn_pair, core(attn_pair)))
    attn_all = attn_all.reshape(2, 4, half_head, D)
    grad_qkv_rows = attn_all[:, :3].transpose(1, 0, 2, 3).reshape(3 * feat, D)
    grad_out = attn_all[:, 3].reshape(feat, D)
    new_col_qkv, *qkv_sums = statistics(grad_qkv_rows, col_qkv.reshape(-1))
    new_row_out, *out_sums = statistics(grad_out, row_out)

    skip_x, *sums = tie(skip_x, *qkv_sums, *out_sums)
    skip_pair = jnp.stack([skip_last, skip_x])
    (skip_all,) = tie(in_order(skip_pair, core(skip_pair)))
    grad_skip_rows = skip_all.reshape(2 * feat, D)

    new_row_skip, *skip_sums = statistics(grad_skip_rows, row_skip.reshape(-1))
    sums = list(skip_sums) + sums + list(ffn_sums)
    totals = all_narrow(
        jnp.concatenate([jnp.stack(sums[0::2] + sums[1::2]), norm_sums, old_sums])
    )
    gain_total = totals[10:12]
    bias_total = totals[12:14]
    wide_mean = totals[:5] / rows_all
    new_wide = DECAY * old_wide + (1.0 - DECAY) * wide_mean
    row_mean = jnp.where(
        along_wide,
        jnp.mean(new_wide, axis=1, keepdims=True),
        DECAY * (totals[14, :5].reshape(5, 1) / rows_all)
        + (1.0 - DECAY) * jnp.mean(wide_mean, axis=1, keepdims=True),
    )
    square_total = jnp.sum(totals[5:10] / new_wide, axis=1, keepdims=True) * row_mean
    ratios = jnp.sqrt(square_total / (rows_all * D)) / CLIP_LEVEL
    scales = lax.rsqrt(new_wide) * (-(STEP_RATE * jnp.sqrt(row_mean) / jnp.maximum(1.0, ratios)))
    new_col_skip, new_row_qkv, new_col_out, new_row_up, new_col_down = new_wide
    clip_ratio = ratios[:, 0]
    step_skip = step_of(grad_skip_rows, new_row_skip, scales[0])
    step_qkv = step_of(grad_qkv_rows, new_col_qkv, scales[1])
    step_out = step_of(grad_out, new_row_out, scales[2])
    step_up = step_of(grad_up_rows, new_col_up, scales[3])
    step_down = step_of(grad_down, new_row_down, scales[4])
    new_up = up_weight.astype(f32) + step_up.T
    new_down = down_weight.astype(f32) + step_down
    new_skip = skip_weight.astype(f32) + step_skip.reshape(2, feat, D)
    new_qkv = qkv_weight.astype(f32) + step_qkv.reshape(3, feat, D).transpose(2, 0, 1)
    new_second_gain, gain_step = plain_update(gain_total, second_gain)
    new_second_bias, bias_step = plain_update(bias_total, second_bias)
    return (
        block_out,
        grad_stream,
        grad_skip_in,
        columns(grad_skip_rows).reshape(2, feat, -1),
        columns(grad_qkv_rows).reshape(3, feat, -1).transpose(2, 0, 1),
        columns(grad_out),
        grad_up_out,
        grad_down_out,
        gain_total,
        bias_total,
        new_row_skip.reshape(2, feat),
        new_col_skip,
        new_row_qkv,
        new_col_qkv.reshape(3, feat),
        new_row_out,
        new_col_out,
        new_row_up,
        new_col_up,
        new_row_down,
        new_col_down,
        new_second_gain,
        new_second_bias[0],
        new_second_bias[1],
        new_skip,
        new_qkv,
        step_out,
        new_up,
        new_down,
        gain_step,
        bias_step,
        clip_ratio,
    )


def solution(mesh):
    wide, narrow = mesh.shape["wide"], mesh.shape["narrow"]
    body = chips if (wide == 4 and narrow == 8) else local
    in_specs = (
        P("wide", "narrow"),
        P("wide", "narrow"),
        P("wide", "narrow"),
        P(None, "narrow", None),
        P(None, None, "narrow"),
        P("narrow", None),
        P(None, "narrow"),
        P("narrow", None),
        P(),
        P(),
        P(None, "narrow"),
        P(),
        P(),
        P(None, "narrow"),
        P("narrow"),
        P(),
        P(),
        P("narrow"),
        P("narrow"),
        P(),
        P(),
        P(),
    )
    out_specs = (
        P("wide", "narrow"),
        P("wide", "narrow"),
        P("wide", "narrow"),
        P(None, "narrow", "wide"),
        P("wide", None, "narrow"),
        P("narrow", "wide"),
        P("wide", "narrow"),
        P("narrow", "wide"),
        P(),
        P(),
        P(None, "narrow"),
        P(),
        P(),
        P(None, "narrow"),
        P("narrow"),
        P(),
        P(),
        P("narrow"),
        P("narrow"),
        P(),
        P(),
        P(),
        P(),
        P(None, "narrow", None),
        P(None, None, "narrow"),
        P("narrow", None),
        P(None, "narrow"),
        P("narrow", None),
        P(),
        P(),
        P(),
    )
    return jax.shard_map(body, mesh=mesh, in_specs=in_specs, out_specs=out_specs, check_vma=False)
```

```python
import math

import jax
import jax.numpy as jnp
from jax import lax
from jax.experimental import pallas as pl
from jax.experimental.pallas import tpu as pltpu
from jax.sharding import PartitionSpec as P

D = 1152
FF = 4608
SEQ = 258
HEAD = 72


NORM_EPS = 1e-05
EPS_SQUARE = 1e-30
DECAY = 0.5
STEP_RATE = 0.05
CLIP_LEVEL = 0.25


def layer_norm(values, gain, shift):
    average = jnp.mean(values, axis=-1, keepdims=True)
    centered = values - average
    variance = jnp.mean(centered * centered, axis=-1, keepdims=True)
    return centered * lax.rsqrt(variance + NORM_EPS) * gain + shift


def norm_back(values, grad, gain, own_rows):
    average = jnp.mean(values, axis=-1, keepdims=True)
    centered = values - average
    variance = jnp.mean(centered * centered, axis=-1, keepdims=True)
    inverse = lax.rsqrt(variance + NORM_EPS)
    unit = centered * inverse
    scaled = grad * gain
    inner = (
        scaled
        - jnp.mean(scaled, axis=-1, keepdims=True)
        - unit * jnp.mean(scaled * unit, axis=-1, keepdims=True)
    )
    weighted = grad * own_rows
    return (inner * inverse, jnp.sum(weighted * unit, axis=0), jnp.sum(weighted, axis=0))


def gelu_exact(inputs):
    return jax.nn.gelu(inputs, approximate=False)


def matmul(left, right, form):
    return jnp.einsum(form, left, right, preferred_element_type=jnp.float32)


def plain_update(grad, second_old):
    second_new = DECAY * second_old + (1.0 - DECAY) * (grad * grad + EPS_SQUARE)
    update = grad * lax.rsqrt(second_new)
    spread = jnp.sqrt(jnp.mean(update * update))
    update = update / jnp.maximum(1.0, spread / CLIP_LEVEL)
    return (second_new, -(STEP_RATE * update))


def wide_slice(array, dim_index, count, wide_index):
    piece_size = array.shape[dim_index] // count
    return lax.dynamic_slice_in_dim(array, wide_index * piece_size, piece_size, dim_index)


def local(
    stream,
    skip_in,
    cotangent,
    skip_weight,
    qkv_weight,
    out_weight,
    up_weight,
    down_weight,
    norm_gain,
    norm_bias,
    row_skip,
    col_skip,
    row_qkv,
    col_qkv,
    row_out,
    col_out,
    row_up,
    col_up,
    row_down,
    col_down,
    second_gain,
    second_bias,
):
    rows_local, feat_local = stream.shape
    images = rows_local // SEQ
    heads_local = feat_local // HEAD
    scale_factor = 1.0 / math.sqrt(HEAD)
    split_shape = (images, SEQ, heads_local, HEAD)
    narrow_count = lax.axis_size("narrow")
    narrow_index = lax.axis_index("narrow")
    share_rows = -(-rows_local // narrow_count)
    row_start = narrow_index * share_rows
    row_ids = lax.broadcasted_iota(jnp.int32, (rows_local, 1), 0)
    own_mask = ((row_ids >= row_start) & (row_ids < row_start + share_rows)).astype(jnp.float32)

    def full_sum(values):
        return lax.psum(values, "narrow")

    partial_in = matmul(stream, skip_weight[0], "rc,cd->rd") + matmul(
        skip_in, skip_weight[1], "rc,cd->rd"
    )
    hidden_in = full_sum(partial_in)
    normed = layer_norm(hidden_in, norm_gain[0], norm_bias[0]).astype(jnp.bfloat16)
    projected = matmul(normed, qkv_weight, "rd,dtc->rtc").astype(jnp.bfloat16)
    queries = projected[:, 0].reshape(split_shape)
    key_vectors = projected[:, 1].reshape(split_shape)
    value_vectors = projected[:, 2].reshape(split_shape)
    scores = matmul(queries, key_vectors, "bqhe,bkhe->bhqk") * scale_factor
    row_max = jnp.max(scores, axis=-1, keepdims=True)
    exponent = jnp.exp(scores - row_max)
    row_total = jnp.sum(exponent, axis=-1, keepdims=True)
    log_total = row_max + jnp.log(row_total)
    probs_low = (exponent / row_total).astype(jnp.bfloat16)
    attended = (
        matmul(probs_low, value_vectors, "bhqk,bkhe->bqhe")
        .reshape(rows_local, feat_local)
        .astype(jnp.bfloat16)
    )
    attn_part = matmul(attended, out_weight, "rc,cd->rd")
    middle = hidden_in + full_sum(attn_part)
    mixed_in = layer_norm(middle, norm_gain[1], norm_bias[1]).astype(jnp.bfloat16)
    middle_own = lax.dynamic_slice_in_dim(middle, narrow_index * feat_local, feat_local, 1)
    up_input = matmul(mixed_in, up_weight, "rd,df->rf")
    activation = gelu_exact(up_input).astype(jnp.bfloat16)
    down_part = matmul(activation, down_weight, "rf,fd->rd")
    block_out = (
        middle_own + lax.psum_scatter(down_part, "narrow", scatter_dimension=1, tiled=True)
    ).astype(jnp.bfloat16)
    grad_full = lax.all_gather(cotangent, "narrow", axis=1, tiled=True)
    grad_down = matmul(activation, grad_full, "rf,rd->fd")
    grad_act = matmul(grad_full, down_weight, "rd,fd->rf")
    gelu_value, gelu_back = jax.vjp(gelu_exact, up_input)
    grad_up_in = gelu_back(grad_act)[0].astype(jnp.bfloat16)
    grad_up = matmul(mixed_in, grad_up_in, "rd,rf->df")
    mixed_part = matmul(grad_up_in, up_weight, "rf,df->rd")
    grad_mixed = full_sum(mixed_part)
    back_middle, back_gain_two, back_bias_two = norm_back(
        middle, grad_mixed, norm_gain[1], own_mask
    )
    grad_middle = grad_full.astype(jnp.float32) + back_middle
    middle_low = grad_middle.astype(jnp.bfloat16)
    grad_out = matmul(attended, middle_low, "rc,rd->cd")
    grad_attended = (
        matmul(middle_low, out_weight, "rd,cd->rc").astype(jnp.bfloat16).reshape(split_shape)
    )
    scores_again = matmul(queries, key_vectors, "bqhe,bkhe->bhqk") * scale_factor
    probs = jnp.exp(scores_again - log_total)
    probs_again = probs.astype(jnp.bfloat16)
    grad_values = matmul(probs_again, grad_attended, "bhqk,bqhe->bkhe")
    grad_probs = matmul(grad_attended, value_vectors, "bqhe,bkhe->bhqk")
    inner_sum = jnp.sum(probs * grad_probs, axis=-1, keepdims=True)
    grad_scores = (probs * (grad_probs - inner_sum) * scale_factor).astype(jnp.bfloat16)
    grad_queries = matmul(grad_scores, key_vectors, "bhqk,bkhe->bqhe")
    grad_keys = matmul(grad_scores, queries, "bhqk,bqhe->bkhe")
    grad_projected = jnp.stack(
        [
            grad_queries.reshape(rows_local, feat_local),
            grad_keys.reshape(rows_local, feat_local),
            grad_values.reshape(rows_local, feat_local),
        ],
        axis=1,
    ).astype(jnp.bfloat16)
    grad_qkv = matmul(normed, grad_projected, "rd,rtc->dtc")
    normed_part = matmul(grad_projected, qkv_weight, "rtc,dtc->rd")
    grad_normed = full_sum(normed_part)
    back_hidden, back_gain_one, back_bias_one = norm_back(
        hidden_in, grad_normed, norm_gain[0], own_mask
    )
    hidden_low = (grad_middle + back_hidden).astype(jnp.bfloat16)
    grad_skip = jnp.stack(
        [matmul(stream, hidden_low, "rc,rd->cd"), matmul(skip_in, hidden_low, "rc,rd->cd")]
    )
    grad_stream = matmul(hidden_low, skip_weight[0], "rd,cd->rc")
    grad_skip_in = matmul(hidden_low, skip_weight[1], "rd,cd->rc")
    gain_grads = jnp.stack([back_gain_one, back_gain_two])
    bias_grads = jnp.stack([back_bias_one, back_bias_two])
    wide_count = lax.axis_size("wide")
    wide_index = lax.axis_index("wide")
    wide_dims = (2, 0, 1, 0, 1)
    wide_axes = ((0, 1), (1, 2), (0,), (1,), (0,))
    narrow_axes = ((2,), (0,), (1,), (0,), (1,))
    wide_counts = (2 * D, 3 * D, D, FF, FF)
    row_along_wide = (False, True, False, True, False)
    entry_counts = (2 * D * D, 3 * D * D, D * D, D * FF, FF * D)
    old_slots = (0, 0, 1, 0, 2)
    weights = (skip_weight, qkv_weight, out_weight, up_weight, down_weight)
    old_wide = (col_skip, row_qkv, col_out, row_up, col_down)
    old_narrow = (row_skip, col_qkv, row_out, col_up, row_down)
    summed = lax.psum(
        (grad_skip, grad_qkv, grad_out, grad_up, grad_down, gain_grads, bias_grads), "wide"
    )
    pieces = summed[:5]
    gain_section = summed[5]
    bias_section = summed[6]
    squares = [piece * piece + EPS_SQUARE for piece in pieces]
    wide_parts = [jnp.sum(squares[number], axis=wide_axes[number]) for number in range(5)]
    narrow_parts = [jnp.sum(squares[number], axis=narrow_axes[number]) for number in range(5)]
    old_sums = jnp.stack([jnp.sum(row_skip), jnp.sum(row_out), jnp.sum(row_down)])
    stat_total = lax.psum(
        (
            wide_parts[0],
            wide_parts[1],
            wide_parts[2],
            wide_parts[3],
            wide_parts[4],
            old_sums,
            gain_section,
            bias_section,
        ),
        "narrow",
    )
    old_row_means = (stat_total[5][0] / (2 * D), stat_total[5][1] / D, stat_total[5][2] / FF)
    wide_stats = stat_total[:5]
    gain_total = stat_total[6]
    bias_total = stat_total[7]
    new_wide = []
    new_narrow = []
    updates = []
    for number in range(5):
        wide_mean = wide_stats[number] / wide_counts[number]
        wide_new = DECAY * old_wide[number] + (1.0 - DECAY) * wide_mean
        narrow_new = DECAY * old_narrow[number] + (1.0 - DECAY) * narrow_parts[number] / D
        if row_along_wide[number]:
            row_mean = jnp.mean(wide_new)
        else:
            row_mean = DECAY * old_row_means[old_slots[number]] + (1.0 - DECAY) * jnp.mean(
                wide_mean
            )
        dim_index = wide_dims[number]
        piece_size = pieces[number].shape[dim_index]
        broadcast_shape = [1] * pieces[number].ndim
        broadcast_shape[dim_index] = piece_size
        second = (
            jnp.expand_dims(narrow_new, dim_index) * wide_new.reshape(broadcast_shape) / row_mean
        )
        updates.append(pieces[number] * lax.rsqrt(second))
        new_wide.append(wide_new)
        new_narrow.append(narrow_new)
    update_squares = jnp.stack([jnp.sum(update * update) for update in updates])
    square_totals = lax.psum(update_squares, "narrow")
    counts_array = jnp.array(entry_counts, jnp.float32)
    clip_ratio = jnp.sqrt(square_totals / counts_array) / CLIP_LEVEL
    new_pieces = []
    for number in range(5):
        spread = jnp.sqrt(square_totals[number] / entry_counts[number])
        step_piece = -(STEP_RATE * (updates[number] / jnp.maximum(1.0, spread / CLIP_LEVEL)))
        if number == 2:
            new_pieces.append(step_piece)
        else:
            weight_piece = weights[number]
            new_pieces.append(weight_piece.astype(jnp.float32) + step_piece)
    grad_outs = [
        wide_slice(pieces[number], wide_dims[number], wide_count, wide_index) for number in range(5)
    ]
    new_second_gain, gain_step = plain_update(gain_total, second_gain)
    new_second_bias, bias_step = plain_update(bias_total, second_bias)
    return (
        block_out,
        grad_stream,
        grad_skip_in,
        grad_outs[0],
        grad_outs[1],
        grad_outs[2],
        grad_outs[3],
        grad_outs[4],
        gain_total,
        bias_total,
        new_narrow[0],
        new_wide[0],
        new_wide[1],
        new_narrow[1],
        new_narrow[2],
        new_wide[2],
        new_wide[3],
        new_narrow[3],
        new_narrow[4],
        new_wide[4],
        new_second_gain,
        new_second_bias[0],
        new_second_bias[1],
        new_pieces[0],
        new_pieces[1],
        new_pieces[2],
        new_pieces[3],
        new_pieces[4],
        gain_step,
        bias_step,
        clip_ratio,
    )


def unit_parts(values):
    average = jnp.mean(values, axis=-1, keepdims=True)
    centered = values - average
    variance = jnp.mean(centered * centered, axis=-1, keepdims=True)
    inverse = lax.rsqrt(variance + NORM_EPS)
    return centered * inverse, inverse


def norm_back_own(unit, inverse, grad, gain):
    scaled = grad * gain
    inner = (
        scaled
        - jnp.mean(scaled, axis=-1, keepdims=True)
        - unit * jnp.mean(scaled * unit, axis=-1, keepdims=True)
    )
    rows = tuple(range(grad.ndim - 1))
    return inner * inverse, jnp.sum(grad * unit, axis=rows), jnp.sum(grad, axis=rows)


def pick(array, index, axis):
    return lax.dynamic_index_in_dim(array, index, axis, keepdims=False)


PAD = 272


def dot_nt(left, right):
    return lax.dot_general(left, right, (((1,), (1,)), ((), ())), preferred_element_type=jnp.float32)


def dot_nn(left, right):
    return lax.dot_general(left, right, (((1,), (0,)), ((), ())), preferred_element_type=jnp.float32)


def dot_tn(left, right):
    return lax.dot_general(left, right, (((0,), (0,)), ((), ())), preferred_element_type=jnp.float32)


def accumulate(step, refs, value):
    size = refs[0].shape[0]

    @pl.when(step == 0)
    def _():
        for number, ref in enumerate(refs):
            ref[...] = value[number * size : (number + 1) * size]

    @pl.when(step > 0)
    def _():
        for number, ref in enumerate(refs):
            ref[...] += value[number * size : (number + 1) * size]


def all_four(refs):
    return jnp.concatenate([ref[...] for ref in refs], axis=0)


def ffn_first_kernel(order_ref, *refs):
    mixed, cot, weights, parts, (act_ref, grad_ref) = (
        all_four(refs[:4]),
        all_four(refs[4:8]),
        refs[8:12],
        refs[12:16],
        refs[16:],
    )
    up = jnp.concatenate([ref[0, 0] for ref in weights], axis=0)
    down = jnp.concatenate([ref[0, 1] for ref in weights], axis=0)
    up_input = dot_nt(mixed, up)
    gate = 0.5 * (1.0 + lax.erf(up_input * (1.0 / math.sqrt(2.0))))
    act_ref[0] = (up_input * gate).astype(jnp.bfloat16)
    slope = gate + up_input * (jnp.exp(-0.5 * up_input * up_input) * (1.0 / math.sqrt(2.0 * math.pi)))
    grad = (dot_nt(cot, down) * slope).astype(jnp.bfloat16)
    grad_ref[0] = grad
    accumulate(pl.program_id(0), parts, dot_nn(grad, up))


def ffn_second_kernel(order_ref, *refs):
    mixed, cot, (act_ref, grad_ref), weights, parts, (up_near, up_far, down_near, down_far) = (
        all_four(refs[:4]),
        all_four(refs[4:8]),
        refs[8:10],
        refs[10:14],
        refs[14:18],
        refs[18:],
    )
    step = pl.program_id(0)
    down = jnp.concatenate([ref[0, 0] for ref in weights], axis=0)
    grad_up = dot_tn(grad_ref[0], mixed).astype(jnp.bfloat16)
    grad_down = dot_tn(act_ref[0], cot).astype(jnp.bfloat16)
    for j, ref in enumerate((up_near, up_far)):

        @pl.when(step == j)
        def _():
            ref[...] = grad_up.reshape(ref.shape)

    halves = grad_down.reshape((2,) + down_near.shape[1:])
    down_near[0] = halves[0]
    down_far[0] = halves[1]
    accumulate(step, parts, dot_nn(act_ref[0], down))


def ffn_specs(tokens, rows):
    image = pl.BlockSpec((tokens // 4, D), lambda t, m: (0, 0))
    units = pl.BlockSpec((1, tokens, 4 * rows), lambda t, m: (t, 0, 0))
    return image, units


def ffn_first(order, mixed, cot, weights):
    count, _, rows, _ = weights.shape
    tokens = 4 * mixed[0].shape[0]
    image, units = ffn_specs(tokens, rows)

    def weight_spec(slot):
        return pl.BlockSpec((1, 2, rows, D), lambda t, m: (m[4 * t + slot], 0, 0, 0))

    part = jax.ShapeDtypeStruct((tokens // 4, D), jnp.float32)
    hidden = jax.ShapeDtypeStruct((count // 4, tokens, 4 * rows), jnp.bfloat16)
    *parts, act, grad = pl.pallas_call(
        ffn_first_kernel,
        out_shape=[part] * 4 + [hidden] * 2,
        grid_spec=pltpu.PrefetchScalarGridSpec(
            num_scalar_prefetch=1,
            grid=(count // 4,),
            in_specs=[image] * 8 + [weight_spec(slot) for slot in range(4)],
            out_specs=[image] * 4 + [units] * 2,
        ),
        compiler_params=pltpu.CompilerParams(
            dimension_semantics=("arbitrary",), vmem_limit_bytes=56 * 1024 * 1024
        ),
        cost_estimate=pl.CostEstimate(
            flops=6 * tokens * D * count * rows, transcendentals=0, bytes_accessed=24 * 1024 * 1024
        ),
        name="ffn_first",
    )(order, *mixed, *cot, *([weights] * 4))
    return parts, act, grad


def ffn_second(order, mixed, cot, act, grad, weights):
    count, _, rows, _ = weights.shape
    tokens = 4 * mixed[0].shape[0]
    image, units = ffn_specs(tokens, rows)

    def weight_spec(slot):
        return pl.BlockSpec((1, 1, rows, D), lambda t, m: (m[4 * t + slot], 1, 0, 0))

    part = jax.ShapeDtypeStruct((tokens // 4, D), jnp.float32)
    side = jax.ShapeDtypeStruct((4, rows, D), jnp.bfloat16)
    turn = jax.ShapeDtypeStruct((2, 2, rows, D), jnp.bfloat16)
    side_block = pl.BlockSpec((4, rows, D), lambda t, m: (0, 0, 0))
    turn_block = pl.BlockSpec((1, 2, rows, D), lambda t, m: (t, 0, 0, 0))
    *outs, up_near, up_far, down_near, down_far = pl.pallas_call(
        ffn_second_kernel,
        out_shape=[part] * 4 + [side] * 2 + [turn] * 2,
        grid_spec=pltpu.PrefetchScalarGridSpec(
            num_scalar_prefetch=1,
            grid=(count // 4,),
            in_specs=[image] * 8 + [units, units] + [weight_spec(slot) for slot in range(4)],
            out_specs=[image] * 4 + [side_block] * 2 + [turn_block] * 2,
        ),
        compiler_params=pltpu.CompilerParams(
            dimension_semantics=("arbitrary",), vmem_limit_bytes=56 * 1024 * 1024
        ),
        cost_estimate=pl.CostEstimate(
            flops=6 * tokens * D * count * rows, transcendentals=0, bytes_accessed=24 * 1024 * 1024
        ),
        name="ffn_second",
    )(order, *mixed, *cot, act, grad, *([weights] * 4))
    return outs, up_near, up_far, down_near, down_far


def soft(q, k):
    scores = dot_nt(q, k) * (1.0 / math.sqrt(HEAD))
    column = lax.broadcasted_iota(jnp.int32, scores.shape, 1)
    scores = jnp.where(column < SEQ, scores, -1e30)
    exponent = jnp.exp(scores - jnp.max(scores, axis=-1, keepdims=True))
    return exponent / jnp.sum(exponent, axis=-1, keepdims=True)


GROUP = 4


def head_weights(qk_ref, vo_ref):
    qk = [qk_ref[0, head] for head in range(GROUP)]
    v = [vo_ref[0, head, :HEAD] for head in range(GROUP)]
    out = [vo_ref[0, head, HEAD:] for head in range(GROUP)]
    return jnp.concatenate(qk + v, axis=0), jnp.concatenate(out, axis=0)


def head_columns(head):
    first = 2 * HEAD * head
    value = 2 * HEAD * GROUP + HEAD * head
    return (
        slice(first, first + HEAD),
        slice(first + HEAD, first + 2 * HEAD),
        slice(value, value + HEAD),
    )


def both(first_ref, second_ref):
    return jnp.concatenate([first_ref[...], second_ref[...]], axis=0)


def attn_forward_kernel(
    meta_ref, normed_a, normed_b, qk_ref, vo_ref, part_a, part_b, qkv_ref, attended_ref
):
    step = pl.program_id(0)
    weights, out_weight = head_weights(qk_ref, vo_ref)
    qkv_ref[0] = dot_nt(both(normed_a, normed_b), weights).astype(jnp.bfloat16)
    for head in range(GROUP):
        q_at, k_at, v_at = head_columns(head)
        for image in range(2):
            rows = slice(image * PAD, (image + 1) * PAD)
            probs = soft(qkv_ref[0, rows, q_at], qkv_ref[0, rows, k_at]).astype(jnp.bfloat16)
            attended_ref[0, rows, HEAD * head : HEAD * (head + 1)] = dot_nn(
                probs, qkv_ref[0, rows, v_at]
            ).astype(jnp.bfloat16)
    accumulate(step, (part_a, part_b), dot_nn(attended_ref[0], out_weight))


def attn_specs(rows, tokens):
    whole = pl.BlockSpec((tokens, D), lambda s, m: (0, 0))
    half = pl.BlockSpec((tokens // 2, D), lambda s, m: (0, 0))
    qk = pl.BlockSpec((1, GROUP, rows, D), lambda s, m: (m[0], s, 0, 0))
    vo = pl.BlockSpec((1, GROUP, rows, D), lambda s, m: (1 - m[0], s, 0, 0))
    qkv = pl.BlockSpec((1, tokens, 3 * HEAD * GROUP), lambda s, m: (s, 0, 0))
    att = pl.BlockSpec((1, tokens, HEAD * GROUP), lambda s, m: (s, 0, 0))
    return whole, half, qk, vo, qkv, att


def attn_forward(meta, normed, weights):
    heads, rows = weights.shape[1:3]
    tokens = 2 * normed[0].shape[0]
    whole, half, qk, vo, qkv, att = attn_specs(rows, tokens)
    return pl.pallas_call(
        attn_forward_kernel,
        out_shape=[
            jax.ShapeDtypeStruct((tokens // 2, D), jnp.float32),
            jax.ShapeDtypeStruct((tokens // 2, D), jnp.float32),
            jax.ShapeDtypeStruct((heads // GROUP, tokens, 3 * HEAD * GROUP), jnp.bfloat16),
            jax.ShapeDtypeStruct((heads // GROUP, tokens, HEAD * GROUP), jnp.bfloat16),
        ],
        grid_spec=pltpu.PrefetchScalarGridSpec(
            num_scalar_prefetch=1,
            grid=(heads // GROUP,),
            in_specs=[half, half, qk, vo],
            out_specs=[half, half, qkv, att],
        ),
        compiler_params=pltpu.CompilerParams(
            dimension_semantics=("arbitrary",), vmem_limit_bytes=48 * 1024 * 1024
        ),
        cost_estimate=pl.CostEstimate(flops=0, transcendentals=0, bytes_accessed=1024 * 1024),
        name="attn_forward",
    )(meta, *normed, weights, weights)


def attn_backward_kernel(
    meta_ref,
    normed_first,
    normed_second,
    low_first,
    low_second,
    qk_ref,
    vo_ref,
    qkv_ref,
    attended_ref,
    part_a,
    part_b,
    own_ref,
    near_ref,
    far_x_ref,
    far_y_ref,
    grads_s,
    out_s,
):
    step = pl.program_id(0)
    normed = both(normed_first, normed_second)
    low = both(low_first, low_second)
    weights, out_weight = head_weights(qk_ref, vo_ref)
    out_s[...] = dot_nt(low, out_weight).astype(jnp.bfloat16)
    for head in range(GROUP):
        q_at, k_at, v_at = head_columns(head)
        for image in range(2):
            rows = slice(image * PAD, (image + 1) * PAD)
            q = qkv_ref[0, rows, q_at]
            k = qkv_ref[0, rows, k_at]
            v = qkv_ref[0, rows, v_at]
            grad = out_s[rows, HEAD * head : HEAD * (head + 1)]
            probs = soft(q, k)
            grads_s[rows, v_at] = dot_tn(probs.astype(jnp.bfloat16), grad).astype(jnp.bfloat16)
            grad_probs = dot_nt(grad, v)
            inner = jnp.sum(probs * grad_probs, axis=-1, keepdims=True)
            grad_scores = (probs * (grad_probs - inner) * (1.0 / math.sqrt(HEAD))).astype(
                jnp.bfloat16
            )
            grads_s[rows, q_at] = dot_nn(grad_scores, k).astype(jnp.bfloat16)
            grads_s[rows, k_at] = dot_tn(grad_scores, q).astype(jnp.bfloat16)
    projected = grads_s[...]
    accumulate(step, (part_a, part_b), dot_nn(projected, weights))
    mats = dot_tn(projected, normed)
    outs = dot_tn(attended_ref[0], low)
    first = meta_ref[0] == 0
    for head in range(GROUP):
        q_at, k_at, v_at = head_columns(head)
        query_key = mats[q_at.start : k_at.stop]
        value_out = jnp.concatenate([mats[v_at], outs[HEAD * head : HEAD * (head + 1)]], axis=0)
        own_ref[head] = jnp.where(first, query_key, value_out).astype(jnp.bfloat16)
        other = jnp.where(first, value_out, query_key).astype(jnp.bfloat16)

        @pl.when(step == 0)
        def _():
            near_ref[head] = other

        @pl.when(step == 1)
        def _():
            if head < 2:
                far_x_ref[head] = other
            else:
                far_y_ref[head - 2] = other


def attn_backward(meta, normed, low, weights, qkv_kept, attended):
    heads, rows = weights.shape[1:3]
    tokens = 2 * normed[0].shape[0]
    whole, half, qk, vo, qkv, att = attn_specs(rows, tokens)

    def fixed(size):
        return pl.BlockSpec((size, rows, D), lambda s, m: (0, 0, 0))

    return pl.pallas_call(
        attn_backward_kernel,
        out_shape=[
            jax.ShapeDtypeStruct((tokens // 2, D), jnp.float32),
            jax.ShapeDtypeStruct((tokens // 2, D), jnp.float32),
            jax.ShapeDtypeStruct((heads, rows, D), jnp.bfloat16),
            jax.ShapeDtypeStruct((4, rows, D), jnp.bfloat16),
            jax.ShapeDtypeStruct((2, rows, D), jnp.bfloat16),
            jax.ShapeDtypeStruct((2, rows, D), jnp.bfloat16),
        ],
        grid_spec=pltpu.PrefetchScalarGridSpec(
            num_scalar_prefetch=1,
            grid=(heads // GROUP,),
            in_specs=[half, half, half, half, qk, vo, qkv, att],
            out_specs=[
                half,
                half,
                pl.BlockSpec((GROUP, rows, D), lambda s, m: (s, 0, 0)),
                fixed(4),
                fixed(2),
                fixed(2),
            ],
            scratch_shapes=[
                pltpu.VMEM((tokens, 3 * HEAD * GROUP), jnp.bfloat16),
                pltpu.VMEM((tokens, HEAD * GROUP), jnp.bfloat16),
            ],
        ),
        compiler_params=pltpu.CompilerParams(
            dimension_semantics=("arbitrary",), vmem_limit_bytes=56 * 1024 * 1024
        ),
        cost_estimate=pl.CostEstimate(
            flops=4 * tokens * D * heads * 2 * rows,
            transcendentals=0,
            bytes_accessed=24 * 1024 * 1024,
        ),
        name="attn_backward",
    )(meta, *normed, *low, weights, weights, qkv_kept, attended)


def by_narrow(blocks, flag_refs):
    table = [None] * 8
    for place, distance in enumerate((0, 2, 1, 3)):
        for j in range(2):
            table[distance * 2 + j] = blocks[j * 4 + place]
    for number, flag in enumerate(flag_refs):
        bit = 1 << number
        table = [jnp.where(flag == 0, table[i], table[i ^ bit]) for i in range(8)]
    return table


def by_slot(blocks, flag_refs):
    table = list(blocks)
    for number, flag in enumerate(flag_refs):
        bit = 1 << number
        table = [jnp.where(flag == 0, table[i], table[i ^ bit]) for i in range(8)]
    return [table[distance * 2 + j] for j in range(2) for distance in (0, 2, 1, 3)]


def take_kernel(flags_ref, *refs):
    blocks, (mine_ref, give_ref, cot_ref) = refs[:4], refs[4:]
    width = blocks[0].shape[1] // 6
    rows = blocks[0].shape[0]
    first = flags_ref[3] == 0
    for ref in (mine_ref, give_ref, cot_ref):
        ref[rows - 2 :] = jnp.zeros((ref.shape[0] - rows + 2, ref.shape[1]), ref.dtype)
    cots = []
    for j in range(2):
        for place in range(4):
            slot = j * 4 + place
            columns = slice(slot * width, (slot + 1) * width)
            one, two, three = [
                blocks[place][:, (3 * j + kind) * width : (3 * j + kind + 1) * width]
                for kind in range(3)
            ]
            mine_ref[:rows, columns] = jnp.where(first, one, two)
            give_ref[:rows, columns] = jnp.where(first, two, one)
            cots.append(three)
    for number, piece in enumerate(by_narrow(cots, [flags_ref[i] for i in range(3)])):
        cot_ref[:rows, number * width : (number + 1) * width] = piece


def take_tokens(flags, blocks):
    out = jax.ShapeDtypeStruct((PAD, D), jnp.bfloat16)
    full = pl.BlockSpec(memory_space=pltpu.VMEM)
    return pl.pallas_call(
        take_kernel,
        out_shape=[out] * 3,
        in_specs=[pl.BlockSpec(memory_space=pltpu.SMEM)] + [full] * 4,
        out_specs=[full] * 3,
        compiler_params=pltpu.CompilerParams(vmem_limit_bytes=24 * 1024 * 1024),
        cost_estimate=pl.CostEstimate(flops=0, transcendentals=0, bytes_accessed=4 * 1024 * 1024),
        name="take_tokens",
    )(flags, *blocks)


def give_kernel(flags_ref, kept_ref, other_ref, block_ref, near_ref, far_ref):
    rows = near_ref.shape[1]
    width = near_ref.shape[2] // 3
    first = flags_ref[3] == 0
    parts = [block_ref[:rows, n * width : (n + 1) * width] for n in range(8)]
    parts = by_slot(parts, [flags_ref[i] for i in range(3)])
    for slot in range(8):
        columns = slice(slot * width, (slot + 1) * width)
        kept = kept_ref[:rows, columns]
        other = other_ref[:rows, columns]
        target = (near_ref, far_ref)[slot // 4]
        target[slot % 4, :, :width] = jnp.where(first, kept, other)
        target[slot % 4, :, width : 2 * width] = jnp.where(first, other, kept)
        target[slot % 4, :, 2 * width :] = parts[slot]


def give_tokens(flags, kept, other, block):
    out = jax.ShapeDtypeStruct((4, SEQ, 3 * (D // 8)), jnp.bfloat16)
    full = pl.BlockSpec(memory_space=pltpu.VMEM)
    return pl.pallas_call(
        give_kernel,
        out_shape=[out] * 2,
        in_specs=[pl.BlockSpec(memory_space=pltpu.SMEM)] + [full] * 3,
        out_specs=[full] * 2,
        compiler_params=pltpu.CompilerParams(vmem_limit_bytes=24 * 1024 * 1024),
        cost_estimate=pl.CostEstimate(flops=0, transcendentals=0, bytes_accessed=4 * 1024 * 1024),
        name="give_tokens",
    )(flags, kept, other, block)


def join_kernel(near_ref, far_ref, *out_refs):
    width = near_ref.shape[2]
    for place, ref in enumerate(out_refs):
        ref[:, :width] = near_ref[place]
        ref[:, width:] = far_ref[place]


def join_lanes(near, far):
    count, rows, width = near.shape
    full = pl.BlockSpec(memory_space=pltpu.VMEM)
    return pl.pallas_call(
        join_kernel,
        out_shape=[jax.ShapeDtypeStruct((rows, 2 * width), near.dtype)] * count,
        in_specs=[full] * 2,
        out_specs=[full] * count,
        compiler_params=pltpu.CompilerParams(vmem_limit_bytes=24 * 1024 * 1024),
        cost_estimate=pl.CostEstimate(flops=0, transcendentals=0, bytes_accessed=4 * 1024 * 1024),
        name="join_lanes",
    )(near, far)
def pack_kernel(flags_ref, stream_ref, skip_ref, cot_ref, near_ref, give_ref):
    rows = near_ref.shape[1]
    pieces = []
    for number in range(8):
        at = slice(number * rows, (number + 1) * rows)
        piece = jnp.concatenate([stream_ref[:, at], skip_ref[:, at], cot_ref[:, at]], axis=0)
        pieces.append(piece.T)
    pieces = by_slot(pieces, [flags_ref[i] for i in range(3)])
    for place in range(4):
        near_ref[place] = pieces[place]
        give_ref[place] = pieces[4 + place]


def pack_tokens(flags, stream, skip_in, cotangent):
    out = jax.ShapeDtypeStruct((4, SEQ, 3 * stream.shape[0]), stream.dtype)
    full = pl.BlockSpec(memory_space=pltpu.VMEM)
    return pl.pallas_call(
        pack_kernel,
        out_shape=[out] * 2,
        in_specs=[pl.BlockSpec(memory_space=pltpu.SMEM)] + [full] * 3,
        out_specs=[full] * 2,
        compiler_params=pltpu.CompilerParams(vmem_limit_bytes=24 * 1024 * 1024),
        cost_estimate=pl.CostEstimate(flops=0, transcendentals=0, bytes_accessed=4 * 1024 * 1024),
        name="pack_tokens",
    )(flags, stream, skip_in, cotangent)


def back_kernel(flags_ref, *refs):
    blocks, (stream_ref, skip_ref, block_ref) = refs[:4], refs[4:]
    width = stream_ref.shape[0]
    rows = blocks[0].shape[0]
    pieces = [
        blocks[place][:, 3 * j * width : 3 * (j + 1) * width] for j in range(2) for place in range(4)
    ]
    for number, piece in enumerate(by_narrow(pieces, [flags_ref[i] for i in range(3)])):
        at = slice(number * rows, (number + 1) * rows)
        turned = piece.T
        stream_ref[:, at] = turned[:width].astype(jnp.float32)
        skip_ref[:, at] = turned[width : 2 * width].astype(jnp.float32)
        block_ref[:, at] = turned[2 * width :]


def back_tokens(flags, blocks):
    rows, width = blocks[0].shape
    shape = (width // 6, 8 * rows)
    full = pl.BlockSpec(memory_space=pltpu.VMEM)
    return pl.pallas_call(
        back_kernel,
        out_shape=[
            jax.ShapeDtypeStruct(shape, jnp.float32),
            jax.ShapeDtypeStruct(shape, jnp.float32),
            jax.ShapeDtypeStruct(shape, jnp.bfloat16),
        ],
        in_specs=[pl.BlockSpec(memory_space=pltpu.SMEM)] + [full] * 4,
        out_specs=[full] * 3,
        compiler_params=pltpu.CompilerParams(vmem_limit_bytes=24 * 1024 * 1024),
        cost_estimate=pl.CostEstimate(flops=0, transcendentals=0, bytes_accessed=8 * 1024 * 1024),
        name="back_tokens",
    )(flags, *blocks)


def chips(
    stream,
    skip_in,
    cotangent,
    skip_weight,
    qkv_weight,
    out_weight,
    up_weight,
    down_weight,
    norm_gain,
    norm_bias,
    row_skip,
    col_skip,
    row_qkv,
    col_qkv,
    row_out,
    col_out,
    row_up,
    col_up,
    row_down,
    col_down,
    second_gain,
    second_bias,
):
    bf16 = jnp.bfloat16
    f32 = jnp.float32
    axes = ("wide", "narrow")
    wide_count = lax.axis_size("wide")
    narrow_count = lax.axis_size("narrow")
    ZS, YS = narrow_count // 2, 2
    wide_index = lax.axis_index("wide")
    narrow_index = lax.axis_index("narrow")
    xi = wide_index // 2
    ci = wide_index % 2
    zi = narrow_index // 2
    yi = narrow_index % 2
    rows_local, feat = stream.shape
    half_head = feat // 2
    hidden = up_weight.shape[1]
    quarter = hidden // 4
    scale_factor = 1.0 / math.sqrt(HEAD)

    def perm(move):
        pairs = []
        for wide in range(wide_count):
            for narrow in range(narrow_count):
                x, c, z, y = move(wide // 2, wide % 2, narrow // 2, narrow % 2)
                target = (x * 2 + c) * narrow_count + z * 2 + y
                pairs.append((wide * narrow_count + narrow, target))
        return pairs

    def send(value, move):
        return lax.ppermute(value, axes, perm(move))

    def core(value):
        return send(value, lambda x, c, z, y: (x, 1 - c, z, y))

    def over_x(value):
        return send(value, lambda x, c, z, y: (1 - x, c, z, y))

    def over_y(value):
        return send(value, lambda x, c, z, y: (x, c, z, 1 - y))

    def xor_z(value, bit):
        return send(value, lambda x, c, z, y: (x, c, z ^ bit, y))

    def tie(*values):
        return lax.optimization_barrier(values)

    def tie(*values):
        return lax.optimization_barrier(values)

    def add_low(left, right):
        return (left.astype(f32) + right.astype(f32)).astype(bf16)

    def padded(own):
        return jnp.pad(own, ((0, PAD - SEQ), (0, 0)))

    distances = [0]
    bit = ZS // 2
    while bit:
        distances += [distance ^ bit for distance in distances]
        bit //= 2

    def gather_z(block):
        line = block[None]
        bit = ZS // 2
        while bit:
            line = jnp.concatenate([line, xor_z(line, bit)])
            bit //= 2
        return line

    order = jnp.stack(
        [(zi ^ distance) * 2 + (yi ^ j) for j in range(2) for distance in distances]
    ).astype(jnp.int32)

    def canonical(blocks):
        def exchange(table, flag, bit, width):
            return [
                jnp.where(flag == 0, table[index], table[index ^ bit]) for index in range(width)
            ]

        table = [None] * narrow_count
        for place, distance in enumerate(distances):
            for j in range(2):
                table[distance * 2 + j] = blocks[j * ZS + place]
        bit = 1
        while bit < narrow_count:
            table = exchange(table, (narrow_index // bit) % 2, bit, narrow_count)
            bit *= 2
        return table

    def split_y(array):
        grid = array.reshape((ZS, YS) + array.shape[1:])
        return pick(grid, yi, 1), pick(grid, 1 - yi, 1)

    def z_pieces(near, far):
        return [
            jnp.concatenate([pick(near, zi ^ distance, 0), pick(far, zi ^ distance, 0)], axis=-1)
            for distance in distances
        ]

    def z_line(pieces):
        return [pieces[0]] + [
            xor_z(piece, distance) for piece, distance in zip(pieces[1:], distances[1:])
        ]

    def halves_z(total):
        return total[: ZS // 2], total[ZS // 2 :]

    half = ZS // 2
    meta = xi.astype(jnp.int32)[None]
    is_first = ci == 0

    def in_order(pair, other_core):
        four = jnp.stack([pair, other_core])
        return jnp.stack(
            [pick(pick(four, c ^ ci, 0), x ^ xi, 0) for c in range(2) for x in range(2)]
        )

    def all_narrow(value):
        value = value + over_y(value)
        parts = [value] + [xor_z(value, distance) for distance in range(1, ZS)]
        while len(parts) > 1:
            parts = [left + right for left, right in zip(parts[0::2], parts[1::2])]
        return parts[0]

    def columns(array):
        size = D // wide_count
        return lax.dynamic_slice_in_dim(array, wide_index * size, size, array.ndim - 1).astype(f32)

    def statistics(grad, old):
        grad = grad.astype(f32)
        squares = grad * grad + EPS_SQUARE
        new = DECAY * old + (1.0 - DECAY) * (jnp.sum(squares, axis=1) / D)
        return new, jnp.sum(squares, axis=0), jnp.sum(grad * grad * (1.0 / new)[:, None], axis=0)

    def step_of(grad, new, scale):
        return grad.astype(f32) * lax.rsqrt(new)[:, None] * scale[None, :]

    old_wide = jnp.stack([col_skip, row_qkv, col_out, row_up, col_down])
    lane = lax.broadcasted_iota(jnp.int32, (1, D), 1)
    old_sums = (
        jnp.where(lane == 0, jnp.sum(row_skip), 0.0)
        + jnp.where(lane == 2, jnp.sum(row_out), 0.0)
        + jnp.where(lane == 4, jnp.sum(row_down), 0.0)
    )
    rows_all = jnp.array([[2 * D], [3 * D], [D], [FF], [FF]], f32)
    along_wide = jnp.array([[False], [True], [False], [True], [False]])

    flags = jnp.stack([yi, zi % 2, zi // 2, ci]).astype(jnp.int32)
    token_near, token_give = pack_tokens(flags, stream.T, skip_in.T, cotangent.T)
    skip_block = pick(pick(skip_weight, ci, 0).reshape(2, feat // 2, D), xi, 0)
    attn_rows = jnp.concatenate(
        [
            pick(qkv_weight.transpose(1, 2, 0).reshape(3, 2, half_head, D), ci, 1),
            pick(out_weight.reshape(2, half_head, D), ci, 0)[None],
        ]
    ).reshape(2, 2 * half_head, D)
    attn_block = pick(attn_rows, xi, 0)
    skip_block, attn_block, token_give = tie(skip_block, attn_block, token_give)
    token_far = over_y(token_give)
    skip_two = xor_z(skip_block, 2)
    attn_two = xor_z(attn_block, 2)
    skip_line = jnp.stack([skip_block, skip_two])
    attn_line = jnp.stack([attn_block, attn_two])
    skip_line = jnp.concatenate([skip_line, xor_z(skip_line, 1)])
    attn_line = jnp.concatenate([attn_line, xor_z(attn_line, 1)])

    token_far, up_weight, down_weight = tie(token_far, up_weight, down_weight)
    token_blocks = z_line(join_lanes(token_near, token_far))
    skip_beside = over_y(skip_line)
    skip_across = over_x(skip_line)
    ffn_block = jnp.stack(
        [
            lax.dynamic_slice_in_dim(up_weight, (ci * 2 + xi) * quarter, quarter, 1).T,
            lax.dynamic_slice_in_dim(down_weight, (ci * 2 + xi) * quarter, quarter, 0),
        ]
    )

    skip_beside, skip_across, attn_line = tie(skip_beside, skip_across, attn_line)
    skip_corner = jnp.concatenate([over_x(skip_beside[:half]), over_y(skip_across[half:])])
    attn_beside = over_y(attn_line)
    attn_across = over_x(attn_line)

    token_blocks, ffn_block = tie(token_blocks, ffn_block)
    ffn_full = lax.all_gather(ffn_block[None], "narrow", tiled=True)
    mine, give, cot_pad = take_tokens(flags, token_blocks)
    flat = (mine, core(give))
    cot_own = cot_pad[:SEQ]
    attn_corner_x = over_x(attn_beside[:half])
    attn_corner_y = over_y(attn_across[half:])
    skip_near = jnp.concatenate([skip_line, skip_beside])
    skip_away = jnp.concatenate([skip_across, skip_corner])
    skip_mat = jnp.where(
        xi == 0,
        jnp.stack([skip_near, skip_away], axis=1),
        jnp.stack([skip_away, skip_near], axis=1),
    ).reshape(D, D)

    def both_images(own):
        own = padded(own)
        return own, core(own)

    def core_sum(kept, given):
        return (kept + core(given))[:SEQ]

    skip_give = matmul(flat[1], skip_mat, "rc,cd->rd")
    hidden_in = core_sum(matmul(flat[0], skip_mat, "rc,cd->rd"), skip_give)
    unit_one, inverse_one = unit_parts(hidden_in)
    normed = both_images((unit_one * norm_gain[0] + norm_bias[0]).astype(bf16))

    attn_corner = jnp.concatenate([attn_corner_x, attn_corner_y])
    normed, cot_pad, attn_corner = tie(normed, cot_pad, attn_corner)
    cot_pair = (cot_pad, over_x(cot_pad))
    attn_full = jnp.stack(
        [
            jnp.concatenate([attn_line, attn_beside]),
            jnp.concatenate([attn_across, attn_corner]),
        ]
    )
    attn_a, attn_b, qkv_kept, attended = attn_forward(meta, normed, attn_full)
    attn_b, cot_pair = tie(attn_b, cot_pair)
    middle = hidden_in + core_sum(attn_a, attn_b)
    unit_two, inverse_two = unit_parts(middle)
    mixed_own = padded((unit_two * norm_gain[1] + norm_bias[1]).astype(bf16))
    mixed_far = over_x(mixed_own)
    mixed = (mixed_own, mixed_far, core(mixed_own), core(mixed_far))
    cot = (*cot_pair, core(cot_pair[0]), core(cot_pair[1]))

    mixed_parts, act, act_grad = ffn_first(order, mixed, cot, ffn_full)
    mixed_far = mixed_parts[1] + core(mixed_parts[3])
    mixed_far, act = tie(mixed_far, act)
    mixed_far = over_x(mixed_far.astype(bf16))
    mixed_sum = mixed_parts[0] + core(mixed_parts[2])
    down_parts, up_near, up_give, down_near, down_give = ffn_second(
        order, mixed, cot, act, act_grad, ffn_full
    )
    ffn_far_up = over_y(up_give)
    ffn_down_one = xor_z(down_give, 1)

    mixed_far, down_parts = tie(mixed_far, down_parts)
    down_far = over_x((down_parts[1] + core(down_parts[3])).astype(bf16))
    down_sum = down_parts[0] + core(down_parts[2])
    back_middle, gain_two, bias_two = norm_back_own(
        unit_two,
        inverse_two,
        (mixed_sum + mixed_far.astype(f32))[:SEQ],
        norm_gain[1],
    )
    grad_middle = cot_own.astype(f32) + back_middle
    middle_low = both_images(grad_middle.astype(bf16))
    normed_a, normed_b, own, other_near, other_x, other_y = attn_backward(
        meta, normed, middle_low, attn_full, qkv_kept, attended
    )

    normed_b, ffn_far_up, ffn_down_one, down_far, other_x, other_y = tie(
        normed_b, ffn_far_up, ffn_down_one, down_far, other_x, other_y
    )
    attn_from_x = over_x(other_x)
    attn_from_y = over_y(other_y)
    ffn_down = add_low(down_near, ffn_down_one)
    ffn_down_far = over_y(ffn_down[1])
    ffn_up, ffn_up_give = halves_z(add_low(up_near, ffn_far_up))
    ffn_up_one = xor_z(ffn_up_give, 1)
    block_own = (middle + (down_sum + down_far.astype(f32))[:SEQ]).astype(bf16)
    back_hidden, gain_one, bias_one = norm_back_own(
        unit_one, inverse_one, core_sum(normed_a, normed_b), norm_gain[0]
    )
    hidden_low = both_images((grad_middle + back_hidden).astype(bf16))
    hidden_low, attn_from_x = tie(hidden_low, attn_from_x)
    token_grads = [matmul(low, skip_mat, "rd,cd->rc").astype(bf16) for low in hidden_low]
    back_near, back_give = give_tokens(
        flags, token_grads[0], core(token_grads[1]), padded(block_own)
    )
    grad_skip = matmul(
        jnp.concatenate(flat), jnp.concatenate(hidden_low), "rc,rd->cd"
    ).astype(bf16)
    grad_skip = grad_skip.reshape(narrow_count, 2, feat // 2, D)
    skip_own, skip_other = pick(grad_skip, xi, 1), pick(grad_skip, 1 - xi, 1)

    norm_sums = jnp.stack([gain_one, gain_two, bias_one, bias_two])
    norm_sums = norm_sums + core(norm_sums)

    attn_from_y, ffn_down_far, ffn_up_one, back_give, skip_own, skip_other, norm_sums = tie(
        attn_from_y, ffn_down_far, ffn_up_one, back_give, skip_own, skip_other, norm_sums
    )
    back_far = over_y(back_give)
    skip_from_x = over_x(skip_other[ZS : ZS + half])
    skip_from_y = over_y(skip_other[ZS + half :])
    attn_across = over_x(
        jnp.concatenate([other_near[:half], add_low(other_near[half:], attn_from_y)])
    )
    attn_far = jnp.concatenate([add_low(own[ZS : ZS + half], attn_from_x), own[ZS + half :]])
    ffn_both = jnp.stack([add_low(ffn_up, ffn_up_one), add_low(ffn_down[0], ffn_down_far)])
    ffn_two = xor_z(ffn_both[:, 1], 2)

    back_far, skip_from_x, skip_from_y, attn_across, ffn_two, attn_far = tie(
        back_far, skip_from_x, skip_from_y, attn_across, ffn_two, attn_far
    )
    attn_beside = over_y(attn_far)
    back_blocks = z_line(join_lanes(back_near, back_far))
    ffn_own = add_low(ffn_both[:, 0], ffn_two)
    ffn_x = over_x(ffn_own)
    skip_give_x = jnp.concatenate([skip_other[:half], add_low(skip_other[half:ZS], skip_from_y)])
    skip_give_y = jnp.concatenate(
        [add_low(skip_own[ZS : ZS + half], skip_from_x), skip_own[ZS + half :]]
    )

    attn_beside, back_blocks, ffn_x, skip_give_x, skip_give_y = tie(
        attn_beside, back_blocks, ffn_x, skip_give_x, skip_give_y
    )
    attn_total, attn_give = halves_z(
        (own[:ZS].astype(f32) + attn_beside.astype(f32) + attn_across.astype(f32)).astype(bf16)
    )
    attn_one = xor_z(attn_give, 1)
    skip_across = over_x(skip_give_x)
    skip_beside = over_y(skip_give_y)
    ffn_pair = jnp.stack([ffn_own, ffn_x])
    ffn_core = core(ffn_pair)
    back_out = back_tokens(flags, back_blocks)
    (ffn_all,) = tie(in_order(ffn_pair, ffn_core))
    grad_up_rows = ffn_all[:, 0].reshape(hidden, D)
    grad_down = ffn_all[:, 1].reshape(hidden, D)
    new_col_up, *up_sums = statistics(grad_up_rows, col_up)
    new_row_down, *down_sums = statistics(grad_down, row_down)
    ffn_sums = list(up_sums) + list(down_sums)

    attn_one, skip_across, skip_beside, ffn_sums, back_out = tie(
        attn_one, skip_across, skip_beside, ffn_sums, back_out
    )
    attn_total = add_low(attn_total, attn_one)
    attn_two = xor_z(attn_total[1], 2)
    skip_total, skip_give = halves_z(
        (skip_own[:ZS].astype(f32) + skip_beside.astype(f32) + skip_across.astype(f32)).astype(
            bf16
        )
    )
    skip_one = xor_z(skip_give, 1)
    grad_stream, grad_skip_in, block_out = [part.T for part in back_out]

    norm_far = over_x(norm_sums)

    attn_two, skip_one, norm_far = tie(attn_two, skip_one, norm_far)
    norm_sums = norm_sums + norm_far
    attn_own = add_low(attn_total[0], attn_two)
    attn_x = over_x(attn_own)
    skip_total = add_low(skip_total, skip_one)
    skip_two = xor_z(skip_total[1], 2)
    grad_up_out = columns(grad_up_rows).T
    grad_down_out = columns(grad_down)

    attn_x, skip_two, grad_up_out, grad_down_out = tie(
        attn_x, skip_two, grad_up_out, grad_down_out
    )
    skip_last = add_low(skip_total[0], skip_two)
    skip_x = over_x(skip_last)
    attn_pair = jnp.stack([attn_own, attn_x])
    (attn_all,) = tie(in_order(attn_pair, core(attn_pair)))
    attn_all = attn_all.reshape(2, 4, half_head, D)
    grad_qkv_rows = attn_all[:, :3].transpose(1, 0, 2, 3).reshape(3 * feat, D)
    grad_out = attn_all[:, 3].reshape(feat, D)
    new_col_qkv, *qkv_sums = statistics(grad_qkv_rows, col_qkv.reshape(-1))
    new_row_out, *out_sums = statistics(grad_out, row_out)

    skip_x, *sums = tie(skip_x, *qkv_sums, *out_sums)
    skip_pair = jnp.stack([skip_last, skip_x])
    (skip_all,) = tie(in_order(skip_pair, core(skip_pair)))
    grad_skip_rows = skip_all.reshape(2 * feat, D)

    new_row_skip, *skip_sums = statistics(grad_skip_rows, row_skip.reshape(-1))
    sums = list(skip_sums) + sums + list(ffn_sums)
    totals = all_narrow(
        jnp.concatenate([jnp.stack(sums[0::2] + sums[1::2]), norm_sums, old_sums])
    )
    gain_total = totals[10:12]
    bias_total = totals[12:14]
    wide_mean = totals[:5] / rows_all
    new_wide = DECAY * old_wide + (1.0 - DECAY) * wide_mean
    row_mean = jnp.where(
        along_wide,
        jnp.mean(new_wide, axis=1, keepdims=True),
        DECAY * (totals[14, :5].reshape(5, 1) / rows_all)
        + (1.0 - DECAY) * jnp.mean(wide_mean, axis=1, keepdims=True),
    )
    square_total = jnp.sum(totals[5:10] / new_wide, axis=1, keepdims=True) * row_mean
    ratios = jnp.sqrt(square_total / (rows_all * D)) / CLIP_LEVEL
    scales = lax.rsqrt(new_wide) * (-(STEP_RATE * jnp.sqrt(row_mean) / jnp.maximum(1.0, ratios)))
    new_col_skip, new_row_qkv, new_col_out, new_row_up, new_col_down = new_wide
    clip_ratio = ratios[:, 0]
    step_skip = step_of(grad_skip_rows, new_row_skip, scales[0])
    step_qkv = step_of(grad_qkv_rows, new_col_qkv, scales[1])
    step_out = step_of(grad_out, new_row_out, scales[2])
    step_up = step_of(grad_up_rows, new_col_up, scales[3])
    step_down = step_of(grad_down, new_row_down, scales[4])
    new_up = up_weight.astype(f32) + step_up.T
    new_down = down_weight.astype(f32) + step_down
    new_skip = skip_weight.astype(f32) + step_skip.reshape(2, feat, D)
    new_qkv = qkv_weight.astype(f32) + step_qkv.reshape(3, feat, D).transpose(2, 0, 1)
    new_second_gain, gain_step = plain_update(gain_total, second_gain)
    new_second_bias, bias_step = plain_update(bias_total, second_bias)
    return (
        block_out,
        grad_stream,
        grad_skip_in,
        columns(grad_skip_rows).reshape(2, feat, -1),
        columns(grad_qkv_rows).reshape(3, feat, -1).transpose(2, 0, 1),
        columns(grad_out),
        grad_up_out,
        grad_down_out,
        gain_total,
        bias_total,
        new_row_skip.reshape(2, feat),
        new_col_skip,
        new_row_qkv,
        new_col_qkv.reshape(3, feat),
        new_row_out,
        new_col_out,
        new_row_up,
        new_col_up,
        new_row_down,
        new_col_down,
        new_second_gain,
        new_second_bias[0],
        new_second_bias[1],
        new_skip,
        new_qkv,
        step_out,
        new_up,
        new_down,
        gain_step,
        bias_step,
        clip_ratio,
    )


def solution(mesh):
    wide, narrow = mesh.shape["wide"], mesh.shape["narrow"]
    body = chips if (wide == 4 and narrow == 8) else local
    in_specs = (
        P("wide", "narrow"),
        P("wide", "narrow"),
        P("wide", "narrow"),
        P(None, "narrow", None),
        P(None, None, "narrow"),
        P("narrow", None),
        P(None, "narrow"),
        P("narrow", None),
        P(),
        P(),
        P(None, "narrow"),
        P(),
        P(),
        P(None, "narrow"),
        P("narrow"),
        P(),
        P(),
        P("narrow"),
        P("narrow"),
        P(),
        P(),
        P(),
    )
    out_specs = (
        P("wide", "narrow"),
        P("wide", "narrow"),
        P("wide", "narrow"),
        P(None, "narrow", "wide"),
        P("wide", None, "narrow"),
        P("narrow", "wide"),
        P("wide", "narrow"),
        P("narrow", "wide"),
        P(),
        P(),
        P(None, "narrow"),
        P(),
        P(),
        P(None, "narrow"),
        P("narrow"),
        P(),
        P(),
        P("narrow"),
        P("narrow"),
        P(),
        P(),
        P(),
        P(),
        P(None, "narrow", None),
        P(None, None, "narrow"),
        P("narrow", None),
        P(None, "narrow"),
        P("narrow", None),
        P(),
        P(),
        P(),
    )
    return jax.shard_map(body, mesh=mesh, in_specs=in_specs, out_specs=out_specs, check_vma=False)
```
